32 devices in a mesh: seq: 16 (over z, y, x), dp: 2 (over core).
Axes of the slice: x: 2, y: 2, z: 4, core: 2. Of those that a mesh axis runs over, the one named last changes fastest.
Arguments:
- queries: bfloat16 [2, 4096, 1024], P('dp', 'seq'), may hold values from -8 to 8
- keys: bfloat16 [2, 4096, 1024], P('dp', 'seq'), may hold values from -8 to 8
- values: bfloat16 [2, 4096, 1024], P('dp', 'seq'), may hold values from -6 to 6
- out_grad: bfloat16 [2, 4096, 1024], P('dp', 'seq'), may hold values from -6 to 6
- out_weight: bfloat16 [1024, 1024], replicated, may hold values from -0.1875 to 0.1875
Outputs:
- q_grad: bfloat16 [2, 4096, 1024], P('dp', 'seq')
- k_grad: bfloat16 [2, 4096, 1024], P('dp', 'seq')
- v_grad: bfloat16 [2, 4096, 1024], P('dp', 'seq')
- wo_grad: float32 [1024, 1024], P('seq', 'dp')
The draws below stay inside these ranges and needn't reach their ends.
All inputs are finite; a program needn't handle non-finite values.
Results may differ from the reference program's by a relative error of at most 0.017.
Values may be sent and summed in bfloat16 or wider, within the bound.
No kernel may reach another device: no remote copies, remote signals or barrier semaphores. Data moves between devices by JAX's collectives and lax.ppermute only.
A program may use at most 64 MiB of HBM per device.

```python
import jax
import jax.numpy as jnp
from jax import lax

D = 1024
HEAD_DIM = 64
HALF = 128
T_DEV = 256
SEQ_LEN = 4096
UTT = 2


def pair_draw(key):
    base = jax.random.fold_in(key, 7301)
    key_query, key_keys = jax.random.split(base, 2)
    whole_shape = (UTT, SEQ_LEN, D)
    query_part = jax.random.truncated_normal(key_query, -4.0, 4.0, whole_shape, jnp.float32)
    key_part = jax.random.truncated_normal(key_keys, -4.0, 4.0, whole_shape, jnp.float32)
    return (query_part, key_part)


def draw_queries(key, part):
    return pair_draw(key)[0].astype(jnp.bfloat16)


def draw_keys(key, part):
    return pair_draw(key)[1].astype(jnp.bfloat16)


def block_levels(stream_key, dims, shards, least, high):
    factor_of = 1.0
    for dim, shards_of in shards:
        heights = jax.random.uniform(jax.random.fold_in(jax.random.fold_in(stream_key, 6), dim), (shards_of,), jnp.float32, least / len(shards), high / len(shards))
        factor_of = factor_of * jnp.repeat(jnp.exp(heights), dims[dim] // shards_of).reshape((-1,) + (1,) * (len(dims) - 1 - dim))
    return factor_of


def scatter_about(stream_key, shape, scale, reach, cuts=(), kind=jnp.bfloat16):
    array = scale * jax.random.normal(stream_key, shape, jnp.float32)
    if cuts:
        array = array * block_levels(stream_key, shape, cuts, -0.22, 0.18)
    return jnp.clip(array, -reach, reach).astype(kind)


def setup_inputs(seed: int = 0) -> dict:
    key_of = jax.random.split(jax.random.key(seed), 6)
    queries = draw_queries(jax.random.fold_in(key_of[5], 71), 0)
    keys = draw_keys(jax.random.fold_in(key_of[5], 71), 0)
    values = scatter_about(key_of[2], (UTT, SEQ_LEN, D), 1.0, 6.0, ((0, 2), (1, 16)))
    out_grad = scatter_about(key_of[3], (UTT, SEQ_LEN, D), 1.0, 6.0, ((0, 2), (1, 16)))
    out_weight = scatter_about(key_of[4], (D, D), D ** -0.5, 0.1875)
    return dict(queries=queries, keys=keys, values=values, out_grad=out_grad, out_weight=out_weight)


masked_score = -1.0e30


def block_grads(query_rows, key_rows, value_rows, dattn_rows, query_first, key_first):
    count_q = query_rows.shape[0]
    count_k = key_rows.shape[0]
    head_count = D // HEAD_DIM
    scaling = HEAD_DIM ** -0.5
    query_head = query_rows.astype(jnp.float32).reshape(count_q, head_count, HEAD_DIM)
    key_head = key_rows.astype(jnp.float32).reshape(count_k, head_count, HEAD_DIM)
    value_head = value_rows.astype(jnp.float32).reshape(count_k, head_count, HEAD_DIM)
    dattn_head = dattn_rows.astype(jnp.float32).reshape(count_q, head_count, HEAD_DIM)
    query_pos = query_first + jnp.arange(count_q, dtype=jnp.int32)
    key_pos = key_first + jnp.arange(count_k, dtype=jnp.int32)
    inside = (key_pos[None, :] >= query_pos[:, None] - HALF) & (key_pos[None, :] < query_pos[:, None] + HALF)
    inside = inside & (key_pos[None, :] >= 0) & (key_pos[None, :] < SEQ_LEN)
    scores = jnp.einsum("qhd,khd->hqk", query_head, key_head) * scaling
    scores = jnp.where(inside[None], scores, masked_score)
    row_max = jnp.max(scores, axis=-1, keepdims=True)
    log_total = row_max + jnp.log(jnp.sum(jnp.exp(scores - row_max), axis=-1, keepdims=True))
    weights = jnp.exp(scores - log_total)
    weights_bf = lax.optimization_barrier(weights.astype(jnp.bfloat16)).astype(jnp.float32)
    attended = jnp.einsum("hqk,khd->qhd", weights_bf, value_head).astype(jnp.bfloat16)
    attended_wide = lax.optimization_barrier(attended).astype(jnp.float32)
    row_delta = jnp.sum(dattn_head * attended_wide, axis=-1)
    value_grad = jnp.einsum("hqk,qhd->khd", weights_bf, dattn_head)
    dweights = jnp.einsum("qhd,khd->hqk", dattn_head, value_head)
    dscore = (weights * (dweights - row_delta.T[:, :, None])).astype(jnp.bfloat16)
    dscore = lax.optimization_barrier(dscore).astype(jnp.float32)
    query_grad = jnp.einsum("hqk,khd->qhd", dscore, key_head) * scaling
    key_grad = jnp.einsum("hqk,qhd->khd", dscore, query_head) * scaling
    return (attended.reshape(count_q, D), query_grad.reshape(count_q, D),
            key_grad.reshape(count_k, D), value_grad.reshape(count_k, D))


def reference(queries, keys, values, out_grad, out_weight):
    query_list = []
    key_list = []
    value_list = []
    weight_total = jnp.zeros((D, D), jnp.float32)
    blocks = SEQ_LEN // T_DEV
    span = T_DEV + 2 * HALF
    for utterance in range(UTT):
        query_all = queries[utterance]
        grad_all = out_grad[utterance]
        dattn = jnp.dot(grad_all, out_weight.T, preferred_element_type=jnp.float32).astype(jnp.bfloat16)
        keys_pad = jnp.pad(keys[utterance], ((HALF, HALF), (0, 0)))
        values_pad = jnp.pad(values[utterance], ((HALF, HALF), (0, 0)))

        def block_step(accumulators, block_index):
            key_acc, value_acc = accumulators
            start = (block_index * T_DEV).astype(jnp.int32)
            query_rows = lax.dynamic_slice_in_dim(query_all, start, T_DEV, 0)
            dattn_rows = lax.dynamic_slice_in_dim(dattn, start, T_DEV, 0)
            key_rows = lax.dynamic_slice_in_dim(keys_pad, start, span, 0)
            value_rows = lax.dynamic_slice_in_dim(values_pad, start, span, 0)
            attended, query_grad, key_grad, value_grad = block_grads(
                query_rows, key_rows, value_rows, dattn_rows, start, start - HALF)
            key_acc = lax.dynamic_update_slice_in_dim(
                key_acc, lax.dynamic_slice_in_dim(key_acc, start, span, 0) + key_grad, start, 0)
            value_acc = lax.dynamic_update_slice_in_dim(
                value_acc, lax.dynamic_slice_in_dim(value_acc, start, span, 0) + value_grad, start, 0)
            return (key_acc, value_acc), (attended, query_grad.astype(jnp.bfloat16))

        zero_rows = jnp.zeros((SEQ_LEN + 2 * HALF, D), jnp.float32)
        (key_acc, value_acc), (attended_all, query_all_grad) = lax.scan(
            block_step, (zero_rows, zero_rows), jnp.arange(blocks, dtype=jnp.int32))
        attended_all = attended_all.reshape(SEQ_LEN, D)
        weight_total = weight_total + jnp.dot(attended_all.T, grad_all, preferred_element_type=jnp.float32)
        query_list.append(query_all_grad.reshape(SEQ_LEN, D))
        key_list.append(key_acc[HALF:HALF + SEQ_LEN].astype(jnp.bfloat16))
        value_list.append(value_acc[HALF:HALF + SEQ_LEN].astype(jnp.bfloat16))
    wo_grad = weight_total * ((UTT * SEQ_LEN) ** -0.5)
    return (jnp.stack(query_list), jnp.stack(key_list), jnp.stack(value_list), wo_grad)
```

```python
import functools

import jax
import jax.numpy as jnp
from jax import lax
from jax.experimental import pallas as pl
from jax.experimental.pallas import tpu as pltpu
from jax.sharding import PartitionSpec as P

HEAD_DIM = 64
HALF = 128
PAIR = 2 * HEAD_DIM
GROUPS = 1
masked_score = -1e30
f32 = jnp.float32
bf16 = jnp.bfloat16


def contract(a, b, dims):
    return lax.dot_general(a, b, (dims, ((), ())), preferred_element_type=f32)


NN = ((1,), (0,))
NT = ((1,), (1,))
TN = ((0,), (0,))


def attention_kernel(bias_ref, q_ref, da_ref, k_ref, v_ref, klo_ref, vlo_ref, khi_ref, vhi_ref,
                     at_ref, dq_ref, dk_ref, dv_ref, glo_ref, ghi_ref):
    scale = HEAD_DIM ** -0.5
    first_head = lax.broadcasted_iota(jnp.int32, (HALF, PAIR), 1) < HEAD_DIM
    key_at = lax.broadcasted_iota(jnp.int32, (HALF, 2 * HALF), 0)
    query_at = lax.broadcasted_iota(jnp.int32, (HALF, 2 * HALF), 1) % HALF
    below = key_at >= query_at
    k_all = jnp.concatenate([klo_ref[...], k_ref[...], khi_ref[...]], axis=0)
    v_all = jnp.concatenate([vlo_ref[...], v_ref[...], vhi_ref[...]], axis=0)
    blocks = q_ref.shape[0] // HALF
    dk_parts = []
    dv_parts = []
    for block in range(blocks):
        rows = slice(block * HALF, (block + 1) * HALF)
        q_one = q_ref[rows, :].astype(f32) * scale
        da_one = da_ref[rows, :].astype(f32)
        q_two = jnp.concatenate([jnp.where(first_head, q_one, 0.0), jnp.where(first_head, 0.0, q_one)], axis=0).astype(bf16)
        da_two = jnp.concatenate([jnp.where(first_head, da_one, 0.0), jnp.where(first_head, 0.0, da_one)], axis=0).astype(bf16)
        keys = k_all[block * HALF : (block + 3) * HALF]
        vals = v_all[block * HALF : (block + 3) * HALF]
        score = contract(keys, q_two, NT)
        s_first = score[:HALF]
        s_mid = score[HALF : 2 * HALF]
        s_last = score[2 * HALF :]
        if block == 0:
            s_first = s_first + bias_ref[0]
        if block == blocks - 1:
            s_last = s_last + bias_ref[1]
        s_edge = jnp.where(below, s_first, s_last)
        top = jnp.max(jnp.maximum(s_edge, s_mid), axis=0, keepdims=True)
        e_edge = jnp.exp(s_edge - top)
        e_mid = jnp.exp(s_mid - top)
        inv = 1.0 / jnp.sum(e_edge + e_mid, axis=0, keepdims=True)
        p_edge = e_edge * inv
        p_mid = e_mid * inv
        p_all = jnp.concatenate([jnp.where(below, p_edge, 0.0).astype(bf16), p_mid.astype(bf16),
                                 jnp.where(below, 0.0, p_edge).astype(bf16)], axis=0)
        dp = contract(vals, da_two, NT)
        d_edge = jnp.where(below, dp[:HALF], dp[2 * HALF :])
        d_mid = dp[HALF : 2 * HALF]
        delta = jnp.sum(p_edge * d_edge + p_mid * d_mid, axis=0, keepdims=True)
        ds_edge = p_edge * (d_edge - delta)
        ds_mid = p_mid * (d_mid - delta)
        ds_all = jnp.concatenate([jnp.where(below, ds_edge, 0.0).astype(bf16), ds_mid.astype(bf16),
                                  jnp.where(below, 0.0, ds_edge).astype(bf16)], axis=0)
        at = contract(vals, p_all, TN)
        at_ref[:HEAD_DIM, rows] = at[:HEAD_DIM, :HALF].astype(bf16)
        at_ref[HEAD_DIM:, rows] = at[HEAD_DIM:, HALF:].astype(bf16)
        dqt = contract(keys, ds_all, TN)
        dqt = jnp.concatenate([dqt[:HEAD_DIM, :HALF], dqt[HEAD_DIM:, HALF:]], axis=0) * scale
        dq_ref[rows, :] = dqt.T.astype(bf16)
        dv_parts.append(contract(p_all, da_two, NN))
        dk_parts.append(contract(ds_all, q_two, NN))
    glo_ref[0] = dk_parts[0][:HALF].astype(bf16)
    glo_ref[1] = dv_parts[0][:HALF].astype(bf16)
    ghi_ref[0] = dk_parts[-1][2 * HALF :].astype(bf16)
    ghi_ref[1] = dv_parts[-1][2 * HALF :].astype(bf16)
    for ref, parts in ((dk_ref, dk_parts), (dv_ref, dv_parts)):
        for row in range(blocks):
            total = None
            for block in range(blocks):
                at_row = row + 1 - block
                if 0 <= at_row < 3:
                    piece = parts[block][at_row * HALF : (at_row + 1) * HALF]
                    total = piece if total is None else total + piece
            ref[row * HALF : (row + 1) * HALF, :] = total


def attention(bias, q, da, k, v, lo, hi, first_pair, pairs):
    rows = q.shape[0]
    wide = pl.BlockSpec((rows, PAIR), lambda i: (0, i + first_pair))
    edge = lambda which: pl.BlockSpec((None, HALF, PAIR), lambda i: (which, 0, i))
    cols = pairs * PAIR
    return pl.pallas_call(
        attention_kernel,
        grid=(pairs,),
        in_specs=[pl.BlockSpec(memory_space=pltpu.SMEM), wide, wide, wide, wide, edge(0), edge(1), edge(0), edge(1)],
        out_specs=[
            pl.BlockSpec((PAIR, rows), lambda i: (i, 0)),
            pl.BlockSpec((rows, PAIR), lambda i: (0, i)),
            pl.BlockSpec((rows, PAIR), lambda i: (0, i)),
            pl.BlockSpec((rows, PAIR), lambda i: (0, i)),
            pl.BlockSpec((2, HALF, PAIR), lambda i: (0, 0, i)),
            pl.BlockSpec((2, HALF, PAIR), lambda i: (0, 0, i)),
        ],
        out_shape=[
            jax.ShapeDtypeStruct((cols, rows), bf16),
            jax.ShapeDtypeStruct((rows, cols), bf16),
            jax.ShapeDtypeStruct((rows, cols), f32),
            jax.ShapeDtypeStruct((rows, cols), f32),
            jax.ShapeDtypeStruct((2, HALF, cols), bf16),
            jax.ShapeDtypeStruct((2, HALF, cols), bf16),
        ],
        cost_estimate=pl.CostEstimate(flops=12 * rows * 3 * HALF * cols, bytes_accessed=16 * rows * cols,
                                      transcendentals=rows * 2 * HALF * cols // HEAD_DIM),
        name="attention",
    )(bias, q, da, k, v, lo, lo, hi, hi)


def upward(value, count):
    return lax.ppermute(value, "seq", [(i, i + 1) for i in range(count - 1)])


def downward(value, count):
    return lax.ppermute(value, "seq", [(i + 1, i) for i in range(count - 1)])


def stages(count):
    if count & (count - 1):
        return [(1, count)]
    found = []
    if count >= 4:
        found.append((2, 2))
        stride = 4
        while stride < count:
            radix = min(4, count // stride)
            found.append((stride, radix))
            stride *= radix
    if count >= 2:
        found.append((1, 2))
    return found


def scattered_sum(term, count):
    width = term.shape[1]
    me = lax.axis_index("seq")
    block = term.reshape((count, term.shape[0] // count, width))
    left = [(1, count)]
    for stride, radix in stages(count):
        outer, inner = None, None
        axis = 0
        dims = [size for _, size in left]
        for place, (low, size) in enumerate(left):
            if low <= stride < low * size:
                axis, base, total = place, low, size
        inner = stride // base
        outer = total // (inner * radix)
        shape = dims[:axis] + [outer, radix, inner] + dims[axis + 1 :] + list(block.shape[-2:])
        block = block.reshape(shape)
        digit = (me // stride) % radix
        at = axis + 1
        total_sum = None
        received = []
        for step in range(1, radix):
            pairs = []
            for source in range(count):
                place = (source // stride) % radix
                if radix & (radix - 1):
                    other = (place + step) % radix
                else:
                    other = place ^ step
                pairs.append((source, source + (other - place) * stride))
            other = (digit + step) % radix if radix & (radix - 1) else digit ^ step
            sent = lax.dynamic_index_in_dim(block, other, at, keepdims=False)
            received.append(lax.ppermute(sent, "seq", pairs))
        total_sum = lax.dynamic_index_in_dim(block, digit, at, keepdims=False).astype(f32)
        for piece in received:
            total_sum = total_sum + piece.astype(f32)
        new_left = left[:axis] + [(stride * radix, outer), (base, inner)] + left[axis + 1 :]
        block = total_sum
        if (stride, radix) != stages(count)[-1]:
            block = block.astype(bf16)
        keep = [(low, size) for low, size in new_left if size > 1]
        block = block.reshape([size for _, size in keep] + list(total_sum.shape[-2:]))
        left = keep
    return block.reshape(term.shape[0] // count, width)


def on_device(queries, keys, values, out_grad, out_weight):
    q, k, v, g = queries[0], keys[0], values[0], out_grad[0]
    rows, width = q.shape
    seq_count = lax.axis_size("seq")
    dp_count = lax.axis_size("dp")
    place = lax.axis_index("seq")
    mine = lax.axis_index("dp")
    pair_count = width // PAIR
    groups = GROUPS if pair_count % GROUPS == 0 else 1
    per_group = pair_count // groups
    halo = []
    for group in range(groups):
        cols = slice(group * per_group * PAIR, (group + 1) * per_group * PAIR)
        lo = upward(jnp.stack([k[rows - HALF :, cols], v[rows - HALF :, cols]]), seq_count)
        hi = downward(jnp.stack([k[:HALF, cols], v[:HALF, cols]]), seq_count)
        halo.append((lo, hi))
    dattn = contract(g, out_weight, NT).astype(bf16)
    own_width = width // dp_count
    g_parts = [lax.dynamic_slice_in_dim(g, mine * own_width, own_width, 1)]
    for step in range(1, dp_count):
        other = (mine + step) % dp_count
        sent = lax.dynamic_slice_in_dim(g, other * own_width, own_width, 1)
        g_parts.append(lax.ppermute(sent, "dp", [(i, (i + step) % dp_count) for i in range(dp_count)]))
    bias = jnp.stack([jnp.where(place == 0, masked_score, 0.0), jnp.where(place == seq_count - 1, masked_score, 0.0)]).astype(f32)
    term_parts = []
    dq_parts, dk_parts, dv_parts = [], [], []
    for group in range(groups):
        lo, hi = halo[group]
        at, dq, dk, dv, glo, ghi = attention(bias, q, dattn, k, v, lo, hi, group * per_group, per_group)
        from_above = downward(glo, seq_count)
        from_below = upward(ghi, seq_count)
        at_parts = [at]
        for step in range(1, dp_count):
            at_parts.append(lax.ppermute(at, "dp", [(i, (i + step) % dp_count) for i in range(dp_count)]))
        term = None
        for at_part, g_part in zip(at_parts, g_parts):
            piece = contract(at_part, g_part, NN)
            term = piece if term is None else term + piece
        term_parts.append(term.astype(bf16))
        edge = jnp.concatenate([from_below, from_above], axis=1).astype(f32)
        if rows > 2 * HALF:
            gap = jnp.zeros((2, rows - 2 * HALF) + edge.shape[2:], f32)
            edge = jnp.concatenate([from_below.astype(f32), gap, from_above.astype(f32)], axis=1)
        dq_parts.append(dq)
        dk_parts.append((dk + edge[0]).astype(bf16))
        dv_parts.append((dv + edge[1]).astype(bf16))
    join = lambda parts, axis: parts[0] if len(parts) == 1 else jnp.concatenate(parts, axis=axis)
    frames = rows * seq_count * dp_count
    wo_grad = scattered_sum(join(term_parts, 0), seq_count) * frames ** -0.5
    return join(dq_parts, 1)[None], join(dk_parts, 1)[None], join(dv_parts, 1)[None], wo_grad


def solution(mesh):
    spread = P("dp", "seq", None)
    return jax.shard_map(
        on_device,
        mesh=mesh,
        in_specs=(spread, spread, spread, spread, P()),
        out_specs=(spread, spread, spread, P("seq", "dp")),
        check_vma=False,
    )
```

```python
import jax
import jax.numpy as jnp
from jax import lax
from jax.experimental import pallas as pl
from jax.experimental.pallas import tpu as pltpu
from jax.sharding import PartitionSpec as P

HEAD_DIM = 64
HALF = 128
PAIR = 2 * HEAD_DIM
masked_score = -1e30
f32 = jnp.float32
bf16 = jnp.bfloat16


NN = ((1,), (0,))
NT = ((1,), (1,))
TN = ((0,), (0,))


def contract(a, b, dims):
    return lax.dot_general(a, b, (dims, ((), ())), preferred_element_type=f32)


def half_kernel(side_ref, bias_ref, q_ref, da_ref, near_k_ref, near_v_ref, far_k_ref, far_v_ref, rim_k_ref, rim_v_ref, *rest):
    earlier, outs = rest[:-5], rest[-5:]
    at_ref, dq_ref, dk_ref, dv_ref, back_ref = outs
    side = side_ref[0]
    scale = HEAD_DIM ** -0.5
    first_head = lax.broadcasted_iota(jnp.int32, (HALF, PAIR), 1) < HEAD_DIM
    ahead = lax.broadcasted_iota(jnp.int32, (HALF, 2 * HALF), 0) - lax.broadcasted_iota(jnp.int32, (HALF, 2 * HALF), 1) % HALF
    in_rim = ahead * (1 - 2 * side) >= side
    q_one = q_ref[...].astype(f32) * scale
    da_one = da_ref[...].astype(f32)
    q_two = jnp.concatenate([jnp.where(first_head, q_one, 0.0), jnp.where(first_head, 0.0, q_one)], axis=0).astype(bf16)
    da_two = jnp.concatenate([jnp.where(first_head, da_one, 0.0), jnp.where(first_head, 0.0, da_one)], axis=0).astype(bf16)
    keys = jnp.concatenate([rim_k_ref[...], near_k_ref[...], far_k_ref[...]], axis=0)
    vals = jnp.concatenate([rim_v_ref[...], near_v_ref[...], far_v_ref[...]], axis=0)
    score = contract(keys, q_two, NT)
    s_edge = jnp.where(in_rim, score[:HALF] + bias_ref[0], score[2 * HALF :])
    s_near = score[HALF : 2 * HALF]
    top = jnp.max(jnp.maximum(s_edge, s_near), axis=0, keepdims=True)
    e_edge = jnp.exp(s_edge - top)
    e_near = jnp.exp(s_near - top)
    inv = 1.0 / jnp.sum(e_edge + e_near, axis=0, keepdims=True)
    p_edge = e_edge * inv
    p_near = e_near * inv
    p_all = jnp.concatenate([jnp.where(in_rim, p_edge, 0.0).astype(bf16), p_near.astype(bf16),
                             jnp.where(in_rim, 0.0, p_edge).astype(bf16)], axis=0)
    dp = contract(vals, da_two, NT)
    d_edge = jnp.where(in_rim, dp[:HALF], dp[2 * HALF :])
    d_near = dp[HALF : 2 * HALF]
    delta = jnp.sum(p_edge * d_edge + p_near * d_near, axis=0, keepdims=True)
    ds_edge = p_edge * (d_edge - delta)
    ds_near = p_near * (d_near - delta)
    ds_all = jnp.concatenate([jnp.where(in_rim, ds_edge, 0.0).astype(bf16), ds_near.astype(bf16),
                              jnp.where(in_rim, 0.0, ds_edge).astype(bf16)], axis=0)
    at = contract(vals, p_all, TN)
    at_ref[:HEAD_DIM, :] = at[:HEAD_DIM, :HALF].astype(bf16)
    at_ref[HEAD_DIM:, :] = at[HEAD_DIM:, HALF:].astype(bf16)
    dqt = contract(keys, ds_all, TN)
    dqt = jnp.concatenate([dqt[:HEAD_DIM, :HALF], dqt[HEAD_DIM:, HALF:]], axis=0) * scale
    dq_ref[...] = dqt.T.astype(bf16)
    near_rows = pl.ds(pl.multiple_of(side * HALF, HALF), HALF)
    far_rows = pl.ds(pl.multiple_of((1 - side) * HALF, HALF), HALF)
    for which, (ref, left, right) in enumerate(((dk_ref, ds_all, q_two), (dv_ref, p_all, da_two))):
        part = contract(left, right, NN)
        back_ref[which] = part[:HALF].astype(bf16)
        near, far = part[HALF : 2 * HALF], part[2 * HALF :]
        if earlier:
            near = near + earlier[1 + which][near_rows, :]
            far = far + earlier[1 + which][far_rows, :]
        ref[near_rows, :] = near
        ref[far_rows, :] = far


def half_attention(side, bias, q, da, k, v, rim, earlier, name):
    rows, width = q.shape
    near = pl.BlockSpec((HALF, PAIR), lambda i, s: (s[0], i))
    far = pl.BlockSpec((HALF, PAIR), lambda i, s: (1 - s[0], i))
    edge = lambda which: pl.BlockSpec((None, HALF, PAIR), lambda i, s: (which, 0, i))
    whole = pl.BlockSpec((rows, PAIR), lambda i, s: (0, i))
    in_specs = [pl.BlockSpec(memory_space=pltpu.SMEM), near, near, near, near, far, far, edge(0), edge(1)]
    operands = [side, bias, q, da, k, v, k, v, rim, rim]
    aliases = {}
    if earlier:
        aliases = {len(operands): 1}
        in_specs += [pl.BlockSpec(memory_space=pl.ANY), whole, whole]
        operands += list(earlier)
    return pl.pallas_call(
        half_kernel,
        grid_spec=pltpu.PrefetchScalarGridSpec(
            num_scalar_prefetch=1,
            grid=(width // PAIR,),
            in_specs=in_specs,
            out_specs=[
                pl.BlockSpec((PAIR, HALF), lambda i, s: (i, 0)),
                near,
                whole,
                whole,
                pl.BlockSpec((2, HALF, PAIR), lambda i, s: (0, 0, i)),
            ],
        ),
        out_shape=[
            jax.ShapeDtypeStruct((width, HALF), bf16),
            jax.ShapeDtypeStruct((rows, width), bf16),
            jax.ShapeDtypeStruct((rows, width), f32),
            jax.ShapeDtypeStruct((rows, width), f32),
            jax.ShapeDtypeStruct((2, HALF, width), bf16),
        ],
        input_output_aliases=aliases,
        cost_estimate=pl.CostEstimate(flops=12 * HALF * 3 * HALF * width, bytes_accessed=16 * rows * width,
                                      transcendentals=HALF * 2 * HALF * width // HEAD_DIM),
        name=name,
    )(*operands)


def product_kernel(*refs):
    out_ref = refs[-1]
    count = (len(refs) - 1) // 2
    left = jnp.concatenate([ref[...] for ref in refs[:count]], axis=1)
    right = jnp.concatenate([ref[...] for ref in refs[count:-1]], axis=0)
    out_ref[...] = contract(left, right, NN).astype(out_ref.dtype)


def product(lefts, rights):
    return pl.pallas_call(
        product_kernel,
        out_shape=jax.ShapeDtypeStruct((lefts[0].shape[0], rights[0].shape[1]), bf16),
        name="product",
    )(*lefts, *rights)


def swapped(value, stride, count):
    return lax.ppermute(value, "seq", [(i, i ^ stride) for i in range(count)])


def turned(value, count):
    return [lax.ppermute(value, "dp", [(i, (i + step) % count) for i in range(count)]) for step in range(1, count)]


def upper_stages(count):
    found = []
    stride = 4
    while stride < count:
        radix = min(4, count // stride)
        found.append((stride, radix))
        stride *= radix
    return found


def scattered_sum(block, strides, stages, me, count):
    tail = list(block.shape[-2:])
    left = strides
    for number, (stride, radix) in enumerate(stages):
        axis = [place for place, (low, size) in enumerate(left) if low <= stride < low * size][0]
        base, total = left[axis]
        inner = stride // base
        outer = total // (inner * radix)
        dims = [size for _, size in left]
        block = block.reshape(dims[:axis] + [outer, radix, inner] + dims[axis + 1 :] + tail)
        digit = (me // stride) % radix
        received = []
        for step in range(1, radix):
            pairs = [(source, source ^ (step * stride)) for source in range(count)]
            sent = lax.dynamic_index_in_dim(block, digit ^ step, axis + 1, keepdims=False)
            received.append(lax.ppermute(sent, "seq", pairs))
        total_sum = lax.dynamic_index_in_dim(block, digit, axis + 1, keepdims=False).astype(f32)
        for piece in received:
            total_sum = total_sum + piece.astype(f32)
        block = total_sum if number == len(stages) - 1 else total_sum.astype(bf16)
        left = left[:axis] + [(stride * radix, outer), (base, inner)] + left[axis + 1 :]
        keep = [(low, size) for low, size in left if size > 1]
        block = block.reshape([size for _, size in keep] + tail)
        left = keep
    return block.reshape(tail)


def on_device(queries, keys, values, out_grad, out_weight):
    q, k, v, g = queries[0], keys[0], values[0], out_grad[0]
    rows, width = q.shape
    assert rows == 2 * HALF
    count = lax.axis_size("seq")
    dp_count = lax.axis_size("dp")
    assert count >= 8 and count & (count - 1) == 0
    place = lax.axis_index("seq")
    mine = lax.axis_index("dp")
    odd = place % 2
    sides = (odd, 1 - odd)
    long_pairs = [(i, i + 1 if i % 2 else i - 1) for i in range(1, count - 1)]
    near_pairs = [(i, i ^ 1) for i in range(count)]

    def rim_of(side):
        start = side * HALF
        return jnp.stack([lax.dynamic_slice_in_dim(k, start, HALF, 0), lax.dynamic_slice_in_dim(v, start, HALF, 0)])

    first_rim = lax.ppermute(rim_of(sides[0]), "seq", long_pairs)
    dattn = contract(g, out_weight, NT).astype(bf16)
    own_width = width // dp_count
    g_parts = [lax.dynamic_slice_in_dim(g, mine * own_width, own_width, 1)]
    for step in range(1, dp_count):
        sent = lax.dynamic_slice_in_dim(g, (mine + step) % dp_count * own_width, own_width, 1)
        g_parts.append(lax.ppermute(sent, "dp", [(i, (i + step) % dp_count) for i in range(dp_count)]))
    second_sent, dattn, g_last = lax.optimization_barrier((rim_of(sides[1]), dattn, g_parts[-1]))
    g_parts[-1] = g_last
    second_rim = lax.ppermute(second_sent, "seq", near_pairs)
    g_here = jnp.stack(g_parts)
    g_there = swapped(g_here, 2, count)

    scalars = [jnp.reshape(side, (1,)).astype(jnp.int32) for side in sides]
    alone = [jnp.where(side == 0, place == 0, place == count - 1) for side in sides]
    bias = [jnp.where(one, masked_score, 0.0).astype(f32).reshape(1) for one in alone]
    block = width // count
    y_digit = (place // 2) % 2

    def exchanged(at):
        parts = at.reshape(count // 4, 2, 2 * block, HALF)
        kept = lax.dynamic_index_in_dim(parts, y_digit, 1, keepdims=False).reshape(width // 2, HALF)
        sent = lax.dynamic_index_in_dim(parts, 1 - y_digit, 1, keepdims=False).reshape(width // 2, HALF)
        return kept, swapped(sent, 2, count)

    at1, dq, dk, dv, back1 = half_attention(scalars[0], bias[0], q, dattn, k, v, first_rim, None, "first_half")
    from_long = lax.ppermute(back1, "seq", long_pairs)
    here1 = exchanged(at1)
    at2, dq, dk, dv, back2 = half_attention(scalars[1], bias[1], q, dattn, k, v, second_rim, (dq, dk, dv), "second_half")
    here2 = exchanged(at2)
    from_near = lax.ppermute(back2, "seq", near_pairs)

    lefts, rights = [], []
    for side, here in zip(sides, (here1, here2)):
        pack = jnp.stack(here)
        for utt, part in enumerate([pack] + turned(pack, dp_count)):
            for row, source in ((0, g_here), (1, g_there)):
                lefts.append(part[row])
                rights.append(lax.dynamic_slice_in_dim(source[utt], side * HALF, HALF, 0))
    term = product(lefts, rights)
    strides = [(4, count // 4), (1, 2)]
    term = term.reshape(count // 4, 2, block, own_width)
    frames = rows * count * dp_count
    wo_grad = scattered_sum(term, strides, upper_stages(count) + [(1, 2)], place, count) * frames ** -0.5

    is_odd = odd == 1
    low = jnp.where(is_odd, from_near, from_long).astype(f32)
    high = jnp.where(is_odd, from_long, from_near).astype(f32)
    rim_sum = jnp.concatenate([low, high], axis=1)
    return dq[None], (dk + rim_sum[0]).astype(bf16)[None], (dv + rim_sum[1]).astype(bf16)[None], wo_grad


def solution(mesh):
    spread = P("dp", "seq", None)
    return jax.shard_map(
        on_device,
        mesh=mesh,
        in_specs=(spread, spread, spread, spread, P()),
        out_specs=(spread, spread, spread, P("seq", "dp")),
        check_vma=False,
    )
```

```python
import jax
import jax.numpy as jnp
from jax import lax
from jax.experimental import pallas as pl
from jax.experimental.pallas import tpu as pltpu
from jax.sharding import PartitionSpec as P


HEAD_DIM = 64
HALF = 128
PAIR = 2 * HEAD_DIM
UNROLL = 4
masked_score = -1e30
f32 = jnp.float32
bf16 = jnp.bfloat16


NN = ((1,), (0,))
NT = ((1,), (1,))
TN = ((0,), (0,))

in_vmem = pl.BlockSpec(memory_space=pltpu.VMEM)
in_smem = pl.BlockSpec(memory_space=pltpu.SMEM)


def contract(a, b, dims):
    return lax.dot_general(a, b, (dims, ((), ())), preferred_element_type=f32)


def half_kernel(meta_ref, bias_ref, q_ref, da_ref, k_ref, v_ref, rim_ref, *rest):
    earlier, outs = rest[:-6], rest[-6:]
    keep_ref, send_ref, dq_ref, dk_ref, dv_ref, back_ref = outs
    side = meta_ref[0]
    y_digit = meta_ref[1]
    scale = HEAD_DIM ** -0.5
    first_head = lax.broadcasted_iota(jnp.int32, (HALF, PAIR), 1) < HEAD_DIM
    ahead = lax.broadcasted_iota(jnp.int32, (HALF, 2 * HALF), 0) - lax.broadcasted_iota(jnp.int32, (HALF, 2 * HALF), 1) % HALF
    in_rim = ahead * (1 - 2 * side) >= side
    near_rows = pl.ds(pl.multiple_of(side * HALF, HALF), HALF)
    far_rows = pl.ds(pl.multiple_of((1 - side) * HALF, HALF), HALF)
    if earlier:
        dq_ref[far_rows, :] = earlier[0][far_rows, :]

    def one(pair, place, at_ref):
        cols = pl.ds(pl.multiple_of(pair * PAIR, PAIR), PAIR)
        q_one = q_ref[near_rows, cols].astype(f32) * scale
        da_one = da_ref[near_rows, cols].astype(f32)
        q_two = jnp.concatenate([jnp.where(first_head, q_one, 0.0), jnp.where(first_head, 0.0, q_one)], axis=0).astype(bf16)
        da_two = jnp.concatenate([jnp.where(first_head, da_one, 0.0), jnp.where(first_head, 0.0, da_one)], axis=0).astype(bf16)
        keys = jnp.concatenate([rim_ref[0, :, cols], k_ref[near_rows, cols], k_ref[far_rows, cols]], axis=0)
        vals = jnp.concatenate([rim_ref[1, :, cols], v_ref[near_rows, cols], v_ref[far_rows, cols]], axis=0)
        score = contract(keys, q_two, NT)
        s_edge = jnp.where(in_rim, score[:HALF] + bias_ref[0], score[2 * HALF :])
        s_near = score[HALF : 2 * HALF]
        top = jnp.max(jnp.maximum(s_edge, s_near), axis=0, keepdims=True)
        e_edge = jnp.exp(s_edge - top)
        e_near = jnp.exp(s_near - top)
        inv = 1.0 / jnp.sum(e_edge + e_near, axis=0, keepdims=True)
        p_edge = e_edge * inv
        p_near = e_near * inv
        p_all = jnp.concatenate([jnp.where(in_rim, p_edge, 0.0).astype(bf16), p_near.astype(bf16),
                                 jnp.where(in_rim, 0.0, p_edge).astype(bf16)], axis=0)
        dp = contract(vals, da_two, NT)
        d_edge = jnp.where(in_rim, dp[:HALF], dp[2 * HALF :])
        d_near = dp[HALF : 2 * HALF]
        delta = jnp.sum(p_edge * d_edge + p_near * d_near, axis=0, keepdims=True)
        ds_edge = p_edge * (d_edge - delta)
        ds_near = p_near * (d_near - delta)
        ds_all = jnp.concatenate([jnp.where(in_rim, ds_edge, 0.0).astype(bf16), ds_near.astype(bf16),
                                  jnp.where(in_rim, 0.0, ds_edge).astype(bf16)], axis=0)
        at = contract(vals, p_all, TN)
        start = pl.multiple_of(place * PAIR, PAIR)
        at_ref[pl.ds(start, HEAD_DIM), :] = at[:HEAD_DIM, :HALF].astype(bf16)
        at_ref[pl.ds(start + HEAD_DIM, HEAD_DIM), :] = at[HEAD_DIM:, HALF:].astype(bf16)
        dqt = contract(keys, ds_all, TN)
        dqt = jnp.concatenate([dqt[:HEAD_DIM, :HALF], dqt[HEAD_DIM:, HALF:]], axis=0) * scale
        dq_ref[near_rows, cols] = dqt.T.astype(bf16)
        for which, (ref, left, right) in enumerate(((dk_ref, ds_all, q_two), (dv_ref, p_all, da_two))):
            part = contract(left, right, NN)
            back_ref[which, :, cols] = part[:HALF].astype(bf16)
            near, far = part[HALF : 2 * HALF], part[2 * HALF :]
            if earlier:
                near = near + earlier[1 + which][near_rows, cols]
                far = far + earlier[1 + which][far_rows, cols]
            ref[near_rows, cols] = near
            ref[far_rows, cols] = far

    def body(place, carry):
        one(2 * place + y_digit, place, keep_ref)
        one(2 * place + 1 - y_digit, place, send_ref)
        return carry

    lax.fori_loop(0, q_ref.shape[1] // (2 * PAIR), body, 0, unroll=UNROLL)


def half_attention(meta, bias, q, da, k, v, rim, earlier):
    rows, width = q.shape
    operands = [meta, bias, q, da, k, v, rim] + (list(earlier) if earlier else [])
    return pl.pallas_call(
        half_kernel,
        in_specs=[in_smem, in_smem] + [in_vmem] * (len(operands) - 2),
        out_specs=[in_vmem] * 6,
        out_shape=[
            jax.ShapeDtypeStruct((width // 2, HALF), bf16),
            jax.ShapeDtypeStruct((width // 2, HALF), bf16),
            jax.ShapeDtypeStruct((rows, width), bf16),
            jax.ShapeDtypeStruct((rows, width), f32),
            jax.ShapeDtypeStruct((rows, width), f32),
            jax.ShapeDtypeStruct((2, HALF, width), bf16),
        ],
        cost_estimate=pl.CostEstimate(flops=12 * HALF * 3 * HALF * width, bytes_accessed=16 * rows * width,
                                      transcendentals=HALF * 2 * HALF * width // HEAD_DIM),
        compiler_params=pltpu.CompilerParams(vmem_limit_bytes=24 << 20),
    )(*operands)


def rim_kernel(side_ref, k_ref, v_ref, out_ref):
    out_ref[0] = k_ref[...]
    out_ref[1] = v_ref[...]


def packed_rim(side, k, v):
    width = k.shape[1]
    block = pl.BlockSpec((HALF, width), lambda i, s: (s[0], 0))
    return pl.pallas_call(
        rim_kernel,
        grid_spec=pltpu.PrefetchScalarGridSpec(
            num_scalar_prefetch=1, grid=(1,), in_specs=[block, block],
            out_specs=pl.BlockSpec((2, HALF, width), lambda i, s: (0, 0, 0)),
        ),
        out_shape=jax.ShapeDtypeStruct((2, HALF, width), bf16),
    )(side, k, v)


def product_kernel(meta_ref, *refs):
    side, mine, z_digit = meta_ref[0], meta_ref[2], meta_ref[3]
    ats, (g_ref, g_dp_ref, g_y_ref, g_y_dp_ref), outs = refs[:8], refs[8:12], refs[12:]
    own = outs[0].shape[1]
    size = outs[0].shape[0]
    rights = []
    for row in (side, 1 - side):
        rows = pl.ds(pl.multiple_of(row * HALF, HALF), HALF)
        cols = pl.ds(pl.multiple_of(mine * own, own), own)
        rights += [g_ref[rows, cols], g_y_ref[rows, cols], g_dp_ref[rows, :], g_y_dp_ref[rows, :]]
    right = jnp.concatenate(rights, axis=0)
    for step, out_ref in enumerate(outs):
        rows = pl.ds(pl.multiple_of((z_digit ^ step) * size, size), size)
        left = jnp.concatenate([ref[rows, :] for ref in ats], axis=1)
        out_ref[...] = contract(left, right, NN).astype(out_ref.dtype)


def products(meta, ats, gs, radix, own):
    size = ats[0].shape[0] // radix
    return pl.pallas_call(
        product_kernel,
        in_specs=[in_smem] + [in_vmem] * 12,
        out_specs=[in_vmem] * radix,
        out_shape=[jax.ShapeDtypeStruct((size, own), f32)] + [jax.ShapeDtypeStruct((size, own), bf16)] * (radix - 1),
        compiler_params=pltpu.CompilerParams(vmem_limit_bytes=12 << 20),
        name="product",
    )(meta, *ats, *gs)


def sum_kernel(meta_ref, own_ref, *refs):
    pieces, (keep_ref, send_ref) = refs[:-2], refs[-2:]
    half = keep_ref.shape[0]
    for x_digit, ref in ((meta_ref[4], keep_ref), (1 - meta_ref[4], send_ref)):
        rows = pl.ds(pl.multiple_of(x_digit * half, half), half)
        total = own_ref[rows, :]
        for piece in pieces:
            total = total + piece[rows, :].astype(f32)
        ref[...] = total.astype(ref.dtype)


def summed(meta, own, pieces):
    half = own.shape[0] // 2
    return pl.pallas_call(
        sum_kernel,
        in_specs=[in_smem] + [in_vmem] * (1 + len(pieces)),
        out_specs=[in_vmem] * 2,
        out_shape=[jax.ShapeDtypeStruct((half, own.shape[1]), f32), jax.ShapeDtypeStruct((half, own.shape[1]), bf16)],
        compiler_params=pltpu.CompilerParams(vmem_limit_bytes=12 << 20),
        name="summed",
    )(meta, own, *pieces)


def join_kernel(meta_ref, dk_ref, dv_ref, long_ref, near_ref, dk_out, dv_out):
    side = meta_ref[0]
    for row, rim in ((side, long_ref), (1 - side, near_ref)):
        rows = pl.ds(pl.multiple_of(row * HALF, HALF), HALF)
        dk_out[rows, :] = (dk_ref[rows, :] + rim[0].astype(f32)).astype(bf16)
        dv_out[rows, :] = (dv_ref[rows, :] + rim[1].astype(f32)).astype(bf16)


def joined(meta, dk, dv, from_long, from_near):
    shape = jax.ShapeDtypeStruct(dk.shape, bf16)
    return pl.pallas_call(
        join_kernel,
        in_specs=[in_smem] + [in_vmem] * 4,
        out_specs=[in_vmem] * 2,
        out_shape=[shape, shape],
        compiler_params=pltpu.CompilerParams(vmem_limit_bytes=12 << 20),
        name="joined",
    )(meta, dk, dv, from_long, from_near)


def swapped(value, stride, count):
    return lax.ppermute(value, "seq", [(i, i ^ stride) for i in range(count)])


def turned(value, count):
    return [lax.ppermute(value, "dp", [(i, (i + step) % count) for i in range(count)]) for step in range(1, count)]


def upper_stages(count):
    found = []
    stride = 4
    while stride < count:
        radix = min(4, count // stride)
        found.append((stride, radix))
        stride *= radix
    return found


def scattered_sum(block, strides, stages, me, count):
    tail = list(block.shape[-2:])
    left = strides
    for number, (stride, radix) in enumerate(stages):
        axis = [place for place, (low, size) in enumerate(left) if low <= stride < low * size][0]
        base, total = left[axis]
        inner = stride // base
        outer = total // (inner * radix)
        dims = [size for _, size in left]
        block = block.reshape(dims[:axis] + [outer, radix, inner] + dims[axis + 1 :] + tail)
        digit = (me // stride) % radix
        received = []
        for step in range(1, radix):
            pairs = [(source, source ^ (step * stride)) for source in range(count)]
            sent = lax.dynamic_index_in_dim(block, digit ^ step, axis + 1, keepdims=False)
            received.append(lax.ppermute(sent, "seq", pairs))
        total_sum = lax.dynamic_index_in_dim(block, digit, axis + 1, keepdims=False).astype(f32)
        for piece in received:
            total_sum = total_sum + piece.astype(f32)
        block = total_sum if number == len(stages) - 1 else total_sum.astype(bf16)
        left = left[:axis] + [(stride * radix, outer), (base, inner)] + left[axis + 1 :]
        keep = [(low, size) for low, size in left if size > 1]
        block = block.reshape([size for _, size in keep] + tail)
        left = keep
    return block.reshape(tail)


def on_device(queries, keys, values, out_grad, out_weight):
    q, k, v, g = queries[0], keys[0], values[0], out_grad[0]
    rows, width = q.shape
    assert rows == 2 * HALF
    count = lax.axis_size("seq")
    dp_count = lax.axis_size("dp")
    assert count >= 8 and count & (count - 1) == 0
    place = lax.axis_index("seq")
    mine = lax.axis_index("dp")
    odd = place % 2
    y_digit = (place // 2) % 2
    sides = (odd, 1 - odd)
    long_pairs = [(i, i + 1 if i % 2 else i - 1) for i in range(1, count - 1)]
    near_pairs = [(i, i ^ 1) for i in range(count)]
    block = width // count
    own_width = width // dp_count
    stages = upper_stages(count)
    direct = 2 * block == PAIR and len(stages) == 1 and dp_count == 2
    metas = [jnp.stack([side, y_digit if direct else 0 * y_digit, mine, place // 4 % stages[0][1], odd]).astype(jnp.int32) for side in sides]
    alone = [jnp.where(side == 0, place == 0, place == count - 1) for side in sides]
    bias = [jnp.where(one, masked_score, 0.0).astype(f32).reshape(1) for one in alone]

    rim1 = packed_rim(metas[0][:1], k, v)
    first_rim = lax.ppermute(rim1, "seq", long_pairs)
    dattn = contract(g, out_weight, NT).astype(bf16)
    rim2 = packed_rim(metas[1][:1], k, v)
    rim2, dattn = lax.optimization_barrier((rim2, dattn))
    second_rim = lax.ppermute(rim2, "seq", near_pairs)

    def other_half(array):
        return lax.dynamic_slice_in_dim(array, (mine + 1) % dp_count * own_width, own_width, 1)

    if direct:
        g_y = swapped(g, 2, count)
        g_dp = turned(other_half(g), dp_count)[0]
        g_y_dp = turned(other_half(g_y), dp_count)[0]
        gs = [g, g_dp, g_y, g_y_dp]

    keep1, send1, dq, dk, dv, back1 = half_attention(metas[0], bias[0], q, dattn, k, v, first_rim, None)
    from_long = lax.ppermute(back1, "seq", long_pairs)
    if direct:
        at_y1 = swapped(send1, 2, count)
        at_dp1 = turned(keep1, dp_count)[0]
        at_y_dp1 = turned(at_y1, dp_count)[0]
    keep2, send2, dq, dk, dv, back2 = half_attention(metas[1], bias[1], q, dattn, k, v, second_rim, (dq, dk, dv))
    if direct:
        at_y2 = swapped(send2, 2, count)
        at_dp2 = turned(keep2, dp_count)[0]
        at_y_dp2 = turned(at_y2, dp_count)[0]
    from_near = lax.ppermute(back2, "seq", near_pairs)

    frames = rows * count * dp_count
    if direct:
        ats = [keep1, at_y1, at_dp1, at_y_dp1, keep2, at_y2, at_dp2, at_y_dp2]
        terms = products(metas[0], ats, gs, count // 4, own_width)
        pieces = []
        for step in range(1, count // 4):
            pieces.append(swapped(terms[step], 4 * step, count))
        kept, sent = summed(metas[0], terms[0], pieces)
        wo_grad = kept + swapped(sent, 1, count).astype(f32)
    else:
        wo_grad = general_sum((keep1, send1), (keep2, send2), g, sides, place, mine, y_digit, count, dp_count)
    dk, dv = joined(metas[0], dk, dv, from_long, from_near)
    return dq[None], dk[None], dv[None], wo_grad * frames ** -0.5


def general_sum(first, second, g, sides, place, mine, y_digit, count, dp_count):
    width = g.shape[1]
    block = width // count
    own_width = width // dp_count
    g_parts = [lax.dynamic_slice_in_dim(g, mine * own_width, own_width, 1)]
    for step in range(1, dp_count):
        sent = lax.dynamic_slice_in_dim(g, (mine + step) % dp_count * own_width, own_width, 1)
        g_parts.append(lax.ppermute(sent, "dp", [(i, (i + step) % dp_count) for i in range(dp_count)]))
    g_here = jnp.stack(g_parts)
    g_there = swapped(g_here, 2, count)
    term = None
    for side, (even, odd) in zip(sides, (first, second)):
        at = jnp.stack([even.reshape(-1, PAIR, HALF), odd.reshape(-1, PAIR, HALF)], axis=1)
        parts = at.reshape(count // 4, 2, 2 * block, HALF)
        kept = lax.dynamic_index_in_dim(parts, y_digit, 1, keepdims=False).reshape(width // 2, HALF)
        sent = lax.dynamic_index_in_dim(parts, 1 - y_digit, 1, keepdims=False).reshape(width // 2, HALF)
        pack = jnp.stack([kept, swapped(sent, 2, count)])
        for utt, part in enumerate([pack] + turned(pack, dp_count)):
            for row, source in ((0, g_here), (1, g_there)):
                piece = contract(part[row], lax.dynamic_slice_in_dim(source[utt], side * HALF, HALF, 0), NN)
                term = piece if term is None else term + piece
    term = term.astype(bf16).reshape(count // 4, 2, block, own_width)
    return scattered_sum(term, [(4, count // 4), (1, 2)], upper_stages(count) + [(1, 2)], place, count)


def solution(mesh):
    spread = P("dp", "seq", None)
    return jax.shard_map(
        on_device,
        mesh=mesh,
        in_specs=(spread, spread, spread, spread, P()),
        out_specs=(spread, spread, spread, P("seq", "dp")),
        check_vma=False,
    )
```

```python
import jax
import jax.numpy as jnp
from jax import lax
from jax.experimental import pallas as pl
from jax.experimental.pallas import tpu as pltpu
from jax.sharding import PartitionSpec as P


HEAD_DIM = 64
HALF = 128
PAIR = 2 * HEAD_DIM
masked_score = -1e30
f32 = jnp.float32
bf16 = jnp.bfloat16


NN = ((1,), (0,))
NT = ((1,), (1,))
TN = ((0,), (0,))

in_vmem = pl.BlockSpec(memory_space=pltpu.VMEM)
in_smem = pl.BlockSpec(memory_space=pltpu.SMEM)


def contract(a, b, dims):
    return lax.dot_general(a, b, (dims, ((), ())), preferred_element_type=f32)


def half_kernel(meta_ref, bias_ref, q_hbm, da_hbm, k_hbm, v_hbm, rim_hbm, keep_ref, send_ref, back_ref, dq_hbm, dk_hbm, dv_hbm,
                one_ref, wide_ref, two_ref, score_ref, dp_ref, p_ref, ds_ref, dq_ref, own_ref, in_sem, out_sem):
    side = meta_ref[0]
    y_digit = meta_ref[1]
    scale = HEAD_DIM ** -0.5
    near_rows = pl.ds(pl.multiple_of(side * HALF, HALF), HALF)
    far_rows = pl.ds(pl.multiple_of((1 - side) * HALF, HALF), HALF)
    pairs = one_ref.shape[0]

    def columns(number):
        pair = 2 * (number // 2) + (y_digit if number % 2 == 0 else 1 - y_digit)
        return pl.ds(pl.multiple_of(pair * PAIR, PAIR), PAIR)

    def fetches(number):
        cols = columns(number)
        found = []
        for which, (thin, thick) in enumerate(((q_hbm, k_hbm), (da_hbm, v_hbm))):
            found.append((thin.at[near_rows, cols], one_ref.at[number, which]))
            found.append((rim_hbm.at[which, :, cols], wide_ref.at[number, which, pl.ds(0, HALF)]))
            found.append((thick.at[near_rows, cols], wide_ref.at[number, which, pl.ds(HALF, HALF)]))
            found.append((thick.at[far_rows, cols], wide_ref.at[number, which, pl.ds(2 * HALF, HALF)]))
        return [pltpu.make_async_copy(a, b, in_sem.at[number, place]) for place, (a, b) in enumerate(found)]

    def stores(number):
        cols = columns(number)
        found = [(dq_ref.at[number], dq_hbm.at[:, cols]), (own_ref.at[number, 0], dk_hbm.at[:, cols]), (own_ref.at[number, 1], dv_hbm.at[:, cols])]
        return [pltpu.make_async_copy(a, b, out_sem.at[number, place]) for place, (a, b) in enumerate(found)]

    def multiply(number):
        for copy in fetches(number):
            copy.wait()
        slot = number % 3
        first_head = lax.broadcasted_iota(jnp.int32, (HALF, PAIR), 1) < HEAD_DIM
        for which, (factor, out) in enumerate(((scale, score_ref), (1.0, dp_ref))):
            one = one_ref[number, which].astype(f32) * factor
            two_ref[slot, which, :HALF] = jnp.where(first_head, one, 0.0).astype(bf16)
            two_ref[slot, which, HALF:] = jnp.where(first_head, 0.0, one).astype(bf16)
            out[number % 2] = contract(wide_ref[number, which], two_ref[slot, which], NT)

    def weigh(number):
        slot = number % 2
        ahead = lax.broadcasted_iota(jnp.int32, (HALF, 2 * HALF), 0) - lax.broadcasted_iota(jnp.int32, (HALF, 2 * HALF), 1) % HALF
        in_rim = ahead * (1 - 2 * side) >= side
        s_edge = jnp.where(in_rim, score_ref[slot, :HALF] + bias_ref[0], score_ref[slot, 2 * HALF :])
        s_near = score_ref[slot, HALF : 2 * HALF]
        top = jnp.max(jnp.maximum(s_edge, s_near), axis=0, keepdims=True)
        e_edge = jnp.exp(s_edge - top)
        e_near = jnp.exp(s_near - top)
        inv = 1.0 / jnp.sum(e_edge + e_near, axis=0, keepdims=True)
        p_edge = e_edge * inv
        p_near = e_near * inv
        d_edge = jnp.where(in_rim, dp_ref[slot, :HALF], dp_ref[slot, 2 * HALF :])
        d_near = dp_ref[slot, HALF : 2 * HALF]
        delta = jnp.sum(p_edge * d_edge + p_near * d_near, axis=0, keepdims=True)
        for ref, edge, near in ((p_ref, p_edge, p_near), (ds_ref, p_edge * (d_edge - delta), p_near * (d_near - delta))):
            ref[slot, :HALF] = jnp.where(in_rim, edge, 0.0).astype(bf16)
            ref[slot, HALF : 2 * HALF] = near.astype(bf16)
            ref[slot, 2 * HALF :] = jnp.where(in_rim, 0.0, edge).astype(bf16)

    def spread(number):
        slot = number % 2
        at_ref = send_ref if number % 2 else keep_ref
        start = number // 2 * PAIR
        at = contract(wide_ref[number, 1], p_ref[slot], TN)
        at_ref[start : start + HEAD_DIM, :] = at[:HEAD_DIM, :HALF].astype(bf16)
        at_ref[start + HEAD_DIM : start + PAIR, :] = at[HEAD_DIM:, HALF:].astype(bf16)
        for which, left in enumerate((ds_ref, p_ref)):
            part = contract(left[slot], two_ref[number % 3, which], NN)
            back_ref[which, :, columns(number)] = part[:HALF].astype(bf16)
            own_ref[number, which, near_rows, :] = part[HALF : 2 * HALF].astype(bf16)
            own_ref[number, which, far_rows, :] = part[2 * HALF :].astype(bf16)
        dqt = contract(wide_ref[number, 0], ds_ref[slot], TN)
        dqt = jnp.concatenate([dqt[:HEAD_DIM, :HALF], dqt[HEAD_DIM:, HALF:]], axis=0) * scale
        dq_ref[number] = dqt.T.astype(bf16)
        for copy in stores(number):
            copy.start()

    for number in range(pairs):
        for copy in fetches(number):
            copy.start()
    for step in range(pairs + 2):
        if step < pairs:
            multiply(step)
        if 0 <= step - 2:
            spread(step - 2)
        if 0 <= step - 1 < pairs:
            weigh(step - 1)
    for number in range(pairs):
        for copy in stores(number):
            copy.wait()


def half_attention(meta, bias, q, da, k, v, rim):
    rows, width = q.shape
    pairs = width // PAIR
    in_hbm = pl.BlockSpec(memory_space=pltpu.HBM)
    held = [pltpu.with_memory_space_constraint(array, pltpu.HBM) for array in (q, da, k, v)]
    return pl.pallas_call(
        half_kernel,
        in_specs=[in_smem, in_smem] + [in_hbm] * 4 + [pl.BlockSpec(memory_space=pl.ANY)],
        out_specs=[in_vmem] * 3 + [in_hbm] * 3,
        out_shape=[
            jax.ShapeDtypeStruct((width // 2, HALF), bf16),
            jax.ShapeDtypeStruct((width // 2, HALF), bf16),
            jax.ShapeDtypeStruct((2, HALF, width), bf16),
            pltpu.HBM((HALF, width), bf16),
            pltpu.HBM((rows, width), bf16),
            pltpu.HBM((rows, width), bf16),
        ],
        scratch_shapes=[
            pltpu.VMEM((pairs, 2, HALF, PAIR), bf16),
            pltpu.VMEM((pairs, 2, 3 * HALF, PAIR), bf16),
            pltpu.VMEM((3, 2, 2 * HALF, PAIR), bf16),
            pltpu.VMEM((2, 3 * HALF, 2 * HALF), f32),
            pltpu.VMEM((2, 3 * HALF, 2 * HALF), f32),
            pltpu.VMEM((2, 3 * HALF, 2 * HALF), bf16),
            pltpu.VMEM((2, 3 * HALF, 2 * HALF), bf16),
            pltpu.VMEM((pairs, HALF, PAIR), bf16),
            pltpu.VMEM((pairs, 2, rows, PAIR), bf16),
            pltpu.SemaphoreType.DMA((pairs, 8)),
            pltpu.SemaphoreType.DMA((pairs, 3)),
        ],
        cost_estimate=pl.CostEstimate(flops=12 * HALF * 3 * HALF * width, bytes_accessed=16 * rows * width,
                                      transcendentals=HALF * 2 * HALF * width // HEAD_DIM),
        compiler_params=pltpu.CompilerParams(vmem_limit_bytes=24 << 20),
    )(meta, bias, *held, rim)


def rim_kernel(side_ref, k_ref, v_ref, out_ref):
    out_ref[0] = k_ref[...]
    out_ref[1] = v_ref[...]


def packed_rim(side, k, v):
    width = k.shape[1]
    block = pl.BlockSpec((HALF, width), lambda i, s: (s[0], 0))
    return pl.pallas_call(
        rim_kernel,
        grid_spec=pltpu.PrefetchScalarGridSpec(
            num_scalar_prefetch=1, grid=(1,), in_specs=[block, block],
            out_specs=pl.BlockSpec((2, HALF, width), lambda i, s: (0, 0, 0)),
        ),
        out_shape=jax.ShapeDtypeStruct((2, HALF, width), bf16),
    )(side, k, v)


def product_kernel(meta_ref, *refs):
    side, mine, z_digit = meta_ref[0], meta_ref[2], meta_ref[3]
    ats, (g_ref, g_dp_ref, g_y_ref, g_y_dp_ref), outs = refs[:8], refs[8:12], refs[12:]
    own = outs[0].shape[1]
    size = outs[0].shape[0]
    rights = []
    for row in (side, 1 - side):
        rows = pl.ds(pl.multiple_of(row * HALF, HALF), HALF)
        cols = pl.ds(pl.multiple_of(mine * own, own), own)
        rights += [ref[rows, cols] for ref in (g_ref, g_y_ref, g_dp_ref, g_y_dp_ref)]
    right = jnp.concatenate(rights, axis=0)
    for step, out_ref in enumerate(outs):
        rows = pl.ds(pl.multiple_of((z_digit ^ step) * size, size), size)
        left = jnp.concatenate([ref[rows, :] for ref in ats], axis=1)
        out_ref[...] = contract(left, right, NN).astype(out_ref.dtype)


def products(meta, ats, gs, radix, own):
    size = ats[0].shape[0] // radix
    return pl.pallas_call(
        product_kernel,
        in_specs=[in_smem] + [in_vmem] * 12,
        out_specs=[in_vmem] * radix,
        out_shape=[jax.ShapeDtypeStruct((size, own), f32)] + [jax.ShapeDtypeStruct((size, own), bf16)] * (radix - 1),
        compiler_params=pltpu.CompilerParams(vmem_limit_bytes=12 << 20),
        name="product",
    )(meta, *ats, *gs)


def sum_kernel(meta_ref, own_ref, *refs):
    pieces, (keep_ref, send_ref) = refs[:-2], refs[-2:]
    half = keep_ref.shape[0]
    for x_digit, ref in ((meta_ref[4], keep_ref), (1 - meta_ref[4], send_ref)):
        rows = pl.ds(pl.multiple_of(x_digit * half, half), half)
        total = own_ref[rows, :]
        for piece in pieces:
            total = total + piece[rows, :].astype(f32)
        ref[...] = total.astype(ref.dtype)


def summed(meta, own, pieces):
    half = own.shape[0] // 2
    return pl.pallas_call(
        sum_kernel,
        in_specs=[in_smem] + [in_vmem] * (1 + len(pieces)),
        out_specs=[in_vmem] * 2,
        out_shape=[jax.ShapeDtypeStruct((half, own.shape[1]), f32), jax.ShapeDtypeStruct((half, own.shape[1]), bf16)],
        compiler_params=pltpu.CompilerParams(vmem_limit_bytes=12 << 20),
        name="summed",
    )(meta, own, *pieces)


def join_kernel(meta_ref, dq1_ref, dk1_ref, dv1_ref, dq2_ref, dk2_ref, dv2_ref, long_ref, near_ref, dq_out, dk_out, dv_out):
    side = meta_ref[0]
    for row, rim, dq_ref in ((side, long_ref, dq1_ref), (1 - side, near_ref, dq2_ref)):
        rows = pl.ds(pl.multiple_of(row * HALF, HALF), HALF)
        dq_out[rows, :] = dq_ref[...]
        for which, (one, two, out) in enumerate(((dk1_ref, dk2_ref, dk_out), (dv1_ref, dv2_ref, dv_out))):
            total = one[rows, :].astype(f32) + two[rows, :].astype(f32) + rim[which].astype(f32)
            out[rows, :] = total.astype(bf16)


def joined(meta, own1, own2, from_long, from_near):
    shape = jax.ShapeDtypeStruct(own1[1].shape, bf16)
    return pl.pallas_call(
        join_kernel,
        in_specs=[in_smem] + [in_vmem] * 8,
        out_specs=[in_vmem] * 3,
        out_shape=[shape] * 3,
        compiler_params=pltpu.CompilerParams(vmem_limit_bytes=12 << 20),
        name="joined",
    )(meta, *own1, *own2, from_long, from_near)


def swapped(value, stride, count):
    return lax.ppermute(value, "seq", [(i, i ^ stride) for i in range(count)])


def turned(value, count):
    return [lax.ppermute(value, "dp", [(i, (i + step) % count) for i in range(count)]) for step in range(1, count)]


def upper_stages(count):
    found = []
    stride = 4
    while stride < count:
        radix = min(4, count // stride)
        found.append((stride, radix))
        stride *= radix
    return found


def scattered_sum(block, strides, stages, me, count):
    tail = list(block.shape[-2:])
    left = strides
    for number, (stride, radix) in enumerate(stages):
        axis = [place for place, (low, size) in enumerate(left) if low <= stride < low * size][0]
        base, total = left[axis]
        inner = stride // base
        outer = total // (inner * radix)
        dims = [size for _, size in left]
        block = block.reshape(dims[:axis] + [outer, radix, inner] + dims[axis + 1 :] + tail)
        digit = (me // stride) % radix
        received = []
        for step in range(1, radix):
            pairs = [(source, source ^ (step * stride)) for source in range(count)]
            sent = lax.dynamic_index_in_dim(block, digit ^ step, axis + 1, keepdims=False)
            received.append(lax.ppermute(sent, "seq", pairs))
        total_sum = lax.dynamic_index_in_dim(block, digit, axis + 1, keepdims=False).astype(f32)
        for piece in received:
            total_sum = total_sum + piece.astype(f32)
        block = total_sum if number == len(stages) - 1 else total_sum.astype(bf16)
        left = left[:axis] + [(stride * radix, outer), (base, inner)] + left[axis + 1 :]
        keep = [(low, size) for low, size in left if size > 1]
        block = block.reshape([size for _, size in keep] + tail)
        left = keep
    return block.reshape(tail)


def on_device(queries, keys, values, out_grad, out_weight):
    q, k, v, g = queries[0], keys[0], values[0], out_grad[0]
    rows, width = q.shape
    assert rows == 2 * HALF
    count = lax.axis_size("seq")
    dp_count = lax.axis_size("dp")
    assert count >= 8 and count & (count - 1) == 0
    place = lax.axis_index("seq")
    mine = lax.axis_index("dp")
    odd = place % 2
    y_digit = (place // 2) % 2
    sides = (odd, 1 - odd)
    long_pairs = [(i, i + 1 if i % 2 else i - 1) for i in range(1, count - 1)]
    near_pairs = [(i, i ^ 1) for i in range(count)]
    block = width // count
    own_width = width // dp_count
    stages = upper_stages(count)
    direct = 2 * block == PAIR and len(stages) == 1 and dp_count == 2
    metas = [jnp.stack([side, y_digit if direct else 0 * y_digit, mine, place // 4 % stages[0][1], odd]).astype(jnp.int32) for side in sides]
    alone = [jnp.where(side == 0, place == 0, place == count - 1) for side in sides]
    bias = [jnp.where(one, masked_score, 0.0).astype(f32).reshape(1) for one in alone]

    rim1 = packed_rim(metas[0][:1], k, v)
    first_rim = lax.ppermute(rim1, "seq", long_pairs)
    dattn = contract(g, out_weight, NT).astype(bf16)
    rim2 = packed_rim(metas[1][:1], k, v)
    rim2, dattn = lax.optimization_barrier((rim2, dattn))
    second_rim = lax.ppermute(rim2, "seq", near_pairs)

    if direct:
        g_y = swapped(g, 2, count)
        g_dp = turned(g, dp_count)[0]
        g_y_dp = turned(g_y, dp_count)[0]
        gs = [g, g_dp, g_y, g_y_dp]

    keep1, send1, back1, *own1 = half_attention(metas[0], bias[0], q, dattn, k, v, first_rim)
    from_long = lax.ppermute(back1, "seq", long_pairs)
    if direct:
        at_y1 = swapped(send1, 2, count)
        at_dp1 = turned(keep1, dp_count)[0]
        at_y_dp1 = turned(at_y1, dp_count)[0]
    keep2, send2, back2, *own2 = half_attention(metas[1], bias[1], q, dattn, k, v, second_rim)
    if direct:
        at_y2 = swapped(send2, 2, count)
        at_dp2 = turned(keep2, dp_count)[0]
        at_y_dp2 = turned(at_y2, dp_count)[0]
    from_near = lax.ppermute(back2, "seq", near_pairs)

    frames = rows * count * dp_count
    if direct:
        ats = [keep1, at_y1, at_dp1, at_y_dp1, keep2, at_y2, at_dp2, at_y_dp2]
        terms = products(metas[0], ats, gs, count // 4, own_width)
        pieces = []
        for step in range(1, count // 4):
            pieces.append(swapped(terms[step], 4 * step, count))
        kept, sent = summed(metas[0], terms[0], pieces)
        wo_grad = kept + swapped(sent, 1, count).astype(f32)
    else:
        wo_grad = general_sum((keep1, send1), (keep2, send2), g, sides, place, mine, y_digit, count, dp_count)
    dq, dk, dv = joined(metas[0], own1, own2, from_long, from_near)
    return dq[None], dk[None], dv[None], wo_grad * frames ** -0.5


def general_sum(first, second, g, sides, place, mine, y_digit, count, dp_count):
    width = g.shape[1]
    block = width // count
    own_width = width // dp_count
    g_parts = [lax.dynamic_slice_in_dim(g, mine * own_width, own_width, 1)]
    for step in range(1, dp_count):
        sent = lax.dynamic_slice_in_dim(g, (mine + step) % dp_count * own_width, own_width, 1)
        g_parts.append(lax.ppermute(sent, "dp", [(i, (i + step) % dp_count) for i in range(dp_count)]))
    g_here = jnp.stack(g_parts)
    g_there = swapped(g_here, 2, count)
    term = None
    for side, (even, odd) in zip(sides, (first, second)):
        at = jnp.stack([even.reshape(-1, PAIR, HALF), odd.reshape(-1, PAIR, HALF)], axis=1)
        parts = at.reshape(count // 4, 2, 2 * block, HALF)
        kept = lax.dynamic_index_in_dim(parts, y_digit, 1, keepdims=False).reshape(width // 2, HALF)
        sent = lax.dynamic_index_in_dim(parts, 1 - y_digit, 1, keepdims=False).reshape(width // 2, HALF)
        pack = jnp.stack([kept, swapped(sent, 2, count)])
        for utt, part in enumerate([pack] + turned(pack, dp_count)):
            for row, source in ((0, g_here), (1, g_there)):
                piece = contract(part[row], lax.dynamic_slice_in_dim(source[utt], side * HALF, HALF, 0), NN)
                term = piece if term is None else term + piece
    term = term.astype(bf16).reshape(count // 4, 2, block, own_width)
    return scattered_sum(term, [(4, count // 4), (1, 2)], upper_stages(count) + [(1, 2)], place, count)


def solution(mesh):
    spread = P("dp", "seq", None)
    return jax.shard_map(
        on_device,
        mesh=mesh,
        in_specs=(spread, spread, spread, spread, P()),
        out_specs=(spread, spread, spread, P("seq", "dp")),
        check_vma=False,
    )
```

```python
import jax
import jax.numpy as jnp
from jax import lax
from jax.experimental import pallas as pl
from jax.experimental.pallas import tpu as pltpu
from jax.sharding import PartitionSpec as P


HEAD_DIM = 64
HALF = 128
PAIR = 2 * HEAD_DIM
masked_score = -1e30
f32 = jnp.float32
bf16 = jnp.bfloat16


NN = ((1,), (0,))
NT = ((1,), (1,))
TN = ((0,), (0,))

in_vmem = pl.BlockSpec(memory_space=pltpu.VMEM)
in_smem = pl.BlockSpec(memory_space=pltpu.SMEM)


def contract(a, b, dims):
    return lax.dot_general(a, b, (dims, ((), ())), preferred_element_type=f32)


def half_kernel(meta_ref, bias_ref, thin_hbm, thick_hbm, rim_hbm, keep_ref, send_ref, back_ref, dq_hbm, own_hbm,
                one_ref, wide_ref, two_ref, score_ref, dp_ref, p_ref, ds_ref, dq_ref, own_ref, in_sem, out_sem):
    side = meta_ref[0]
    y_digit = meta_ref[1]
    scale = HEAD_DIM ** -0.5
    near_rows = pl.ds(pl.multiple_of(side * HALF, HALF), HALF)
    far_rows = pl.ds(pl.multiple_of((1 - side) * HALF, HALF), HALF)
    pairs = one_ref.shape[0]

    def pair_of(number):
        return 2 * (number // 2) + (y_digit if number % 2 == 0 else 1 - y_digit)

    def fetches(number):
        pair = pair_of(number)
        found = [(thin_hbm.at[pair, :, side], one_ref.at[number])]
        for place, source in enumerate((rim_hbm.at[pair], thick_hbm.at[pair, :, side], thick_hbm.at[pair, :, 1 - side])):
            found.append((source, wide_ref.at[number, :, pl.ds(place * HALF, HALF)]))
        return [pltpu.make_async_copy(a, b, in_sem.at[number, place]) for place, (a, b) in enumerate(found)]

    def stores(number):
        pair = pair_of(number)
        found = [(dq_ref.at[number], dq_hbm.at[pair]), (own_ref.at[number], own_hbm.at[pair])]
        return [pltpu.make_async_copy(a, b, out_sem.at[number, place]) for place, (a, b) in enumerate(found)]

    def multiply(number):
        for copy in fetches(number):
            copy.wait()
        slot = number % 3
        first_head = lax.broadcasted_iota(jnp.int32, (HALF, PAIR), 1) < HEAD_DIM
        for which, (factor, out) in enumerate(((scale, score_ref), (1.0, dp_ref))):
            one = one_ref[number, which].astype(f32) * factor
            two_ref[slot, which, :HALF] = jnp.where(first_head, one, 0.0).astype(bf16)
            two_ref[slot, which, HALF:] = jnp.where(first_head, 0.0, one).astype(bf16)
            out[number % 2] = contract(wide_ref[number, which], two_ref[slot, which], NT)

    def weigh(number):
        slot = number % 2
        ahead = lax.broadcasted_iota(jnp.int32, (HALF, 2 * HALF), 0) - lax.broadcasted_iota(jnp.int32, (HALF, 2 * HALF), 1) % HALF
        in_rim = ahead * (1 - 2 * side) >= side
        s_edge = jnp.where(in_rim, score_ref[slot, :HALF] + bias_ref[0], score_ref[slot, 2 * HALF :])
        s_near = score_ref[slot, HALF : 2 * HALF]
        top = jnp.max(jnp.maximum(s_edge, s_near), axis=0, keepdims=True)
        e_edge = jnp.exp(s_edge - top)
        e_near = jnp.exp(s_near - top)
        inv = 1.0 / jnp.sum(e_edge + e_near, axis=0, keepdims=True)
        p_edge = e_edge * inv
        p_near = e_near * inv
        d_edge = jnp.where(in_rim, dp_ref[slot, :HALF], dp_ref[slot, 2 * HALF :])
        d_near = dp_ref[slot, HALF : 2 * HALF]
        delta = jnp.sum(p_edge * d_edge + p_near * d_near, axis=0, keepdims=True)
        for ref, edge, near in ((p_ref, p_edge, p_near), (ds_ref, p_edge * (d_edge - delta), p_near * (d_near - delta))):
            ref[slot, :HALF] = jnp.where(in_rim, edge, 0.0).astype(bf16)
            ref[slot, HALF : 2 * HALF] = near.astype(bf16)
            ref[slot, 2 * HALF :] = jnp.where(in_rim, 0.0, edge).astype(bf16)

    def spread(number):
        slot = number % 2
        at_ref = send_ref if number % 2 else keep_ref
        start = number // 2 * PAIR
        at = contract(wide_ref[number, 1], p_ref[slot], TN)
        at_ref[start : start + HEAD_DIM, :] = at[:HEAD_DIM, :HALF].astype(bf16)
        at_ref[start + HEAD_DIM : start + PAIR, :] = at[HEAD_DIM:, HALF:].astype(bf16)
        for which, left in enumerate((ds_ref, p_ref)):
            part = contract(left[slot], two_ref[number % 3, which], NN)
            back_ref[pair_of(number), which] = part[:HALF].astype(bf16)
            own_ref[number, which, near_rows, :] = part[HALF : 2 * HALF].astype(bf16)
            own_ref[number, which, far_rows, :] = part[2 * HALF :].astype(bf16)
        dqt = contract(wide_ref[number, 0], ds_ref[slot], TN)
        dqt = jnp.concatenate([dqt[:HEAD_DIM, :HALF], dqt[HEAD_DIM:, HALF:]], axis=0) * scale
        dq_ref[number] = dqt.T.astype(bf16)
        for copy in stores(number):
            copy.start()

    for number in range(pairs):
        for copy in fetches(number):
            copy.start()
    for step in range(pairs + 2):
        if step < pairs:
            multiply(step)
        if 0 <= step - 2:
            spread(step - 2)
        if 0 <= step - 1 < pairs:
            weigh(step - 1)
    for number in range(pairs):
        for copy in stores(number):
            copy.wait()


def half_attention(meta, bias, thin, thick, rim):
    pairs, _, blocks, _, _ = thick.shape
    rows = blocks * HALF
    width = pairs * PAIR
    in_hbm = pl.BlockSpec(memory_space=pltpu.HBM)
    held = [pltpu.with_memory_space_constraint(array, pltpu.HBM) for array in (thin, thick)]
    return pl.pallas_call(
        half_kernel,
        in_specs=[in_smem, in_smem, in_hbm, in_hbm, pl.BlockSpec(memory_space=pl.ANY)],
        out_specs=[in_vmem] * 3 + [in_hbm] * 2,
        out_shape=[
            jax.ShapeDtypeStruct((width // 2, HALF), bf16),
            jax.ShapeDtypeStruct((width // 2, HALF), bf16),
            jax.ShapeDtypeStruct((pairs, 2, HALF, PAIR), bf16),
            pltpu.HBM((pairs, HALF, PAIR), bf16),
            pltpu.HBM((pairs, 2, rows, PAIR), bf16),
        ],
        scratch_shapes=[
            pltpu.VMEM((pairs, 2, HALF, PAIR), bf16),
            pltpu.VMEM((pairs, 2, 3 * HALF, PAIR), bf16),
            pltpu.VMEM((3, 2, 2 * HALF, PAIR), bf16),
            pltpu.VMEM((2, 3 * HALF, 2 * HALF), f32),
            pltpu.VMEM((2, 3 * HALF, 2 * HALF), f32),
            pltpu.VMEM((2, 3 * HALF, 2 * HALF), bf16),
            pltpu.VMEM((2, 3 * HALF, 2 * HALF), bf16),
            pltpu.VMEM((pairs, HALF, PAIR), bf16),
            pltpu.VMEM((pairs, 2, rows, PAIR), bf16),
            pltpu.SemaphoreType.DMA((pairs, 4)),
            pltpu.SemaphoreType.DMA((pairs, 2)),
        ],
        cost_estimate=pl.CostEstimate(flops=12 * HALF * 3 * HALF * width, bytes_accessed=16 * rows * width,
                                      transcendentals=HALF * 2 * HALF * width // HEAD_DIM),
        compiler_params=pltpu.CompilerParams(vmem_limit_bytes=24 << 20),
    )(meta, bias, *held, rim)


def rim_kernel(side_ref, k_ref, v_ref, out_ref):
    for pair in range(out_ref.shape[0]):
        cols = slice(pair * PAIR, (pair + 1) * PAIR)
        out_ref[pair, 0] = k_ref[:, cols]
        out_ref[pair, 1] = v_ref[:, cols]


def packed_rim(side, k, v):
    width = k.shape[1]
    block = pl.BlockSpec((HALF, width), lambda i, s: (s[0], 0))
    shape = (width // PAIR, 2, HALF, PAIR)
    return pl.pallas_call(
        rim_kernel,
        grid_spec=pltpu.PrefetchScalarGridSpec(
            num_scalar_prefetch=1, grid=(1,), in_specs=[block, block],
            out_specs=pl.BlockSpec(shape, lambda i, s: (0, 0, 0, 0)),
        ),
        out_shape=jax.ShapeDtypeStruct(shape, bf16),
    )(side, k, v)


def prepare_kernel(meta_ref, q_ref, k_ref, v_ref, g_ref, w_ref, thin_ref, thick_ref, rim_ref):
    pairs, _, blocks, _, _ = thin_ref.shape
    for pair in range(pairs):
        cols = slice(pair * PAIR, (pair + 1) * PAIR)
        for block in range(blocks):
            rows = slice(block * HALF, (block + 1) * HALF)
            thin_ref[pair, 0, block] = q_ref[rows, cols]
            thick_ref[pair, 0, block] = k_ref[rows, cols]
            thick_ref[pair, 1, block] = v_ref[rows, cols]
        rim_rows = pl.ds(pl.multiple_of((1 - meta_ref[0]) * HALF, HALF), HALF)
        rim_ref[pair, 0] = k_ref[rim_rows, cols]
        rim_ref[pair, 1] = v_ref[rim_rows, cols]
    step = 2 * PAIR
    for col in range(0, w_ref.shape[0], step):
        part = contract(g_ref[...], w_ref[col : col + step, :], NT).astype(bf16)
        for pair in range(2):
            for block in range(blocks):
                thin_ref[col // PAIR + pair, 1, block] = part[block * HALF : (block + 1) * HALF, pair * PAIR : (pair + 1) * PAIR]


def prepared(meta, q, k, v, g, w):
    rows, width = q.shape
    pairs, blocks = width // PAIR, rows // HALF
    whole = jax.ShapeDtypeStruct((pairs, 2, blocks, HALF, PAIR), bf16)
    return pl.pallas_call(
        prepare_kernel,
        in_specs=[in_smem] + [in_vmem] * 5,
        out_specs=[in_vmem] * 3,
        out_shape=[whole, whole, jax.ShapeDtypeStruct((pairs, 2, HALF, PAIR), bf16)],
        cost_estimate=pl.CostEstimate(flops=2 * rows * width * width, bytes_accessed=14 * rows * width + 2 * width * width, transcendentals=0),
        name="prepared",
    )(meta, q, k, v, g, w)


def product_kernel(meta_ref, *refs):
    side, mine, z_digit = meta_ref[0], meta_ref[2], meta_ref[3]
    ats, (g_ref, g_dp_ref, g_y_ref, g_y_dp_ref), outs = refs[:8], refs[8:12], refs[12:]
    own = outs[0].shape[1]
    size = outs[0].shape[0]
    rights = []
    for row in (side, 1 - side):
        rows = pl.ds(pl.multiple_of(row * HALF, HALF), HALF)
        cols = pl.ds(pl.multiple_of(mine * own, own), own)
        rights += [ref[rows, cols] for ref in (g_ref, g_y_ref, g_dp_ref, g_y_dp_ref)]
    right = jnp.concatenate(rights, axis=0)
    for step, out_ref in enumerate(outs):
        rows = pl.ds(pl.multiple_of((z_digit ^ step) * size, size), size)
        left = jnp.concatenate([ref[rows, :] for ref in ats], axis=1)
        out_ref[...] = contract(left, right, NN).astype(out_ref.dtype)


def products(meta, ats, gs, radix, own):
    size = ats[0].shape[0] // radix
    return pl.pallas_call(
        product_kernel,
        in_specs=[in_smem] + [in_vmem] * 12,
        out_specs=[in_vmem] * radix,
        out_shape=[jax.ShapeDtypeStruct((size, own), f32)] + [jax.ShapeDtypeStruct((size, own), bf16)] * (radix - 1),
        compiler_params=pltpu.CompilerParams(vmem_limit_bytes=12 << 20),
        name="product",
    )(meta, *ats, *gs)


def sum_kernel(meta_ref, own_ref, *refs):
    pieces, (keep_ref, send_ref) = refs[:-2], refs[-2:]
    half = keep_ref.shape[0]
    for x_digit, ref in ((meta_ref[4], keep_ref), (1 - meta_ref[4], send_ref)):
        rows = pl.ds(pl.multiple_of(x_digit * half, half), half)
        total = own_ref[rows, :]
        for piece in pieces:
            total = total + piece[rows, :].astype(f32)
        ref[...] = total.astype(ref.dtype)


def summed(meta, own, pieces):
    half = own.shape[0] // 2
    return pl.pallas_call(
        sum_kernel,
        in_specs=[in_smem] + [in_vmem] * (1 + len(pieces)),
        out_specs=[in_vmem] * 2,
        out_shape=[jax.ShapeDtypeStruct((half, own.shape[1]), f32), jax.ShapeDtypeStruct((half, own.shape[1]), bf16)],
        compiler_params=pltpu.CompilerParams(vmem_limit_bytes=12 << 20),
        name="summed",
    )(meta, own, *pieces)


def join_kernel(meta_ref, dq1_ref, own1_ref, dq2_ref, own2_ref, long_ref, near_ref, dq_out, dk_out, dv_out):
    side = meta_ref[0]
    for row, rim, dq_ref in ((side, long_ref, dq1_ref), (1 - side, near_ref, dq2_ref)):
        rows = pl.ds(pl.multiple_of(row * HALF, HALF), HALF)
        for pair in range(dq1_ref.shape[0]):
            cols = slice(pair * PAIR, (pair + 1) * PAIR)
            dq_out[rows, cols] = dq_ref[pair]
            for which, out in enumerate((dk_out, dv_out)):
                total = own1_ref[pair, which, rows].astype(f32) + own2_ref[pair, which, rows].astype(f32)
                out[rows, cols] = (total + rim[pair, which].astype(f32)).astype(bf16)


def joined(meta, own1, own2, from_long, from_near, shape):
    out = jax.ShapeDtypeStruct(shape, bf16)
    return pl.pallas_call(
        join_kernel,
        in_specs=[in_smem] + [in_vmem] * 6,
        out_specs=[in_vmem] * 3,
        out_shape=[out] * 3,
        compiler_params=pltpu.CompilerParams(vmem_limit_bytes=12 << 20),
        name="joined",
    )(meta, *own1, *own2, from_long, from_near)


def swapped(value, stride, count):
    return lax.ppermute(value, "seq", [(i, i ^ stride) for i in range(count)])


def turned(value, count):
    return [lax.ppermute(value, "dp", [(i, (i + step) % count) for i in range(count)]) for step in range(1, count)]


def upper_stages(count):
    found = []
    stride = 4
    while stride < count:
        radix = min(4, count // stride)
        found.append((stride, radix))
        stride *= radix
    return found


def scattered_sum(block, strides, stages, me, count):
    tail = list(block.shape[-2:])
    left = strides
    for number, (stride, radix) in enumerate(stages):
        axis = [place for place, (low, size) in enumerate(left) if low <= stride < low * size][0]
        base, total = left[axis]
        inner = stride // base
        outer = total // (inner * radix)
        dims = [size for _, size in left]
        block = block.reshape(dims[:axis] + [outer, radix, inner] + dims[axis + 1 :] + tail)
        digit = (me // stride) % radix
        received = []
        for step in range(1, radix):
            pairs = [(source, source ^ (step * stride)) for source in range(count)]
            sent = lax.dynamic_index_in_dim(block, digit ^ step, axis + 1, keepdims=False)
            received.append(lax.ppermute(sent, "seq", pairs))
        total_sum = lax.dynamic_index_in_dim(block, digit, axis + 1, keepdims=False).astype(f32)
        for piece in received:
            total_sum = total_sum + piece.astype(f32)
        block = total_sum if number == len(stages) - 1 else total_sum.astype(bf16)
        left = left[:axis] + [(stride * radix, outer), (base, inner)] + left[axis + 1 :]
        keep = [(low, size) for low, size in left if size > 1]
        block = block.reshape([size for _, size in keep] + tail)
        left = keep
    return block.reshape(tail)


def on_device(queries, keys, values, out_grad, out_weight):
    q, k, v, g = queries[0], keys[0], values[0], out_grad[0]
    rows, width = q.shape
    assert rows == 2 * HALF
    count = lax.axis_size("seq")
    dp_count = lax.axis_size("dp")
    assert count >= 8 and count & (count - 1) == 0
    place = lax.axis_index("seq")
    mine = lax.axis_index("dp")
    odd = place % 2
    y_digit = (place // 2) % 2
    sides = (odd, 1 - odd)
    long_pairs = [(i, i + 1 if i % 2 else i - 1) for i in range(1, count - 1)]
    near_pairs = [(i, i ^ 1) for i in range(count)]
    block = width // count
    own_width = width // dp_count
    stages = upper_stages(count)
    direct = 2 * block == PAIR and len(stages) == 1 and dp_count == 2
    metas = [jnp.stack([side, y_digit if direct else 0 * y_digit, mine, place // 4 % stages[0][1], odd]).astype(jnp.int32) for side in sides]
    alone = [jnp.where(side == 0, place == 0, place == count - 1) for side in sides]
    bias = [jnp.where(one, masked_score, 0.0).astype(f32).reshape(1) for one in alone]

    rim1 = packed_rim(metas[0][:1], k, v)
    first_rim = lax.ppermute(rim1, "seq", long_pairs)
    thin, thick, rim2 = prepared(metas[0], q, k, v, g, out_weight)
    second_rim = lax.ppermute(rim2, "seq", near_pairs)

    if direct:
        g_y = swapped(g, 2, count)
        g_dp = turned(g, dp_count)[0]
        g_y_dp = turned(g_y, dp_count)[0]
        gs = [g, g_dp, g_y, g_y_dp]

    keep1, send1, back1, *own1 = half_attention(metas[0], bias[0], thin, thick, first_rim)
    from_long = lax.ppermute(back1, "seq", long_pairs)
    if direct:
        at_y1 = swapped(send1, 2, count)
        at_dp1 = turned(keep1, dp_count)[0]
        at_y_dp1 = turned(at_y1, dp_count)[0]
    keep2, send2, back2, *own2 = half_attention(metas[1], bias[1], thin, thick, second_rim)
    if direct:
        at_y2 = swapped(send2, 2, count)
        at_dp2 = turned(keep2, dp_count)[0]
        at_y_dp2 = turned(at_y2, dp_count)[0]
    from_near = lax.ppermute(back2, "seq", near_pairs)

    frames = rows * count * dp_count
    if direct:
        ats = [keep1, at_y1, at_dp1, at_y_dp1, keep2, at_y2, at_dp2, at_y_dp2]
        terms = products(metas[0], ats, gs, count // 4, own_width)
        pieces = []
        for step in range(1, count // 4):
            pieces.append(swapped(terms[step], 4 * step, count))
        kept, sent = summed(metas[0], terms[0], pieces)
        wo_grad = kept + swapped(sent, 1, count).astype(f32)
    else:
        wo_grad = general_sum((keep1, send1), (keep2, send2), g, sides, place, mine, y_digit, count, dp_count)
    dq, dk, dv = joined(metas[0], own1, own2, from_long, from_near, q.shape)
    return dq[None], dk[None], dv[None], wo_grad * frames ** -0.5


def general_sum(first, second, g, sides, place, mine, y_digit, count, dp_count):
    width = g.shape[1]
    block = width // count
    own_width = width // dp_count
    g_parts = [lax.dynamic_slice_in_dim(g, mine * own_width, own_width, 1)]
    for step in range(1, dp_count):
        sent = lax.dynamic_slice_in_dim(g, (mine + step) % dp_count * own_width, own_width, 1)
        g_parts.append(lax.ppermute(sent, "dp", [(i, (i + step) % dp_count) for i in range(dp_count)]))
    g_here = jnp.stack(g_parts)
    g_there = swapped(g_here, 2, count)
    term = None
    for side, (even, odd) in zip(sides, (first, second)):
        at = jnp.stack([even.reshape(-1, PAIR, HALF), odd.reshape(-1, PAIR, HALF)], axis=1)
        parts = at.reshape(count // 4, 2, 2 * block, HALF)
        kept = lax.dynamic_index_in_dim(parts, y_digit, 1, keepdims=False).reshape(width // 2, HALF)
        sent = lax.dynamic_index_in_dim(parts, 1 - y_digit, 1, keepdims=False).reshape(width // 2, HALF)
        pack = jnp.stack([kept, swapped(sent, 2, count)])
        for utt, part in enumerate([pack] + turned(pack, dp_count)):
            for row, source in ((0, g_here), (1, g_there)):
                piece = contract(part[row], lax.dynamic_slice_in_dim(source[utt], side * HALF, HALF, 0), NN)
                term = piece if term is None else term + piece
    term = term.astype(bf16).reshape(count // 4, 2, block, own_width)
    return scattered_sum(term, [(4, count // 4), (1, 2)], upper_stages(count) + [(1, 2)], place, count)


def solution(mesh):
    spread = P("dp", "seq", None)
    return jax.shard_map(
        on_device,
        mesh=mesh,
        in_specs=(spread, spread, spread, spread, P()),
        out_specs=(spread, spread, spread, P("seq", "dp")),
        check_vma=False,
    )
```

```python
import functools

import jax
import jax.numpy as jnp
from jax import lax
from jax.experimental import pallas as pl
from jax.experimental.pallas import tpu as pltpu
from jax.sharding import PartitionSpec as P


HEAD_DIM = 64
HALF = 128
PAIR = 2 * HEAD_DIM
masked_score = -1e30
f32 = jnp.float32
bf16 = jnp.bfloat16


NN = ((1,), (0,))
NT = ((1,), (1,))
TN = ((0,), (0,))

in_vmem = pl.BlockSpec(memory_space=pltpu.VMEM)
in_smem = pl.BlockSpec(memory_space=pltpu.SMEM)


def contract(a, b, dims):
    return lax.dot_general(a, b, (dims, ((), ())), preferred_element_type=f32)


def half_kernel(meta_ref, thin_hbm, thick_hbm, rim_hbm, keep_ref, send_ref, back_ref, dq_hbm, own_hbm,
                one_ref, wide_ref, two_ref, score_ref, dp_ref, p_ref, ds_ref, dq_ref, own_ref, in_sem, out_sem, *, second):
    side = 1 - meta_ref[0] if second else meta_ref[0]
    alone = meta_ref[6 if second else 5]
    bias = jnp.where(alone == 1, masked_score, 0.0).astype(f32)
    y_digit = meta_ref[1]
    scale = HEAD_DIM ** -0.5
    near_rows = pl.ds(pl.multiple_of(side * HALF, HALF), HALF)
    far_rows = pl.ds(pl.multiple_of((1 - side) * HALF, HALF), HALF)
    pairs = one_ref.shape[0]
    early = 2
    middle = pairs // 2

    def pair_of(number):
        return 2 * (number // 2) + (y_digit if number % 2 == 0 else 1 - y_digit)

    def fetches(group):
        some = pl.ds(0, early) if group == 0 else pl.ds(early, pairs - early)
        found = [(thin_hbm.at[some, :, side], one_ref.at[some])]
        for place, source in enumerate((rim_hbm.at[some], thick_hbm.at[some, :, side], thick_hbm.at[some, :, 1 - side])):
            found.append((source, wide_ref.at[some, :, pl.ds(place * HALF, HALF)]))
        return [pltpu.make_async_copy(a, b, in_sem.at[group, place]) for place, (a, b) in enumerate(found)]

    def stores(group):
        some = pl.ds(group * middle, middle)
        found = [(dq_ref.at[some], dq_hbm.at[some]), (own_ref.at[some], own_hbm.at[some])]
        return [pltpu.make_async_copy(a, b, out_sem.at[group, place]) for place, (a, b) in enumerate(found)]

    def multiply(number):
        pair = pair_of(number)
        slot = number % 3
        first_head = lax.broadcasted_iota(jnp.int32, (HALF, PAIR), 1) < HEAD_DIM
        for which, (factor, out) in enumerate(((scale, score_ref), (1.0, dp_ref))):
            one = one_ref[pair, which].astype(f32) * factor
            two_ref[slot, which, :HALF] = jnp.where(first_head, one, 0.0).astype(bf16)
            two_ref[slot, which, HALF:] = jnp.where(first_head, 0.0, one).astype(bf16)
            out[number % 2] = contract(wide_ref[pair, which], two_ref[slot, which], NT)

    def weigh(number):
        slot = number % 2
        ahead = lax.broadcasted_iota(jnp.int32, (HALF, 2 * HALF), 0) - lax.broadcasted_iota(jnp.int32, (HALF, 2 * HALF), 1) % HALF
        in_rim = ahead * (1 - 2 * side) >= side
        s_edge = jnp.where(in_rim, score_ref[slot, :HALF] + bias, score_ref[slot, 2 * HALF :])
        s_near = score_ref[slot, HALF : 2 * HALF]
        top = jnp.max(jnp.maximum(s_edge, s_near), axis=0, keepdims=True)
        e_edge = jnp.exp(s_edge - top)
        e_near = jnp.exp(s_near - top)
        inv = 1.0 / jnp.sum(e_edge + e_near, axis=0, keepdims=True)
        p_edge = e_edge * inv
        p_near = e_near * inv
        d_edge = jnp.where(in_rim, dp_ref[slot, :HALF], dp_ref[slot, 2 * HALF :])
        d_near = dp_ref[slot, HALF : 2 * HALF]
        delta = jnp.sum(p_edge * d_edge + p_near * d_near, axis=0, keepdims=True)
        for ref, edge, near in ((p_ref, p_edge, p_near), (ds_ref, p_edge * (d_edge - delta), p_near * (d_near - delta))):
            ref[slot, :HALF] = jnp.where(in_rim, edge, 0.0).astype(bf16)
            ref[slot, HALF : 2 * HALF] = near.astype(bf16)
            ref[slot, 2 * HALF :] = jnp.where(in_rim, 0.0, edge).astype(bf16)

    def spread(number):
        slot = number % 2
        pair = pair_of(number)
        at_ref = send_ref if number % 2 else keep_ref
        start = number // 2 * PAIR
        at = contract(wide_ref[pair, 1], p_ref[slot], TN)
        at_ref[start : start + HEAD_DIM, :] = at[:HEAD_DIM, :HALF].astype(bf16)
        at_ref[start + HEAD_DIM : start + PAIR, :] = at[HEAD_DIM:, HALF:].astype(bf16)
        for which, left in enumerate((ds_ref, p_ref)):
            part = contract(left[slot], two_ref[number % 3, which], NN)
            back_ref[pair, which] = part[:HALF].astype(bf16)
            own_ref[pair, which, near_rows, :] = part[HALF : 2 * HALF].astype(bf16)
            own_ref[pair, which, far_rows, :] = part[2 * HALF :].astype(bf16)
        dqt = contract(wide_ref[pair, 0], ds_ref[slot], TN)
        dqt = jnp.concatenate([dqt[:HEAD_DIM, :HALF], dqt[HEAD_DIM:, HALF:]], axis=0) * scale
        dq_ref[pair] = dqt.T.astype(bf16)
        if (number + 1) % middle == 0:
            for copy in stores(number // middle):
                copy.start()

    for group in range(2):
        for copy in fetches(group):
            copy.start()
    for step in range(pairs + 2):
        if step in (0, early):
            for copy in fetches(step // early):
                copy.wait()
        if step < pairs:
            multiply(step)
        if 0 <= step - 2:
            spread(step - 2)
        if 0 <= step - 1 < pairs:
            weigh(step - 1)
    for group in range(2):
        for copy in stores(group):
            copy.wait()


def half_attention(meta, thin, thick, rim, second):
    pairs, _, blocks, _, _ = thick.shape
    rows = blocks * HALF
    width = pairs * PAIR
    in_hbm = pl.BlockSpec(memory_space=pltpu.HBM)
    held = [pltpu.with_memory_space_constraint(array, pltpu.HBM) for array in (thin, thick)]
    return pl.pallas_call(
        functools.partial(half_kernel, second=second),
        in_specs=[in_smem, in_hbm, in_hbm, pl.BlockSpec(memory_space=pl.ANY)],
        out_specs=[in_vmem] * 3 + [in_hbm] * 2,
        out_shape=[
            jax.ShapeDtypeStruct((width // 2, HALF), bf16),
            jax.ShapeDtypeStruct((width // 2, HALF), bf16),
            jax.ShapeDtypeStruct((pairs, 2, HALF, PAIR), bf16),
            pltpu.HBM((pairs, HALF, PAIR), bf16),
            pltpu.HBM((pairs, 2, rows, PAIR), bf16),
        ],
        scratch_shapes=[
            pltpu.VMEM((pairs, 2, HALF, PAIR), bf16),
            pltpu.VMEM((pairs, 2, 3 * HALF, PAIR), bf16),
            pltpu.VMEM((3, 2, 2 * HALF, PAIR), bf16),
            pltpu.VMEM((2, 3 * HALF, 2 * HALF), f32),
            pltpu.VMEM((2, 3 * HALF, 2 * HALF), f32),
            pltpu.VMEM((2, 3 * HALF, 2 * HALF), bf16),
            pltpu.VMEM((2, 3 * HALF, 2 * HALF), bf16),
            pltpu.VMEM((pairs, HALF, PAIR), bf16),
            pltpu.VMEM((pairs, 2, rows, PAIR), bf16),
            pltpu.SemaphoreType.DMA((2, 4)),
            pltpu.SemaphoreType.DMA((2, 2)),
        ],
        cost_estimate=pl.CostEstimate(flops=12 * HALF * 3 * HALF * width, bytes_accessed=16 * rows * width,
                                      transcendentals=HALF * 2 * HALF * width // HEAD_DIM),
        compiler_params=pltpu.CompilerParams(vmem_limit_bytes=24 << 20),
    )(meta, *held, rim)


def rim_kernel(side_ref, k_ref, v_ref, out_ref):
    for pair in range(out_ref.shape[0]):
        cols = slice(pair * PAIR, (pair + 1) * PAIR)
        out_ref[pair, 0] = k_ref[:, cols]
        out_ref[pair, 1] = v_ref[:, cols]


def packed_rim(side, k, v):
    width = k.shape[1]
    block = pl.BlockSpec((HALF, width), lambda i, s: (s[0], 0))
    shape = (width // PAIR, 2, HALF, PAIR)
    return pl.pallas_call(
        rim_kernel,
        grid_spec=pltpu.PrefetchScalarGridSpec(
            num_scalar_prefetch=1, grid=(1,), in_specs=[block, block],
            out_specs=pl.BlockSpec(shape, lambda i, s: (0, 0, 0, 0)),
        ),
        out_shape=jax.ShapeDtypeStruct(shape, bf16),
    )(side, k, v)


def prepare_kernel(meta_ref, q_ref, k_ref, v_ref, g_ref, w_ref, thin_ref, thick_ref, rim_ref):
    pairs, _, blocks, _, _ = thin_ref.shape
    for pair in range(pairs):
        cols = slice(pair * PAIR, (pair + 1) * PAIR)
        for block in range(blocks):
            rows = slice(block * HALF, (block + 1) * HALF)
            thin_ref[pair, 0, block] = q_ref[rows, cols]
            thick_ref[pair, 0, block] = k_ref[rows, cols]
            thick_ref[pair, 1, block] = v_ref[rows, cols]
        rim_rows = pl.ds(pl.multiple_of((1 - meta_ref[0]) * HALF, HALF), HALF)
        rim_ref[pair, 0] = k_ref[rim_rows, cols]
        rim_ref[pair, 1] = v_ref[rim_rows, cols]
    step = 2 * PAIR
    for col in range(0, w_ref.shape[0], step):
        part = contract(g_ref[...], w_ref[col : col + step, :], NT).astype(bf16)
        for pair in range(2):
            for block in range(blocks):
                thin_ref[col // PAIR + pair, 1, block] = part[block * HALF : (block + 1) * HALF, pair * PAIR : (pair + 1) * PAIR]


def prepared(meta, q, k, v, g, w):
    rows, width = q.shape
    pairs, blocks = width // PAIR, rows // HALF
    whole = jax.ShapeDtypeStruct((pairs, 2, blocks, HALF, PAIR), bf16)
    return pl.pallas_call(
        prepare_kernel,
        in_specs=[in_smem] + [in_vmem] * 5,
        out_specs=[in_vmem] * 3,
        out_shape=[whole, whole, jax.ShapeDtypeStruct((pairs, 2, HALF, PAIR), bf16)],
        cost_estimate=pl.CostEstimate(flops=2 * rows * width * width, bytes_accessed=14 * rows * width + 2 * width * width, transcendentals=0),
        name="prepared",
    )(meta, q, k, v, g, w)


def product_kernel(meta_ref, *refs):
    side, mine, z_digit = meta_ref[0], meta_ref[2], meta_ref[3]
    ats, (g_ref, g_dp_ref, g_y_ref, g_y_dp_ref), outs = refs[:8], refs[8:12], refs[12:]
    own = outs[0].shape[1]
    size = outs[0].shape[0]
    rights = []
    for row in (side, 1 - side):
        rows = pl.ds(pl.multiple_of(row * HALF, HALF), HALF)
        cols = pl.ds(pl.multiple_of(mine * own, own), own)
        rights += [ref[rows, cols] for ref in (g_ref, g_y_ref, g_dp_ref, g_y_dp_ref)]
    right = jnp.concatenate(rights, axis=0)
    for step, out_ref in enumerate(outs):
        rows = pl.ds(pl.multiple_of((z_digit ^ step) * size, size), size)
        left = jnp.concatenate([ref[rows, :] for ref in ats], axis=1)
        out_ref[...] = contract(left, right, NN).astype(out_ref.dtype)


def products(meta, ats, gs, radix, own):
    size = ats[0].shape[0] // radix
    return pl.pallas_call(
        product_kernel,
        in_specs=[in_smem] + [in_vmem] * 12,
        out_specs=[in_vmem] * radix,
        out_shape=[jax.ShapeDtypeStruct((size, own), f32)] + [jax.ShapeDtypeStruct((size, own), bf16)] * (radix - 1),
        compiler_params=pltpu.CompilerParams(vmem_limit_bytes=12 << 20),
        name="product",
    )(meta, *ats, *gs)


def sum_kernel(meta_ref, own_ref, *refs):
    pieces, (keep_ref, send_ref) = refs[:-2], refs[-2:]
    half = keep_ref.shape[0]
    for x_digit, ref in ((meta_ref[4], keep_ref), (1 - meta_ref[4], send_ref)):
        rows = pl.ds(pl.multiple_of(x_digit * half, half), half)
        total = own_ref[rows, :]
        for piece in pieces:
            total = total + piece[rows, :].astype(f32)
        ref[...] = total.astype(ref.dtype)


def summed(meta, own, pieces):
    half = own.shape[0] // 2
    return pl.pallas_call(
        sum_kernel,
        in_specs=[in_smem] + [in_vmem] * (1 + len(pieces)),
        out_specs=[in_vmem] * 2,
        out_shape=[jax.ShapeDtypeStruct((half, own.shape[1]), f32), jax.ShapeDtypeStruct((half, own.shape[1]), bf16)],
        compiler_params=pltpu.CompilerParams(vmem_limit_bytes=12 << 20),
        name="summed",
    )(meta, own, *pieces)


def join_kernel(meta_ref, dq1_ref, own1_ref, dq2_ref, own2_ref, rim1_ref, rim2_ref, dq_out, dk_out, dv_out):
    side = meta_ref[0]
    for row, rim, dq_ref in ((side, rim1_ref, dq1_ref), (1 - side, rim2_ref, dq2_ref)):
        rows = pl.ds(pl.multiple_of(row * HALF, HALF), HALF)
        for pair in range(dq1_ref.shape[0]):
            cols = slice(pair * PAIR, (pair + 1) * PAIR)
            dq_out[rows, cols] = dq_ref[pair]
            for which, out in enumerate((dk_out, dv_out)):
                total = own1_ref[pair, which, rows].astype(f32) + own2_ref[pair, which, rows].astype(f32)
                out[rows, cols] = (total + rim[pair, which].astype(f32)).astype(bf16)


def joined(meta, own1, own2, rim1, rim2, shape):
    out = jax.ShapeDtypeStruct(shape, bf16)
    return pl.pallas_call(
        join_kernel,
        in_specs=[in_smem] + [in_vmem] * 6,
        out_specs=[in_vmem] * 3,
        out_shape=[out] * 3,
        compiler_params=pltpu.CompilerParams(vmem_limit_bytes=12 << 20),
        name="joined",
    )(meta, *own1, *own2, rim1, rim2)


def swapped(value, stride, count):
    return lax.ppermute(value, "seq", [(i, i ^ stride) for i in range(count)])


def turned(value, count):
    return [lax.ppermute(value, "dp", [(i, (i + step) % count) for i in range(count)]) for step in range(1, count)]


def upper_stages(count):
    found = []
    stride = 4
    while stride < count:
        radix = min(4, count // stride)
        found.append((stride, radix))
        stride *= radix
    return found


def scattered_sum(block, strides, stages, me, count):
    tail = list(block.shape[-2:])
    left = strides
    for number, (stride, radix) in enumerate(stages):
        axis = [place for place, (low, size) in enumerate(left) if low <= stride < low * size][0]
        base, total = left[axis]
        inner = stride // base
        outer = total // (inner * radix)
        dims = [size for _, size in left]
        block = block.reshape(dims[:axis] + [outer, radix, inner] + dims[axis + 1 :] + tail)
        digit = (me // stride) % radix
        received = []
        for step in range(1, radix):
            pairs = [(source, source ^ (step * stride)) for source in range(count)]
            sent = lax.dynamic_index_in_dim(block, digit ^ step, axis + 1, keepdims=False)
            received.append(lax.ppermute(sent, "seq", pairs))
        total_sum = lax.dynamic_index_in_dim(block, digit, axis + 1, keepdims=False).astype(f32)
        for piece in received:
            total_sum = total_sum + piece.astype(f32)
        block = total_sum if number == len(stages) - 1 else total_sum.astype(bf16)
        left = left[:axis] + [(stride * radix, outer), (base, inner)] + left[axis + 1 :]
        keep = [(low, size) for low, size in left if size > 1]
        block = block.reshape([size for _, size in keep] + tail)
        left = keep
    return block.reshape(tail)


def on_device(queries, keys, values, out_grad, out_weight):
    q, k, v, g = queries[0], keys[0], values[0], out_grad[0]
    rows, width = q.shape
    assert rows == 2 * HALF
    count = lax.axis_size("seq")
    dp_count = lax.axis_size("dp")
    assert count >= 8 and count & (count - 1) == 0
    place = lax.axis_index("seq")
    mine = lax.axis_index("dp")
    odd = place % 2
    y_digit = (place // 2) % 2
    sides = (1 - odd, odd)
    long_pairs = [(i, i + 1 if i % 2 else i - 1) for i in range(1, count - 1)]
    near_pairs = [(i, i ^ 1) for i in range(count)]
    block = width // count
    own_width = width // dp_count
    stages = upper_stages(count)
    direct = 2 * block == PAIR and len(stages) == 1 and dp_count == 2
    alone = (place == 0) | (place == count - 1)
    meta = jnp.stack([1 - odd, y_digit if direct else 0 * y_digit, mine, place // 4 % stages[0][1], odd, 0 * odd, alone]).astype(jnp.int32)

    rim1 = packed_rim(meta[:1], k, v)
    first_rim = lax.ppermute(rim1, "seq", near_pairs)
    if direct:
        g_y = swapped(g, 2, count)
    thin, thick, rim2 = prepared(meta, q, k, v, g, out_weight)
    second_rim = lax.ppermute(rim2, "seq", long_pairs)
    if direct:
        g_dp = turned(g, dp_count)[0]
        g_y_dp = turned(g_y, dp_count)[0]
        gs = [g, g_dp, g_y, g_y_dp]

    keep1, send1, back1, *own1 = half_attention(meta, thin, thick, first_rim, False)
    from_near = lax.ppermute(back1, "seq", near_pairs)
    if direct:
        at_y1 = swapped(send1, 2, count)
        at_dp1 = turned(keep1, dp_count)[0]
        at_y_dp1 = turned(at_y1, dp_count)[0]
    keep2, send2, back2, *own2 = half_attention(meta, thin, thick, second_rim, True)
    if direct:
        at_y2 = swapped(send2, 2, count)
        at_dp2 = turned(keep2, dp_count)[0]
        at_y_dp2 = turned(at_y2, dp_count)[0]
    from_long = lax.ppermute(back2, "seq", long_pairs)

    frames = rows * count * dp_count
    if direct:
        ats = [keep1, at_y1, at_dp1, at_y_dp1, keep2, at_y2, at_dp2, at_y_dp2]
        terms = products(meta, ats, gs, count // 4, own_width)
        pieces = []
        for step in range(1, count // 4):
            pieces.append(swapped(terms[step], 4 * step, count))
        kept, sent = summed(meta, terms[0], pieces)
        wo_grad = kept + swapped(sent, 1, count).astype(f32)
    else:
        wo_grad = general_sum((keep1, send1), (keep2, send2), g, sides, place, mine, y_digit, count, dp_count)
    dq, dk, dv = joined(meta, own1, own2, from_near, from_long, q.shape)
    return dq[None], dk[None], dv[None], wo_grad * frames ** -0.5


def general_sum(first, second, g, sides, place, mine, y_digit, count, dp_count):
    width = g.shape[1]
    block = width // count
    own_width = width // dp_count
    g_parts = [lax.dynamic_slice_in_dim(g, mine * own_width, own_width, 1)]
    for step in range(1, dp_count):
        sent = lax.dynamic_slice_in_dim(g, (mine + step) % dp_count * own_width, own_width, 1)
        g_parts.append(lax.ppermute(sent, "dp", [(i, (i + step) % dp_count) for i in range(dp_count)]))
    g_here = jnp.stack(g_parts)
    g_there = swapped(g_here, 2, count)
    term = None
    for side, (even, odd) in zip(sides, (first, second)):
        at = jnp.stack([even.reshape(-1, PAIR, HALF), odd.reshape(-1, PAIR, HALF)], axis=1)
        parts = at.reshape(count // 4, 2, 2 * block, HALF)
        kept = lax.dynamic_index_in_dim(parts, y_digit, 1, keepdims=False).reshape(width // 2, HALF)
        sent = lax.dynamic_index_in_dim(parts, 1 - y_digit, 1, keepdims=False).reshape(width // 2, HALF)
        pack = jnp.stack([kept, swapped(sent, 2, count)])
        for utt, part in enumerate([pack] + turned(pack, dp_count)):
            for row, source in ((0, g_here), (1, g_there)):
                piece = contract(part[row], lax.dynamic_slice_in_dim(source[utt], side * HALF, HALF, 0), NN)
                term = piece if term is None else term + piece
    term = term.astype(bf16).reshape(count // 4, 2, block, own_width)
    return scattered_sum(term, [(4, count // 4), (1, 2)], upper_stages(count) + [(1, 2)], place, count)


def solution(mesh):
    spread = P("dp", "seq", None)
    return jax.shard_map(
        on_device,
        mesh=mesh,
        in_specs=(spread, spread, spread, spread, P()),
        out_specs=(spread, spread, spread, P("seq", "dp")),
        check_vma=False,
    )
```

```python
import functools

import jax
import jax.numpy as jnp
from jax import lax
from jax.experimental import pallas as pl
from jax.experimental.pallas import tpu as pltpu
from jax.sharding import PartitionSpec as P


HEAD_DIM = 64
HALF = 128
PAIR = 2 * HEAD_DIM
masked_score = -1e30
f32 = jnp.float32
bf16 = jnp.bfloat16


NN = ((1,), (0,))
NT = ((1,), (1,))
TN = ((0,), (0,))

in_vmem = pl.BlockSpec(memory_space=pltpu.VMEM)
in_smem = pl.BlockSpec(memory_space=pltpu.SMEM)


def contract(a, b, dims):
    return lax.dot_general(a, b, (dims, ((), ())), preferred_element_type=f32)


def half_kernel(meta_ref, thin_hbm, thick_hbm, rim_hbm, keep_ref, send_ref, back_ref, dq_hbm, own_hbm,
                one_ref, wide_ref, two_ref, score_ref, dp_ref, p_ref, ds_ref, dq_ref, own_ref, in_sem, out_sem, *, second):
    side = 1 - meta_ref[0] if second else meta_ref[0]
    alone = meta_ref[6 if second else 5]
    bias = jnp.where(alone == 1, masked_score, 0.0).astype(f32)
    y_digit = meta_ref[1]
    scale = HEAD_DIM ** -0.5
    near_rows = pl.ds(pl.multiple_of(side * HALF, HALF), HALF)
    far_rows = pl.ds(pl.multiple_of((1 - side) * HALF, HALF), HALF)
    pairs = one_ref.shape[0]
    early = 2
    middle = pairs // 2

    def pair_of(number):
        return 2 * (number // 2) + (y_digit if number % 2 == 0 else 1 - y_digit)

    def fetches(group):
        some = pl.ds(0, early) if group == 0 else pl.ds(early, pairs - early)
        found = [(thin_hbm.at[some, :, side], one_ref.at[some])]
        for place, source in enumerate((rim_hbm.at[some], thick_hbm.at[some, :, side], thick_hbm.at[some, :, 1 - side])):
            found.append((source, wide_ref.at[some, :, pl.ds(place * HALF, HALF)]))
        return [pltpu.make_async_copy(a, b, in_sem.at[group, place]) for place, (a, b) in enumerate(found)]

    def stores(group):
        some = pl.ds(group * middle, middle)
        found = [(dq_ref.at[some], dq_hbm.at[some]), (own_ref.at[some], own_hbm.at[some])]
        return [pltpu.make_async_copy(a, b, out_sem.at[group, place]) for place, (a, b) in enumerate(found)]

    def multiply(number):
        pair = pair_of(number)
        slot = number % 3
        first_head = lax.broadcasted_iota(jnp.int32, (HALF, PAIR), 1) < HEAD_DIM
        for which, (factor, out) in enumerate(((scale, score_ref), (1.0, dp_ref))):
            one = one_ref[pair, which].astype(f32) * factor
            two_ref[slot, which, :HALF] = jnp.where(first_head, one, 0.0).astype(bf16)
            two_ref[slot, which, HALF:] = jnp.where(first_head, 0.0, one).astype(bf16)
            out[number % 2] = contract(wide_ref[pair, which], two_ref[slot, which], NT)

    def weigh(number):
        slot = number % 2
        ahead = lax.broadcasted_iota(jnp.int32, (HALF, 2 * HALF), 0) - lax.broadcasted_iota(jnp.int32, (HALF, 2 * HALF), 1) % HALF
        in_rim = ahead * (1 - 2 * side) >= side
        s_edge = jnp.where(in_rim, score_ref[slot, :HALF] + bias, score_ref[slot, 2 * HALF :])
        s_near = score_ref[slot, HALF : 2 * HALF]
        top = jnp.max(jnp.maximum(s_edge, s_near), axis=0, keepdims=True)
        e_edge = jnp.exp(s_edge - top)
        e_near = jnp.exp(s_near - top)
        inv = 1.0 / jnp.sum(e_edge + e_near, axis=0, keepdims=True)
        p_edge = e_edge * inv
        p_near = e_near * inv
        d_edge = jnp.where(in_rim, dp_ref[slot, :HALF], dp_ref[slot, 2 * HALF :])
        d_near = dp_ref[slot, HALF : 2 * HALF]
        delta = jnp.sum(p_edge * d_edge + p_near * d_near, axis=0, keepdims=True)
        for ref, edge, near in ((p_ref, p_edge, p_near), (ds_ref, p_edge * (d_edge - delta), p_near * (d_near - delta))):
            ref[slot, :HALF] = jnp.where(in_rim, edge, 0.0).astype(bf16)
            ref[slot, HALF : 2 * HALF] = near.astype(bf16)
            ref[slot, 2 * HALF :] = jnp.where(in_rim, 0.0, edge).astype(bf16)

    def spread(number):
        slot = number % 2
        pair = pair_of(number)
        at_ref = send_ref if number % 2 else keep_ref
        start = number // 2 * PAIR
        at = contract(wide_ref[pair, 1], p_ref[slot], TN)
        at_ref[start : start + HEAD_DIM, :] = at[:HEAD_DIM, :HALF].astype(bf16)
        at_ref[start + HEAD_DIM : start + PAIR, :] = at[HEAD_DIM:, HALF:].astype(bf16)
        for which, left in enumerate((ds_ref, p_ref)):
            part = contract(left[slot], two_ref[number % 3, which], NN)
            back_ref[pair, which] = part[:HALF].astype(bf16)
            own_ref[pair, which, near_rows, :] = part[HALF : 2 * HALF].astype(bf16)
            own_ref[pair, which, far_rows, :] = part[2 * HALF :].astype(bf16)
        dqt = contract(wide_ref[pair, 0], ds_ref[slot], TN)
        dqt = jnp.concatenate([dqt[:HEAD_DIM, :HALF], dqt[HEAD_DIM:, HALF:]], axis=0) * scale
        dq_ref[pair] = dqt.T.astype(bf16)
        if (number + 1) % middle == 0:
            for copy in stores(number // middle):
                copy.start()

    for group in range(2):
        for copy in fetches(group):
            copy.start()
    for step in range(pairs + 2):
        if step in (0, early):
            for copy in fetches(step // early):
                copy.wait()
        if step < pairs:
            multiply(step)
        if 0 <= step - 2:
            spread(step - 2)
        if 0 <= step - 1 < pairs:
            weigh(step - 1)
    for group in range(2):
        for copy in stores(group):
            copy.wait()


def half_attention(meta, thin, thick, rim, second):
    pairs, _, blocks, _, _ = thick.shape
    rows = blocks * HALF
    width = pairs * PAIR
    in_hbm = pl.BlockSpec(memory_space=pltpu.HBM)
    held = [pltpu.with_memory_space_constraint(array, pltpu.HBM) for array in (thin, thick)]
    return pl.pallas_call(
        functools.partial(half_kernel, second=second),
        in_specs=[in_smem, in_hbm, in_hbm, pl.BlockSpec(memory_space=pl.ANY)],
        out_specs=[in_vmem] * 3 + [in_hbm] * 2,
        out_shape=[
            jax.ShapeDtypeStruct((width // 2, HALF), bf16),
            jax.ShapeDtypeStruct((width // 2, HALF), bf16),
            jax.ShapeDtypeStruct((pairs, 2, HALF, PAIR), bf16),
            pltpu.HBM((pairs, HALF, PAIR), bf16),
            pltpu.HBM((pairs, 2, rows, PAIR), bf16),
        ],
        scratch_shapes=[
            pltpu.VMEM((pairs, 2, HALF, PAIR), bf16),
            pltpu.VMEM((pairs, 2, 3 * HALF, PAIR), bf16),
            pltpu.VMEM((3, 2, 2 * HALF, PAIR), bf16),
            pltpu.VMEM((2, 3 * HALF, 2 * HALF), f32),
            pltpu.VMEM((2, 3 * HALF, 2 * HALF), f32),
            pltpu.VMEM((2, 3 * HALF, 2 * HALF), bf16),
            pltpu.VMEM((2, 3 * HALF, 2 * HALF), bf16),
            pltpu.VMEM((pairs, HALF, PAIR), bf16),
            pltpu.VMEM((pairs, 2, rows, PAIR), bf16),
            pltpu.SemaphoreType.DMA((2, 4)),
            pltpu.SemaphoreType.DMA((2, 2)),
        ],
        cost_estimate=pl.CostEstimate(flops=12 * HALF * 3 * HALF * width, bytes_accessed=16 * rows * width,
                                      transcendentals=HALF * 2 * HALF * width // HEAD_DIM),
        compiler_params=pltpu.CompilerParams(vmem_limit_bytes=24 << 20),
    )(meta, *held, rim)


def rim_kernel(side_ref, k_ref, v_ref, out_ref):
    for pair in range(out_ref.shape[0]):
        cols = slice(pair * PAIR, (pair + 1) * PAIR)
        out_ref[pair, 0] = k_ref[:, cols]
        out_ref[pair, 1] = v_ref[:, cols]


def packed_rim(side, k, v):
    width = k.shape[1]
    block = pl.BlockSpec((HALF, width), lambda i, s: (s[0], 0))
    shape = (width // PAIR, 2, HALF, PAIR)
    return pl.pallas_call(
        rim_kernel,
        grid_spec=pltpu.PrefetchScalarGridSpec(
            num_scalar_prefetch=1, grid=(1,), in_specs=[block, block],
            out_specs=pl.BlockSpec(shape, lambda i, s: (0, 0, 0, 0)),
        ),
        out_shape=jax.ShapeDtypeStruct(shape, bf16),
    )(side, k, v)


def prepare_kernel(meta_ref, q_ref, k_ref, v_ref, g_ref, w_ref, thin_ref, thick_ref, rim_ref):
    pairs, _, blocks, _, _ = thin_ref.shape
    for pair in range(pairs):
        cols = slice(pair * PAIR, (pair + 1) * PAIR)
        for block in range(blocks):
            rows = slice(block * HALF, (block + 1) * HALF)
            thin_ref[pair, 0, block] = q_ref[rows, cols]
            thick_ref[pair, 0, block] = k_ref[rows, cols]
            thick_ref[pair, 1, block] = v_ref[rows, cols]
        rim_rows = pl.ds(pl.multiple_of((1 - meta_ref[0]) * HALF, HALF), HALF)
        rim_ref[pair, 0] = k_ref[rim_rows, cols]
        rim_ref[pair, 1] = v_ref[rim_rows, cols]
    step = 2 * PAIR
    for col in range(0, w_ref.shape[0], step):
        part = contract(g_ref[...], w_ref[col : col + step, :], NT).astype(bf16)
        for pair in range(2):
            for block in range(blocks):
                thin_ref[col // PAIR + pair, 1, block] = part[block * HALF : (block + 1) * HALF, pair * PAIR : (pair + 1) * PAIR]


def prepared(meta, q, k, v, g, w):
    rows, width = q.shape
    pairs, blocks = width // PAIR, rows // HALF
    whole = jax.ShapeDtypeStruct((pairs, 2, blocks, HALF, PAIR), bf16)
    return pl.pallas_call(
        prepare_kernel,
        in_specs=[in_smem] + [in_vmem] * 5,
        out_specs=[in_vmem] * 3,
        out_shape=[whole, whole, jax.ShapeDtypeStruct((pairs, 2, HALF, PAIR), bf16)],
        cost_estimate=pl.CostEstimate(flops=2 * rows * width * width, bytes_accessed=14 * rows * width + 2 * width * width, transcendentals=0),
        name="prepared",
    )(meta, q, k, v, g, w)


def product_kernel(meta_ref, *refs):
    side, mine, z_digit = meta_ref[0], meta_ref[2], meta_ref[3]
    ats, (g_ref, g_dp_ref, g_y_ref, g_y_dp_ref), outs = refs[:8], refs[8:12], refs[12:]
    own = outs[0].shape[1]
    size = outs[0].shape[0]
    rights = []
    for row in (side, 1 - side):
        rows = pl.ds(pl.multiple_of(row * HALF, HALF), HALF)
        cols = pl.ds(pl.multiple_of(mine * own, own), own)
        rights += [ref[rows, cols] for ref in (g_ref, g_y_ref, g_dp_ref, g_y_dp_ref)]
    right = jnp.concatenate(rights, axis=0)
    for step, out_ref in enumerate(outs):
        rows = pl.ds(pl.multiple_of((z_digit ^ step) * size, size), size)
        left = jnp.concatenate([ref[rows, :] for ref in ats], axis=1)
        out_ref[...] = contract(left, right, NN).astype(out_ref.dtype)


def products(meta, ats, gs, radix, own):
    size = ats[0].shape[0] // radix
    return pl.pallas_call(
        product_kernel,
        in_specs=[in_smem] + [in_vmem] * 12,
        out_specs=[in_vmem] * radix,
        out_shape=[jax.ShapeDtypeStruct((size, own), f32)] + [jax.ShapeDtypeStruct((size, own), bf16)] * (radix - 1),
        compiler_params=pltpu.CompilerParams(vmem_limit_bytes=12 << 20),
        name="product",
    )(meta, *ats, *gs)


def sum_kernel(meta_ref, own_ref, *refs):
    pieces, (keep_ref, send_ref) = refs[:-2], refs[-2:]
    half = keep_ref.shape[0]
    for x_digit, ref in ((meta_ref[4], keep_ref), (1 - meta_ref[4], send_ref)):
        rows = pl.ds(pl.multiple_of(x_digit * half, half), half)
        total = own_ref[rows, :]
        for piece in pieces:
            total = total + piece[rows, :].astype(f32)
        ref[...] = total.astype(ref.dtype)


def summed(meta, own, pieces):
    half = own.shape[0] // 2
    return pl.pallas_call(
        sum_kernel,
        in_specs=[in_smem] + [in_vmem] * (1 + len(pieces)),
        out_specs=[in_vmem] * 2,
        out_shape=[jax.ShapeDtypeStruct((half, own.shape[1]), f32), jax.ShapeDtypeStruct((half, own.shape[1]), bf16)],
        compiler_params=pltpu.CompilerParams(vmem_limit_bytes=12 << 20),
        name="summed",
    )(meta, own, *pieces)


def join_kernel(meta_ref, dq1_ref, own1_ref, dq2_ref, own2_ref, rim1_ref, rim2_ref, dq_out, dk_out, dv_out):
    side = meta_ref[0]
    for row, rim, dq_ref in ((side, rim1_ref, dq1_ref), (1 - side, rim2_ref, dq2_ref)):
        rows = pl.ds(pl.multiple_of(row * HALF, HALF), HALF)
        for pair in range(dq1_ref.shape[0]):
            cols = slice(pair * PAIR, (pair + 1) * PAIR)
            dq_out[rows, cols] = dq_ref[pair]
            for which, out in enumerate((dk_out, dv_out)):
                total = own1_ref[pair, which, rows].astype(f32) + own2_ref[pair, which, rows].astype(f32)
                out[rows, cols] = (total + rim[pair, which].astype(f32)).astype(bf16)


def joined(meta, own1, own2, rim1, rim2, shape):
    out = jax.ShapeDtypeStruct(shape, bf16)
    return pl.pallas_call(
        join_kernel,
        in_specs=[in_smem] + [in_vmem] * 6,
        out_specs=[in_vmem] * 3,
        out_shape=[out] * 3,
        compiler_params=pltpu.CompilerParams(vmem_limit_bytes=12 << 20),
        name="joined",
    )(meta, *own1, *own2, rim1, rim2)


def swapped(value, stride, count):
    return lax.ppermute(value, "seq", [(i, i ^ stride) for i in range(count)])


def turned(value, count):
    return [lax.ppermute(value, "dp", [(i, (i + step) % count) for i in range(count)]) for step in range(1, count)]


def upper_stages(count):
    found = []
    stride = 4
    while stride < count:
        radix = min(4, count // stride)
        found.append((stride, radix))
        stride *= radix
    return found


def scattered_sum(block, strides, stages, me, count):
    tail = list(block.shape[-2:])
    left = strides
    for number, (stride, radix) in enumerate(stages):
        axis = [place for place, (low, size) in enumerate(left) if low <= stride < low * size][0]
        base, total = left[axis]
        inner = stride // base
        outer = total // (inner * radix)
        dims = [size for _, size in left]
        block = block.reshape(dims[:axis] + [outer, radix, inner] + dims[axis + 1 :] + tail)
        digit = (me // stride) % radix
        received = []
        for step in range(1, radix):
            pairs = [(source, source ^ (step * stride)) for source in range(count)]
            sent = lax.dynamic_index_in_dim(block, digit ^ step, axis + 1, keepdims=False)
            received.append(lax.ppermute(sent, "seq", pairs))
        total_sum = lax.dynamic_index_in_dim(block, digit, axis + 1, keepdims=False).astype(f32)
        for piece in received:
            total_sum = total_sum + piece.astype(f32)
        block = total_sum if number == len(stages) - 1 else total_sum.astype(bf16)
        left = left[:axis] + [(stride * radix, outer), (base, inner)] + left[axis + 1 :]
        keep = [(low, size) for low, size in left if size > 1]
        block = block.reshape([size for _, size in keep] + tail)
        left = keep
    return block.reshape(tail)


def on_device(queries, keys, values, out_grad, out_weight):
    q, k, v, g = queries[0], keys[0], values[0], out_grad[0]
    rows, width = q.shape
    assert rows == 2 * HALF
    count = lax.axis_size("seq")
    dp_count = lax.axis_size("dp")
    assert count >= 8 and count & (count - 1) == 0
    place = lax.axis_index("seq")
    mine = lax.axis_index("dp")
    odd = place % 2
    y_digit = (place // 2) % 2
    sides = (odd, 1 - odd)
    long_pairs = [(i, i + 1 if i % 2 else i - 1) for i in range(1, count - 1)]
    near_pairs = [(i, i ^ 1) for i in range(count)]
    block = width // count
    own_width = width // dp_count
    stages = upper_stages(count)
    direct = 2 * block == PAIR and len(stages) == 1 and dp_count == 2
    alone = (place == 0) | (place == count - 1)
    meta = jnp.stack([odd, y_digit if direct else 0 * y_digit, mine, place // 4 % stages[0][1], odd, alone, 0 * odd]).astype(jnp.int32)

    rim1 = packed_rim(meta[:1], k, v)
    first_rim = lax.ppermute(rim1, "seq", long_pairs)
    if direct:
        g_y = swapped(g, 2, count)
    thin, thick, rim2 = prepared(meta, q, k, v, g, out_weight)
    second_rim = lax.ppermute(rim2, "seq", near_pairs)
    if direct:
        g_dp = turned(g, dp_count)[0]
        g_y_dp = turned(g_y, dp_count)[0]
        gs = [g, g_dp, g_y, g_y_dp]

    keep1, send1, back1, *own1 = half_attention(meta, thin, thick, first_rim, False)
    from_long = lax.ppermute(back1, "seq", long_pairs)
    if direct:
        at_y1 = swapped(send1, 2, count)
        at_dp1 = turned(keep1, dp_count)[0]
        at_y_dp1 = turned(at_y1, dp_count)[0]
    keep2, send2, back2, *own2 = half_attention(meta, thin, thick, second_rim, True)
    if direct:
        at_y2 = swapped(send2, 2, count)
        at_dp2 = turned(keep2, dp_count)[0]
        at_y_dp2 = turned(at_y2, dp_count)[0]
    from_near = lax.ppermute(back2, "seq", near_pairs)

    frames = rows * count * dp_count
    if direct:
        ats = [keep1, at_y1, at_dp1, at_y_dp1, keep2, at_y2, at_dp2, at_y_dp2]
        terms = products(meta, ats, gs, count // 4, own_width)
        pieces = []
        for step in range(1, count // 4):
            pieces.append(swapped(terms[step], 4 * step, count))
        kept, sent = summed(meta, terms[0], pieces)
        wo_grad = kept + swapped(sent, 1, count).astype(f32)
    else:
        wo_grad = general_sum((keep1, send1), (keep2, send2), g, sides, place, mine, y_digit, count, dp_count)
    dq, dk, dv = joined(meta, own1, own2, from_long, from_near, q.shape)
    return dq[None], dk[None], dv[None], wo_grad * frames ** -0.5


def general_sum(first, second, g, sides, place, mine, y_digit, count, dp_count):
    width = g.shape[1]
    block = width // count
    own_width = width // dp_count
    g_parts = [lax.dynamic_slice_in_dim(g, mine * own_width, own_width, 1)]
    for step in range(1, dp_count):
        sent = lax.dynamic_slice_in_dim(g, (mine + step) % dp_count * own_width, own_width, 1)
        g_parts.append(lax.ppermute(sent, "dp", [(i, (i + step) % dp_count) for i in range(dp_count)]))
    g_here = jnp.stack(g_parts)
    g_there = swapped(g_here, 2, count)
    term = None
    for side, (even, odd) in zip(sides, (first, second)):
        at = jnp.stack([even.reshape(-1, PAIR, HALF), odd.reshape(-1, PAIR, HALF)], axis=1)
        parts = at.reshape(count // 4, 2, 2 * block, HALF)
        kept = lax.dynamic_index_in_dim(parts, y_digit, 1, keepdims=False).reshape(width // 2, HALF)
        sent = lax.dynamic_index_in_dim(parts, 1 - y_digit, 1, keepdims=False).reshape(width // 2, HALF)
        pack = jnp.stack([kept, swapped(sent, 2, count)])
        for utt, part in enumerate([pack] + turned(pack, dp_count)):
            for row, source in ((0, g_here), (1, g_there)):
                piece = contract(part[row], lax.dynamic_slice_in_dim(source[utt], side * HALF, HALF, 0), NN)
                term = piece if term is None else term + piece
    term = term.astype(bf16).reshape(count // 4, 2, block, own_width)
    return scattered_sum(term, [(4, count // 4), (1, 2)], upper_stages(count) + [(1, 2)], place, count)


def solution(mesh):
    spread = P("dp", "seq", None)
    return jax.shard_map(
        on_device,
        mesh=mesh,
        in_specs=(spread, spread, spread, spread, P()),
        out_specs=(spread, spread, spread, P("seq", "dp")),
        check_vma=False,
    )
```

```python
import functools

import jax
import jax.numpy as jnp
from jax import lax
from jax.experimental import pallas as pl
from jax.experimental.pallas import tpu as pltpu
from jax.sharding import PartitionSpec as P


HEAD_DIM = 64
HALF = 128
PAIR = 2 * HEAD_DIM
masked_score = -1e30
f32 = jnp.float32
bf16 = jnp.bfloat16


NN = ((1,), (0,))
NT = ((1,), (1,))
TN = ((0,), (0,))

in_vmem = pl.BlockSpec(memory_space=pltpu.VMEM)
in_smem = pl.BlockSpec(memory_space=pltpu.SMEM)


def contract(a, b, dims):
    return lax.dot_general(a, b, (dims, ((), ())), preferred_element_type=f32)


def half_kernel(meta_ref, thin_hbm, thick_hbm, rim_hbm, *refs, second, front, back):
    refs = list(refs)
    keep_ref, send_ref = [refs.pop(0) for _ in range(2)] if front else (None, None)
    back_ref, dq_hbm, own_hbm = [refs.pop(0) for _ in range(3)] if back else (None, None, None)
    one_ref, wide_ref, two_ref, score_ref, p_ref, in_sem = refs[:6]
    if back:
        dp_ref, ds_ref, dq_ref, own_ref, out_sem = refs[6:]
    side = 1 - meta_ref[0] if second else meta_ref[0]
    alone = meta_ref[6 if second else 5]
    bias = jnp.where(alone == 1, masked_score, 0.0).astype(f32)
    y_digit = meta_ref[1]
    scale = HEAD_DIM ** -0.5
    near_rows = pl.ds(pl.multiple_of(side * HALF, HALF), HALF)
    far_rows = pl.ds(pl.multiple_of((1 - side) * HALF, HALF), HALF)
    pairs = one_ref.shape[0]
    early = 2
    middle = pairs // 2
    kinds = range(2 if back else 1)

    def pair_of(number):
        return 2 * (number // 2) + (y_digit if number % 2 == 0 else 1 - y_digit)

    def fetches(group):
        some = pl.ds(0, early) if group == 0 else pl.ds(early, pairs - early)
        these = pl.ds(0, len(kinds))
        found = [(thin_hbm.at[some, these, side], one_ref.at[some])]
        for place, source in enumerate((rim_hbm.at[some], thick_hbm.at[some, :, side], thick_hbm.at[some, :, 1 - side])):
            found.append((source, wide_ref.at[some, :, pl.ds(place * HALF, HALF)]))
        return [pltpu.make_async_copy(a, b, in_sem.at[group, place]) for place, (a, b) in enumerate(found)]

    def stores(group):
        some = pl.ds(group * middle, middle)
        found = [(dq_ref.at[some], dq_hbm.at[some]), (own_ref.at[some], own_hbm.at[some])]
        return [pltpu.make_async_copy(a, b, out_sem.at[group, place]) for place, (a, b) in enumerate(found)]

    def multiply(number):
        pair = pair_of(number)
        slot = number % 3
        first_head = lax.broadcasted_iota(jnp.int32, (HALF, PAIR), 1) < HEAD_DIM
        for which in kinds:
            one = one_ref[pair, which].astype(f32) * (1.0 if which else scale)
            two_ref[slot, which, :HALF] = jnp.where(first_head, one, 0.0).astype(bf16)
            two_ref[slot, which, HALF:] = jnp.where(first_head, 0.0, one).astype(bf16)
            out = dp_ref if which else score_ref
            out[number % 2] = contract(wide_ref[pair, which], two_ref[slot, which], NT)

    def weigh(number):
        slot = number % 2
        ahead = lax.broadcasted_iota(jnp.int32, (HALF, 2 * HALF), 0) - lax.broadcasted_iota(jnp.int32, (HALF, 2 * HALF), 1) % HALF
        in_rim = ahead * (1 - 2 * side) >= side
        s_edge = jnp.where(in_rim, score_ref[slot, :HALF] + bias, score_ref[slot, 2 * HALF :])
        s_near = score_ref[slot, HALF : 2 * HALF]
        top = jnp.max(jnp.maximum(s_edge, s_near), axis=0, keepdims=True)
        e_edge = jnp.exp(s_edge - top)
        e_near = jnp.exp(s_near - top)
        inv = 1.0 / jnp.sum(e_edge + e_near, axis=0, keepdims=True)
        p_edge = e_edge * inv
        p_near = e_near * inv
        found = [(p_ref, p_edge, p_near)]
        if back:
            d_edge = jnp.where(in_rim, dp_ref[slot, :HALF], dp_ref[slot, 2 * HALF :])
            d_near = dp_ref[slot, HALF : 2 * HALF]
            delta = jnp.sum(p_edge * d_edge + p_near * d_near, axis=0, keepdims=True)
            found.append((ds_ref, p_edge * (d_edge - delta), p_near * (d_near - delta)))
        for ref, edge, near in found:
            ref[slot, :HALF] = jnp.where(in_rim, edge, 0.0).astype(bf16)
            ref[slot, HALF : 2 * HALF] = near.astype(bf16)
            ref[slot, 2 * HALF :] = jnp.where(in_rim, 0.0, edge).astype(bf16)

    def spread(number):
        slot = number % 2
        pair = pair_of(number)
        if front:
            at_ref = send_ref if number % 2 else keep_ref
            start = number // 2 * PAIR
            at = contract(wide_ref[pair, 1], p_ref[slot], TN)
            at_ref[start : start + HEAD_DIM, :] = at[:HEAD_DIM, :HALF].astype(bf16)
            at_ref[start + HEAD_DIM : start + PAIR, :] = at[HEAD_DIM:, HALF:].astype(bf16)
        if not back:
            return
        for which, left in enumerate((ds_ref, p_ref)):
            part = contract(left[slot], two_ref[number % 3, which], NN)
            back_ref[pair, which] = part[:HALF].astype(bf16)
            own_ref[pair, which, near_rows, :] = part[HALF : 2 * HALF].astype(bf16)
            own_ref[pair, which, far_rows, :] = part[2 * HALF :].astype(bf16)
        dqt = contract(wide_ref[pair, 0], ds_ref[slot], TN)
        dqt = jnp.concatenate([dqt[:HEAD_DIM, :HALF], dqt[HEAD_DIM:, HALF:]], axis=0) * scale
        dq_ref[pair] = dqt.T.astype(bf16)
        if (number + 1) % middle == 0:
            for copy in stores(number // middle):
                copy.start()

    for group in range(2):
        for copy in fetches(group):
            copy.start()
    for step in range(pairs + 2):
        if step in (0, early):
            for copy in fetches(step // early):
                copy.wait()
        if step < pairs:
            multiply(step)
        if 0 <= step - 2:
            spread(step - 2)
        if 0 <= step - 1 < pairs:
            weigh(step - 1)
    if back:
        for group in range(2):
            for copy in stores(group):
                copy.wait()


def half_attention(meta, thin, thick, rim, second, front=True, back=True):
    pairs, _, blocks, _, _ = thick.shape
    rows = blocks * HALF
    width = pairs * PAIR
    kinds = 2 if back else 1
    in_hbm = pl.BlockSpec(memory_space=pltpu.HBM)
    held = [pltpu.with_memory_space_constraint(array, pltpu.HBM) for array in (thin, thick)]
    out_specs, out_shape = [], []
    if front:
        out_specs += [in_vmem] * 2
        out_shape += [jax.ShapeDtypeStruct((width // 2, HALF), bf16)] * 2
    if back:
        out_specs += [in_vmem, in_hbm, in_hbm]
        out_shape += [
            jax.ShapeDtypeStruct((pairs, 2, HALF, PAIR), bf16),
            pltpu.HBM((pairs, HALF, PAIR), bf16),
            pltpu.HBM((pairs, 2, rows, PAIR), bf16),
        ]
    scratch = [
        pltpu.VMEM((pairs, kinds, HALF, PAIR), bf16),
        pltpu.VMEM((pairs, 2, 3 * HALF, PAIR), bf16),
        pltpu.VMEM((3, kinds, 2 * HALF, PAIR), bf16),
        pltpu.VMEM((2, 3 * HALF, 2 * HALF), f32),
        pltpu.VMEM((2, 3 * HALF, 2 * HALF), bf16),
        pltpu.SemaphoreType.DMA((2, 4)),
    ]
    if back:
        scratch += [
            pltpu.VMEM((2, 3 * HALF, 2 * HALF), f32),
            pltpu.VMEM((2, 3 * HALF, 2 * HALF), bf16),
            pltpu.VMEM((pairs, HALF, PAIR), bf16),
            pltpu.VMEM((pairs, 2, rows, PAIR), bf16),
            pltpu.SemaphoreType.DMA((2, 2)),
        ]
    return pl.pallas_call(
        functools.partial(half_kernel, second=second, front=front, back=back),
        in_specs=[in_smem, in_hbm, in_hbm, pl.BlockSpec(memory_space=pl.ANY)],
        out_specs=out_specs,
        out_shape=out_shape,
        scratch_shapes=scratch,
        cost_estimate=pl.CostEstimate(flops=(4 * front + 8 * back) * HALF * 3 * HALF * width, bytes_accessed=16 * rows * width,
                                      transcendentals=HALF * 2 * HALF * width // HEAD_DIM),
        compiler_params=pltpu.CompilerParams(vmem_limit_bytes=24 << 20),
    )(meta, *held, rim)


def rim_kernel(side_ref, k_ref, v_ref, out_ref):
    for pair in range(out_ref.shape[0]):
        cols = slice(pair * PAIR, (pair + 1) * PAIR)
        out_ref[pair, 0] = k_ref[:, cols]
        out_ref[pair, 1] = v_ref[:, cols]


def packed_rim(side, k, v):
    width = k.shape[1]
    block = pl.BlockSpec((HALF, width), lambda i, s: (s[0], 0))
    shape = (width // PAIR, 2, HALF, PAIR)
    return pl.pallas_call(
        rim_kernel,
        grid_spec=pltpu.PrefetchScalarGridSpec(
            num_scalar_prefetch=1, grid=(1,), in_specs=[block, block],
            out_specs=pl.BlockSpec(shape, lambda i, s: (0, 0, 0, 0)),
        ),
        out_shape=jax.ShapeDtypeStruct(shape, bf16),
    )(side, k, v)


def prepare_kernel(meta_ref, q_ref, k_ref, v_ref, g_ref, w_ref, thin_ref, thick_ref, rim_ref):
    pairs, _, blocks, _, _ = thin_ref.shape
    for pair in range(pairs):
        cols = slice(pair * PAIR, (pair + 1) * PAIR)
        for block in range(blocks):
            rows = slice(block * HALF, (block + 1) * HALF)
            thin_ref[pair, 0, block] = q_ref[rows, cols]
            thick_ref[pair, 0, block] = k_ref[rows, cols]
            thick_ref[pair, 1, block] = v_ref[rows, cols]
        rim_rows = pl.ds(pl.multiple_of((1 - meta_ref[0]) * HALF, HALF), HALF)
        rim_ref[pair, 0] = k_ref[rim_rows, cols]
        rim_ref[pair, 1] = v_ref[rim_rows, cols]
    step = 2 * PAIR
    for col in range(0, w_ref.shape[0], step):
        part = contract(g_ref[...], w_ref[col : col + step, :], NT).astype(bf16)
        for pair in range(2):
            for block in range(blocks):
                thin_ref[col // PAIR + pair, 1, block] = part[block * HALF : (block + 1) * HALF, pair * PAIR : (pair + 1) * PAIR]


def prepared(meta, q, k, v, g, w):
    rows, width = q.shape
    pairs, blocks = width // PAIR, rows // HALF
    whole = jax.ShapeDtypeStruct((pairs, 2, blocks, HALF, PAIR), bf16)
    return pl.pallas_call(
        prepare_kernel,
        in_specs=[in_smem] + [in_vmem] * 5,
        out_specs=[in_vmem] * 3,
        out_shape=[whole, whole, jax.ShapeDtypeStruct((pairs, 2, HALF, PAIR), bf16)],
        cost_estimate=pl.CostEstimate(flops=2 * rows * width * width, bytes_accessed=14 * rows * width + 2 * width * width, transcendentals=0),
        name="prepared",
    )(meta, q, k, v, g, w)


def product_kernel(meta_ref, *refs):
    side, mine, z_digit = meta_ref[0], meta_ref[2], meta_ref[3]
    ats, (g_ref, g_dp_ref, g_y_ref, g_y_dp_ref), outs = refs[:8], refs[8:12], refs[12:]
    own = outs[0].shape[1]
    size = outs[0].shape[0]
    rights = []
    for row in (side, 1 - side):
        rows = pl.ds(pl.multiple_of(row * HALF, HALF), HALF)
        cols = pl.ds(pl.multiple_of(mine * own, own), own)
        rights += [ref[rows, cols] for ref in (g_ref, g_y_ref, g_dp_ref, g_y_dp_ref)]
    right = jnp.concatenate(rights, axis=0)
    for step, out_ref in enumerate(outs):
        rows = pl.ds(pl.multiple_of((z_digit ^ step) * size, size), size)
        left = jnp.concatenate([ref[rows, :] for ref in ats], axis=1)
        out_ref[...] = contract(left, right, NN).astype(out_ref.dtype)


def products(meta, ats, gs, radix, own):
    size = ats[0].shape[0] // radix
    return pl.pallas_call(
        product_kernel,
        in_specs=[in_smem] + [in_vmem] * 12,
        out_specs=[in_vmem] * radix,
        out_shape=[jax.ShapeDtypeStruct((size, own), f32)] + [jax.ShapeDtypeStruct((size, own), bf16)] * (radix - 1),
        compiler_params=pltpu.CompilerParams(vmem_limit_bytes=12 << 20),
        name="product",
    )(meta, *ats, *gs)


def sum_kernel(meta_ref, own_ref, *refs):
    pieces, (keep_ref, send_ref) = refs[:-2], refs[-2:]
    half = keep_ref.shape[0]
    for x_digit, ref in ((meta_ref[4], keep_ref), (1 - meta_ref[4], send_ref)):
        rows = pl.ds(pl.multiple_of(x_digit * half, half), half)
        total = own_ref[rows, :]
        for piece in pieces:
            total = total + piece[rows, :].astype(f32)
        ref[...] = total.astype(ref.dtype)


def summed(meta, own, pieces):
    half = own.shape[0] // 2
    return pl.pallas_call(
        sum_kernel,
        in_specs=[in_smem] + [in_vmem] * (1 + len(pieces)),
        out_specs=[in_vmem] * 2,
        out_shape=[jax.ShapeDtypeStruct((half, own.shape[1]), f32), jax.ShapeDtypeStruct((half, own.shape[1]), bf16)],
        compiler_params=pltpu.CompilerParams(vmem_limit_bytes=12 << 20),
        name="summed",
    )(meta, own, *pieces)


def join_kernel(meta_ref, dq1_ref, own1_ref, dq2_ref, own2_ref, rim1_ref, rim2_ref, dq_out, dk_out, dv_out):
    side = meta_ref[0]
    for row, rim, dq_ref in ((side, rim1_ref, dq1_ref), (1 - side, rim2_ref, dq2_ref)):
        rows = pl.ds(pl.multiple_of(row * HALF, HALF), HALF)
        for pair in range(dq1_ref.shape[0]):
            cols = slice(pair * PAIR, (pair + 1) * PAIR)
            dq_out[rows, cols] = dq_ref[pair]
            for which, out in enumerate((dk_out, dv_out)):
                total = own1_ref[pair, which, rows].astype(f32) + own2_ref[pair, which, rows].astype(f32)
                out[rows, cols] = (total + rim[pair, which].astype(f32)).astype(bf16)


def joined(meta, own1, own2, rim1, rim2, shape):
    out = jax.ShapeDtypeStruct(shape, bf16)
    return pl.pallas_call(
        join_kernel,
        in_specs=[in_smem] + [in_vmem] * 6,
        out_specs=[in_vmem] * 3,
        out_shape=[out] * 3,
        compiler_params=pltpu.CompilerParams(vmem_limit_bytes=12 << 20),
        name="joined",
    )(meta, *own1, *own2, rim1, rim2)


def swapped(value, stride, count):
    return lax.ppermute(value, "seq", [(i, i ^ stride) for i in range(count)])


def turned(value, count):
    return [lax.ppermute(value, "dp", [(i, (i + step) % count) for i in range(count)]) for step in range(1, count)]


def upper_stages(count):
    found = []
    stride = 4
    while stride < count:
        radix = min(4, count // stride)
        found.append((stride, radix))
        stride *= radix
    return found


def scattered_sum(block, strides, stages, me, count):
    tail = list(block.shape[-2:])
    left = strides
    for number, (stride, radix) in enumerate(stages):
        axis = [place for place, (low, size) in enumerate(left) if low <= stride < low * size][0]
        base, total = left[axis]
        inner = stride // base
        outer = total // (inner * radix)
        dims = [size for _, size in left]
        block = block.reshape(dims[:axis] + [outer, radix, inner] + dims[axis + 1 :] + tail)
        digit = (me // stride) % radix
        received = []
        for step in range(1, radix):
            pairs = [(source, source ^ (step * stride)) for source in range(count)]
            sent = lax.dynamic_index_in_dim(block, digit ^ step, axis + 1, keepdims=False)
            received.append(lax.ppermute(sent, "seq", pairs))
        total_sum = lax.dynamic_index_in_dim(block, digit, axis + 1, keepdims=False).astype(f32)
        for piece in received:
            total_sum = total_sum + piece.astype(f32)
        block = total_sum if number == len(stages) - 1 else total_sum.astype(bf16)
        left = left[:axis] + [(stride * radix, outer), (base, inner)] + left[axis + 1 :]
        keep = [(low, size) for low, size in left if size > 1]
        block = block.reshape([size for _, size in keep] + tail)
        left = keep
    return block.reshape(tail)


def on_device(queries, keys, values, out_grad, out_weight):
    q, k, v, g = queries[0], keys[0], values[0], out_grad[0]
    rows, width = q.shape
    assert rows == 2 * HALF
    count = lax.axis_size("seq")
    dp_count = lax.axis_size("dp")
    assert count >= 8 and count & (count - 1) == 0
    place = lax.axis_index("seq")
    mine = lax.axis_index("dp")
    odd = place % 2
    y_digit = (place // 2) % 2
    sides = (odd, 1 - odd)
    long_pairs = [(i, i + 1 if i % 2 else i - 1) for i in range(1, count - 1)]
    near_pairs = [(i, i ^ 1) for i in range(count)]
    block = width // count
    own_width = width // dp_count
    stages = upper_stages(count)
    direct = 2 * block == PAIR and len(stages) == 1 and dp_count == 2
    alone = (place == 0) | (place == count - 1)
    meta = jnp.stack([odd, y_digit if direct else 0 * y_digit, mine, place // 4 % stages[0][1], odd, alone, 0 * odd]).astype(jnp.int32)

    rim1 = packed_rim(meta[:1], k, v)
    first_rim = lax.ppermute(rim1, "seq", long_pairs)
    if direct:
        g_y = swapped(g, 2, count)
    thin, thick, rim2 = prepared(meta, q, k, v, g, out_weight)
    second_rim = lax.ppermute(rim2, "seq", near_pairs)
    if direct:
        g_dp = turned(g, dp_count)[0]
        g_y_dp = turned(g_y, dp_count)[0]
        gs = [g, g_dp, g_y, g_y_dp]

    keep1, send1, back1, *own1 = half_attention(meta, thin, thick, first_rim, False)
    from_long = lax.ppermute(back1, "seq", long_pairs)
    if direct:
        at_y1 = swapped(send1, 2, count)
        at_dp1 = turned(keep1, dp_count)[0]
        at_y_dp1 = turned(at_y1, dp_count)[0]
    keep2, send2 = half_attention(meta, thin, thick, second_rim, True, back=False)
    back2, *own2 = half_attention(meta, thin, thick, second_rim, True, front=False)
    if direct:
        at_y2 = swapped(send2, 2, count)
        at_dp2 = turned(keep2, dp_count)[0]
        at_y_dp2 = turned(at_y2, dp_count)[0]
    from_near = lax.ppermute(back2, "seq", near_pairs)

    frames = rows * count * dp_count
    if direct:
        ats = [keep1, at_y1, at_dp1, at_y_dp1, keep2, at_y2, at_dp2, at_y_dp2]
        terms = products(meta, ats, gs, count // 4, own_width)
        pieces = []
        for step in range(1, count // 4):
            pieces.append(swapped(terms[step], 4 * step, count))
        kept, sent = summed(meta, terms[0], pieces)
        wo_grad = kept + swapped(sent, 1, count).astype(f32)
    else:
        wo_grad = general_sum((keep1, send1), (keep2, send2), g, sides, place, mine, y_digit, count, dp_count)
    dq, dk, dv = joined(meta, own1, own2, from_long, from_near, q.shape)
    return dq[None], dk[None], dv[None], wo_grad * frames ** -0.5


def general_sum(first, second, g, sides, place, mine, y_digit, count, dp_count):
    width = g.shape[1]
    block = width // count
    own_width = width // dp_count
    g_parts = [lax.dynamic_slice_in_dim(g, mine * own_width, own_width, 1)]
    for step in range(1, dp_count):
        sent = lax.dynamic_slice_in_dim(g, (mine + step) % dp_count * own_width, own_width, 1)
        g_parts.append(lax.ppermute(sent, "dp", [(i, (i + step) % dp_count) for i in range(dp_count)]))
    g_here = jnp.stack(g_parts)
    g_there = swapped(g_here, 2, count)
    term = None
    for side, (even, odd) in zip(sides, (first, second)):
        at = jnp.stack([even.reshape(-1, PAIR, HALF), odd.reshape(-1, PAIR, HALF)], axis=1)
        parts = at.reshape(count // 4, 2, 2 * block, HALF)
        kept = lax.dynamic_index_in_dim(parts, y_digit, 1, keepdims=False).reshape(width // 2, HALF)
        sent = lax.dynamic_index_in_dim(parts, 1 - y_digit, 1, keepdims=False).reshape(width // 2, HALF)
        pack = jnp.stack([kept, swapped(sent, 2, count)])
        for utt, part in enumerate([pack] + turned(pack, dp_count)):
            for row, source in ((0, g_here), (1, g_there)):
                piece = contract(part[row], lax.dynamic_slice_in_dim(source[utt], side * HALF, HALF, 0), NN)
                term = piece if term is None else term + piece
    term = term.astype(bf16).reshape(count // 4, 2, block, own_width)
    return scattered_sum(term, [(4, count // 4), (1, 2)], upper_stages(count) + [(1, 2)], place, count)


def solution(mesh):
    spread = P("dp", "seq", None)
    return jax.shard_map(
        on_device,
        mesh=mesh,
        in_specs=(spread, spread, spread, spread, P()),
        out_specs=(spread, spread, spread, P("seq", "dp")),
        check_vma=False,
    )
```

```python
import functools

import jax
import jax.numpy as jnp
from jax import lax
from jax.experimental import pallas as pl
from jax.experimental.pallas import tpu as pltpu
from jax.sharding import PartitionSpec as P


HEAD_DIM = 64
HALF = 128
PAIR = 2 * HEAD_DIM
masked_score = -1e30
f32 = jnp.float32
bf16 = jnp.bfloat16


NN = ((1,), (0,))
NT = ((1,), (1,))
TN = ((0,), (0,))

in_vmem = pl.BlockSpec(memory_space=pltpu.VMEM)
in_smem = pl.BlockSpec(memory_space=pltpu.SMEM)


def contract(a, b, dims):
    return lax.dot_general(a, b, (dims, ((), ())), preferred_element_type=f32)


def half_kernel(meta_ref, thin_hbm, thick_hbm, rim_hbm, *refs, second, front, back):
    refs = list(refs)
    keep_ref, send_ref = [refs.pop(0) for _ in range(2)] if front else (None, None)
    back_ref, dq_hbm, own_hbm = [refs.pop(0) for _ in range(3)] if back else (None, None, None)
    one_ref, wide_ref, two_ref, score_ref, p_ref, in_sem = refs[:6]
    if back:
        dp_ref, ds_ref, dq_ref, own_ref, out_sem = refs[6:]
    side = 1 - meta_ref[0] if second else meta_ref[0]
    alone = meta_ref[6 if second else 5]
    bias = jnp.where(alone == 1, masked_score, 0.0).astype(f32)
    y_digit = meta_ref[1]
    scale = HEAD_DIM ** -0.5
    near_rows = pl.ds(pl.multiple_of(side * HALF, HALF), HALF)
    far_rows = pl.ds(pl.multiple_of((1 - side) * HALF, HALF), HALF)
    pairs = one_ref.shape[0]
    early = 2
    middle = pairs // 2
    kinds = range(2 if back else 1)

    def pair_of(number):
        return 2 * (number // 2) + (y_digit if number % 2 == 0 else 1 - y_digit)

    def fetches(group):
        some = pl.ds(0, early) if group == 0 else pl.ds(early, pairs - early)
        these = pl.ds(0, len(kinds))
        found = [(thin_hbm.at[some, these, side], one_ref.at[some])]
        for place, source in enumerate((rim_hbm.at[some], thick_hbm.at[some, :, side], thick_hbm.at[some, :, 1 - side])):
            found.append((source, wide_ref.at[some, :, pl.ds(place * HALF, HALF)]))
        return [pltpu.make_async_copy(a, b, in_sem.at[group, place]) for place, (a, b) in enumerate(found)]

    def stores(group):
        some = pl.ds(group * middle, middle)
        found = [(dq_ref.at[some], dq_hbm.at[some]), (own_ref.at[some], own_hbm.at[some])]
        return [pltpu.make_async_copy(a, b, out_sem.at[group, place]) for place, (a, b) in enumerate(found)]

    def multiply(number):
        pair = pair_of(number)
        slot = number % 3
        first_head = lax.broadcasted_iota(jnp.int32, (HALF, PAIR), 1) < HEAD_DIM
        for which in kinds:
            one = one_ref[pair, which].astype(f32) * (1.0 if which else scale)
            two_ref[slot, which, :HALF] = jnp.where(first_head, one, 0.0).astype(bf16)
            two_ref[slot, which, HALF:] = jnp.where(first_head, 0.0, one).astype(bf16)
            out = dp_ref if which else score_ref
            out[number % 2] = contract(wide_ref[pair, which], two_ref[slot, which], NT)

    def weigh(number):
        slot = number % 2
        ahead = lax.broadcasted_iota(jnp.int32, (HALF, 2 * HALF), 0) - lax.broadcasted_iota(jnp.int32, (HALF, 2 * HALF), 1) % HALF
        in_rim = ahead * (1 - 2 * side) >= side
        s_edge = jnp.where(in_rim, score_ref[slot, :HALF] + bias, score_ref[slot, 2 * HALF :])
        s_near = score_ref[slot, HALF : 2 * HALF]
        top = jnp.max(jnp.maximum(s_edge, s_near), axis=0, keepdims=True)
        e_edge = jnp.exp(s_edge - top)
        e_near = jnp.exp(s_near - top)
        inv = 1.0 / jnp.sum(e_edge + e_near, axis=0, keepdims=True)
        p_edge = e_edge * inv
        p_near = e_near * inv
        found = [(p_ref, p_edge, p_near)]
        if back:
            d_edge = jnp.where(in_rim, dp_ref[slot, :HALF], dp_ref[slot, 2 * HALF :])
            d_near = dp_ref[slot, HALF : 2 * HALF]
            delta = jnp.sum(p_edge * d_edge + p_near * d_near, axis=0, keepdims=True)
            found.append((ds_ref, p_edge * (d_edge - delta), p_near * (d_near - delta)))
        for ref, edge, near in found:
            ref[slot, :HALF] = jnp.where(in_rim, edge, 0.0).astype(bf16)
            ref[slot, HALF : 2 * HALF] = near.astype(bf16)
            ref[slot, 2 * HALF :] = jnp.where(in_rim, 0.0, edge).astype(bf16)

    def spread(number):
        slot = number % 2
        pair = pair_of(number)
        if front:
            at_ref = send_ref if number % 2 else keep_ref
            start = number // 2 * PAIR
            at = contract(wide_ref[pair, 1], p_ref[slot], TN)
            at_ref[start : start + HEAD_DIM, :] = at[:HEAD_DIM, :HALF].astype(bf16)
            at_ref[start + HEAD_DIM : start + PAIR, :] = at[HEAD_DIM:, HALF:].astype(bf16)
        if not back:
            return
        for which, left in enumerate((ds_ref, p_ref)):
            part = contract(left[slot], two_ref[number % 3, which], NN)
            back_ref[pair, which] = part[:HALF].astype(bf16)
            own_ref[pair, which, near_rows, :] = part[HALF : 2 * HALF].astype(bf16)
            own_ref[pair, which, far_rows, :] = part[2 * HALF :].astype(bf16)
        dqt = contract(wide_ref[pair, 0], ds_ref[slot], TN)
        dqt = jnp.concatenate([dqt[:HEAD_DIM, :HALF], dqt[HEAD_DIM:, HALF:]], axis=0) * scale
        dq_ref[pair] = dqt.T.astype(bf16)
        if (number + 1) % middle == 0:
            for copy in stores(number // middle):
                copy.start()

    for group in range(2):
        for copy in fetches(group):
            copy.start()
    for step in range(pairs + 2):
        if step in (0, early):
            for copy in fetches(step // early):
                copy.wait()
        if step < pairs:
            multiply(step)
        if 0 <= step - 2:
            spread(step - 2)
        if 0 <= step - 1 < pairs:
            weigh(step - 1)
    if back:
        for group in range(2):
            for copy in stores(group):
                copy.wait()


def half_attention(meta, thin, thick, rim, second, front=True, back=True):
    pairs, _, blocks, _, _ = thick.shape
    rows = blocks * HALF
    width = pairs * PAIR
    kinds = 2 if back else 1
    in_hbm = pl.BlockSpec(memory_space=pltpu.HBM)
    held = [pltpu.with_memory_space_constraint(array, pltpu.HBM) for array in (thin, thick)]
    out_specs, out_shape = [], []
    if front:
        out_specs += [in_vmem] * 2
        out_shape += [jax.ShapeDtypeStruct((width // 2, HALF), bf16)] * 2
    if back:
        out_specs += [in_vmem, in_hbm, in_hbm]
        out_shape += [
            jax.ShapeDtypeStruct((pairs, 2, HALF, PAIR), bf16),
            pltpu.HBM((pairs, HALF, PAIR), bf16),
            pltpu.HBM((pairs, 2, rows, PAIR), bf16),
        ]
    scratch = [
        pltpu.VMEM((pairs, kinds, HALF, PAIR), bf16),
        pltpu.VMEM((pairs, 2, 3 * HALF, PAIR), bf16),
        pltpu.VMEM((3, kinds, 2 * HALF, PAIR), bf16),
        pltpu.VMEM((2, 3 * HALF, 2 * HALF), f32),
        pltpu.VMEM((2, 3 * HALF, 2 * HALF), bf16),
        pltpu.SemaphoreType.DMA((2, 4)),
    ]
    if back:
        scratch += [
            pltpu.VMEM((2, 3 * HALF, 2 * HALF), f32),
            pltpu.VMEM((2, 3 * HALF, 2 * HALF), bf16),
            pltpu.VMEM((pairs, HALF, PAIR), bf16),
            pltpu.VMEM((pairs, 2, rows, PAIR), bf16),
            pltpu.SemaphoreType.DMA((2, 2)),
        ]
    return pl.pallas_call(
        functools.partial(half_kernel, second=second, front=front, back=back),
        in_specs=[in_smem, in_hbm, in_hbm, pl.BlockSpec(memory_space=pl.ANY)],
        out_specs=out_specs,
        out_shape=out_shape,
        scratch_shapes=scratch,
        cost_estimate=pl.CostEstimate(flops=(4 * front + 8 * back) * HALF * 3 * HALF * width, bytes_accessed=16 * rows * width,
                                      transcendentals=HALF * 2 * HALF * width // HEAD_DIM),
        compiler_params=pltpu.CompilerParams(vmem_limit_bytes=24 << 20),
    )(meta, *held, rim)


def rim_kernel(side_ref, k_ref, v_ref, out_ref):
    for pair in range(out_ref.shape[0]):
        cols = slice(pair * PAIR, (pair + 1) * PAIR)
        out_ref[pair, 0] = k_ref[:, cols]
        out_ref[pair, 1] = v_ref[:, cols]


def packed_rim(side, k, v):
    width = k.shape[1]
    block = pl.BlockSpec((HALF, width), lambda i, s: (s[0], 0))
    shape = (width // PAIR, 2, HALF, PAIR)
    return pl.pallas_call(
        rim_kernel,
        grid_spec=pltpu.PrefetchScalarGridSpec(
            num_scalar_prefetch=1, grid=(1,), in_specs=[block, block],
            out_specs=pl.BlockSpec(shape, lambda i, s: (0, 0, 0, 0)),
        ),
        out_shape=jax.ShapeDtypeStruct(shape, bf16),
    )(side, k, v)


def prepare_kernel(meta_ref, q_ref, k_ref, v_ref, g_ref, w_ref, thin_ref, thick_ref, rim_ref):
    pairs, _, blocks, _, _ = thin_ref.shape
    for pair in range(pairs):
        cols = slice(pair * PAIR, (pair + 1) * PAIR)
        for block in range(blocks):
            rows = slice(block * HALF, (block + 1) * HALF)
            thin_ref[pair, 0, block] = q_ref[rows, cols]
            thick_ref[pair, 0, block] = k_ref[rows, cols]
            thick_ref[pair, 1, block] = v_ref[rows, cols]
        rim_rows = pl.ds(pl.multiple_of((1 - meta_ref[0]) * HALF, HALF), HALF)
        rim_ref[pair, 0] = k_ref[rim_rows, cols]
        rim_ref[pair, 1] = v_ref[rim_rows, cols]
    step = 2 * PAIR
    for col in range(0, w_ref.shape[0], step):
        part = contract(g_ref[...], w_ref[col : col + step, :], NT).astype(bf16)
        for pair in range(2):
            for block in range(blocks):
                thin_ref[col // PAIR + pair, 1, block] = part[block * HALF : (block + 1) * HALF, pair * PAIR : (pair + 1) * PAIR]


def prepared(meta, q, k, v, g, w):
    rows, width = q.shape
    pairs, blocks = width // PAIR, rows // HALF
    whole = jax.ShapeDtypeStruct((pairs, 2, blocks, HALF, PAIR), bf16)
    return pl.pallas_call(
        prepare_kernel,
        in_specs=[in_smem] + [in_vmem] * 5,
        out_specs=[in_vmem] * 3,
        out_shape=[whole, whole, jax.ShapeDtypeStruct((pairs, 2, HALF, PAIR), bf16)],
        cost_estimate=pl.CostEstimate(flops=2 * rows * width * width, bytes_accessed=14 * rows * width + 2 * width * width, transcendentals=0),
        name="prepared",
    )(meta, q, k, v, g, w)


def product_kernel(meta_ref, *refs):
    side, mine, z_digit = meta_ref[0], meta_ref[2], meta_ref[3]
    ats, (g_ref, g_dp_ref, g_y_ref, g_y_dp_ref), outs = refs[:8], refs[8:12], refs[12:]
    own = outs[0].shape[1]
    size = outs[0].shape[0]
    rights = []
    for row in (side, 1 - side):
        rows = pl.ds(pl.multiple_of(row * HALF, HALF), HALF)
        cols = pl.ds(pl.multiple_of(mine * own, own), own)
        rights += [ref[rows, cols] for ref in (g_ref, g_y_ref, g_dp_ref, g_y_dp_ref)]
    right = jnp.concatenate(rights, axis=0)
    for step, out_ref in enumerate(outs):
        rows = pl.ds(pl.multiple_of((z_digit ^ step) * size, size), size)
        left = jnp.concatenate([ref[rows, :] for ref in ats], axis=1)
        out_ref[...] = contract(left, right, NN).astype(out_ref.dtype)


def products(meta, ats, gs, radix, own):
    size = ats[0].shape[0] // radix
    return pl.pallas_call(
        product_kernel,
        in_specs=[in_smem] + [in_vmem] * 12,
        out_specs=[in_vmem] * radix,
        out_shape=[jax.ShapeDtypeStruct((size, own), f32)] + [jax.ShapeDtypeStruct((size, own), bf16)] * (radix - 1),
        compiler_params=pltpu.CompilerParams(vmem_limit_bytes=12 << 20),
        name="product",
    )(meta, *ats, *gs)


def sum_kernel(meta_ref, own_ref, *refs):
    pieces, (keep_ref, send_ref) = refs[:-2], refs[-2:]
    half = keep_ref.shape[0]
    for x_digit, ref in ((meta_ref[4], keep_ref), (1 - meta_ref[4], send_ref)):
        rows = pl.ds(pl.multiple_of(x_digit * half, half), half)
        total = own_ref[rows, :]
        for piece in pieces:
            total = total + piece[rows, :].astype(f32)
        ref[...] = total.astype(ref.dtype)


def summed(meta, own, pieces):
    half = own.shape[0] // 2
    return pl.pallas_call(
        sum_kernel,
        in_specs=[in_smem] + [in_vmem] * (1 + len(pieces)),
        out_specs=[in_vmem] * 2,
        out_shape=[jax.ShapeDtypeStruct((half, own.shape[1]), f32), jax.ShapeDtypeStruct((half, own.shape[1]), bf16)],
        compiler_params=pltpu.CompilerParams(vmem_limit_bytes=12 << 20),
        name="summed",
    )(meta, own, *pieces)


def join_kernel(meta_ref, dq1_ref, own1_ref, dq2_ref, own2_ref, rim_ref, dq_out, dk_out, dv_out):
    side = meta_ref[0]
    for row, rim, dq_ref in ((side, rim_ref, dq1_ref), (1 - side, None, dq2_ref)):
        rows = pl.ds(pl.multiple_of(row * HALF, HALF), HALF)
        for pair in range(dq1_ref.shape[0]):
            cols = slice(pair * PAIR, (pair + 1) * PAIR)
            dq_out[rows, cols] = dq_ref[pair]
            for which, out in enumerate((dk_out, dv_out)):
                total = own1_ref[pair, which, rows].astype(f32) + own2_ref[pair, which, rows].astype(f32)
                if rim is not None:
                    total = total + rim[pair, which].astype(f32)
                out[rows, cols] = total.astype(bf16)


def joined(meta, own1, own2, rim, shape):
    out = jax.ShapeDtypeStruct(shape, bf16)
    return pl.pallas_call(
        join_kernel,
        in_specs=[in_smem] + [in_vmem] * 5,
        out_specs=[in_vmem] * 3,
        out_shape=[out] * 3,
        cost_estimate=pl.CostEstimate(flops=6 * shape[0] * shape[1], bytes_accessed=16 * shape[0] * shape[1], transcendentals=0),
        name="joined",
    )(meta, *own1, *own2, rim)


def finish_kernel(meta_ref, dk_hbm, dv_hbm, rim_ref, dk_out, dv_out, rows_ref, in_sem, out_sem):
    rows = pl.ds(pl.multiple_of((1 - meta_ref[0]) * HALF, HALF), HALF)
    loads = [pltpu.make_async_copy(ref.at[rows, :], rows_ref.at[which], in_sem.at[which]) for which, ref in enumerate((dk_hbm, dv_hbm))]
    saves = [pltpu.make_async_copy(rows_ref.at[which], ref.at[rows, :], out_sem.at[which]) for which, ref in enumerate((dk_out, dv_out))]
    for load in loads:
        load.start()
    for which in range(2):
        loads[which].wait()
        for pair in range(rim_ref.shape[0]):
            cols = slice(pair * PAIR, (pair + 1) * PAIR)
            total = rows_ref[which, :, cols].astype(f32) + rim_ref[pair, which].astype(f32)
            rows_ref[which, :, cols] = total.astype(bf16)
        saves[which].start()
    for save in saves:
        save.wait()


def finished(meta, dk, dv, rim):
    in_hbm = pl.BlockSpec(memory_space=pltpu.HBM)
    out = jax.ShapeDtypeStruct(dk.shape, bf16)
    return pl.pallas_call(
        finish_kernel,
        in_specs=[in_smem, in_hbm, in_hbm, in_vmem],
        out_specs=[in_hbm] * 2,
        out_shape=[out] * 2,
        scratch_shapes=[pltpu.VMEM((2, HALF, dk.shape[1]), bf16), pltpu.SemaphoreType.DMA((2,)), pltpu.SemaphoreType.DMA((2,))],
        input_output_aliases={1: 0, 2: 1},
        cost_estimate=pl.CostEstimate(flops=2 * HALF * dk.shape[1], bytes_accessed=12 * HALF * dk.shape[1], transcendentals=0),
        compiler_params=pltpu.CompilerParams(vmem_limit_bytes=12 << 20),
        name="finished",
    )(meta, pltpu.with_memory_space_constraint(dk, pltpu.HBM), pltpu.with_memory_space_constraint(dv, pltpu.HBM), rim)


def swapped(value, stride, count):
    return lax.ppermute(value, "seq", [(i, i ^ stride) for i in range(count)])


def turned(value, count):
    return [lax.ppermute(value, "dp", [(i, (i + step) % count) for i in range(count)]) for step in range(1, count)]


def upper_stages(count):
    found = []
    stride = 4
    while stride < count:
        radix = min(4, count // stride)
        found.append((stride, radix))
        stride *= radix
    return found


def scattered_sum(block, strides, stages, me, count):
    tail = list(block.shape[-2:])
    left = strides
    for number, (stride, radix) in enumerate(stages):
        axis = [place for place, (low, size) in enumerate(left) if low <= stride < low * size][0]
        base, total = left[axis]
        inner = stride // base
        outer = total // (inner * radix)
        dims = [size for _, size in left]
        block = block.reshape(dims[:axis] + [outer, radix, inner] + dims[axis + 1 :] + tail)
        digit = (me // stride) % radix
        received = []
        for step in range(1, radix):
            pairs = [(source, source ^ (step * stride)) for source in range(count)]
            sent = lax.dynamic_index_in_dim(block, digit ^ step, axis + 1, keepdims=False)
            received.append(lax.ppermute(sent, "seq", pairs))
        total_sum = lax.dynamic_index_in_dim(block, digit, axis + 1, keepdims=False).astype(f32)
        for piece in received:
            total_sum = total_sum + piece.astype(f32)
        block = total_sum if number == len(stages) - 1 else total_sum.astype(bf16)
        left = left[:axis] + [(stride * radix, outer), (base, inner)] + left[axis + 1 :]
        keep = [(low, size) for low, size in left if size > 1]
        block = block.reshape([size for _, size in keep] + tail)
        left = keep
    return block.reshape(tail)


def on_device(queries, keys, values, out_grad, out_weight):
    q, k, v, g = queries[0], keys[0], values[0], out_grad[0]
    rows, width = q.shape
    assert rows == 2 * HALF
    count = lax.axis_size("seq")
    dp_count = lax.axis_size("dp")
    assert count >= 8 and count & (count - 1) == 0
    place = lax.axis_index("seq")
    mine = lax.axis_index("dp")
    odd = place % 2
    y_digit = (place // 2) % 2
    sides = (odd, 1 - odd)
    long_pairs = [(i, i + 1 if i % 2 else i - 1) for i in range(1, count - 1)]
    near_pairs = [(i, i ^ 1) for i in range(count)]
    block = width // count
    own_width = width // dp_count
    stages = upper_stages(count)
    direct = 2 * block == PAIR and len(stages) == 1 and dp_count == 2
    alone = (place == 0) | (place == count - 1)
    meta = jnp.stack([odd, y_digit if direct else 0 * y_digit, mine, place // 4 % stages[0][1], odd, alone, 0 * odd]).astype(jnp.int32)

    rim1 = packed_rim(meta[:1], k, v)
    first_rim = lax.ppermute(rim1, "seq", long_pairs)
    if direct:
        g_y = swapped(g, 2, count)
    thin, thick, rim2 = prepared(meta, q, k, v, g, out_weight)
    second_rim = lax.ppermute(rim2, "seq", near_pairs)
    if direct:
        g_dp = turned(g, dp_count)[0]
        g_y_dp = turned(g_y, dp_count)[0]
        gs = [g, g_dp, g_y, g_y_dp]

    keep1, send1, back1, *own1 = half_attention(meta, thin, thick, first_rim, False)
    from_long = lax.ppermute(back1, "seq", long_pairs)
    if direct:
        at_y1 = swapped(send1, 2, count)
        at_dp1 = turned(keep1, dp_count)[0]
        at_y_dp1 = turned(at_y1, dp_count)[0]
    keep2, send2 = half_attention(meta, thin, thick, second_rim, True, back=False)
    back2, *own2 = half_attention(meta, thin, thick, second_rim, True, front=False)
    if direct:
        at_y2 = swapped(send2, 2, count)
        at_dp2 = turned(keep2, dp_count)[0]
        at_y_dp2 = turned(at_y2, dp_count)[0]
    from_near = lax.ppermute(back2, "seq", near_pairs)

    frames = rows * count * dp_count
    if direct:
        ats = [keep1, at_y1, at_dp1, at_y_dp1, keep2, at_y2, at_dp2, at_y_dp2]
        terms = products(meta, ats, gs, count // 4, own_width)
        pieces = []
        for step in range(1, count // 4):
            pieces.append(swapped(terms[step], 4 * step, count))
        kept, sent = summed(meta, terms[0], pieces)
        wo_grad = kept + swapped(sent, 1, count).astype(f32)
    else:
        wo_grad = general_sum((keep1, send1), (keep2, send2), g, sides, place, mine, y_digit, count, dp_count)
    dq, dk, dv = joined(meta, own1, own2, from_long, q.shape)
    dk, dv = finished(meta, dk, dv, from_near)
    return dq[None], dk[None], dv[None], wo_grad * frames ** -0.5


def general_sum(first, second, g, sides, place, mine, y_digit, count, dp_count):
    width = g.shape[1]
    block = width // count
    own_width = width // dp_count
    g_parts = [lax.dynamic_slice_in_dim(g, mine * own_width, own_width, 1)]
    for step in range(1, dp_count):
        sent = lax.dynamic_slice_in_dim(g, (mine + step) % dp_count * own_width, own_width, 1)
        g_parts.append(lax.ppermute(sent, "dp", [(i, (i + step) % dp_count) for i in range(dp_count)]))
    g_here = jnp.stack(g_parts)
    g_there = swapped(g_here, 2, count)
    term = None
    for side, (even, odd) in zip(sides, (first, second)):
        at = jnp.stack([even.reshape(-1, PAIR, HALF), odd.reshape(-1, PAIR, HALF)], axis=1)
        parts = at.reshape(count // 4, 2, 2 * block, HALF)
        kept = lax.dynamic_index_in_dim(parts, y_digit, 1, keepdims=False).reshape(width // 2, HALF)
        sent = lax.dynamic_index_in_dim(parts, 1 - y_digit, 1, keepdims=False).reshape(width // 2, HALF)
        pack = jnp.stack([kept, swapped(sent, 2, count)])
        for utt, part in enumerate([pack] + turned(pack, dp_count)):
            for row, source in ((0, g_here), (1, g_there)):
                piece = contract(part[row], lax.dynamic_slice_in_dim(source[utt], side * HALF, HALF, 0), NN)
                term = piece if term is None else term + piece
    term = term.astype(bf16).reshape(count // 4, 2, block, own_width)
    return scattered_sum(term, [(4, count // 4), (1, 2)], upper_stages(count) + [(1, 2)], place, count)


def solution(mesh):
    spread = P("dp", "seq", None)
    return jax.shard_map(
        on_device,
        mesh=mesh,
        in_specs=(spread, spread, spread, spread, P()),
        out_specs=(spread, spread, spread, P("seq", "dp")),
        check_vma=False,
    )
```

```python
import functools

import jax
import jax.numpy as jnp
from jax import lax
from jax.experimental import pallas as pl
from jax.experimental.pallas import tpu as pltpu
from jax.sharding import PartitionSpec as P


HEAD_DIM = 64
HALF = 128
PAIR = 2 * HEAD_DIM
masked_score = -1e30
f32 = jnp.float32
bf16 = jnp.bfloat16


NN = ((1,), (0,))
NT = ((1,), (1,))
TN = ((0,), (0,))

in_vmem = pl.BlockSpec(memory_space=pltpu.VMEM)
in_smem = pl.BlockSpec(memory_space=pltpu.SMEM)


def contract(a, b, dims):
    return lax.dot_general(a, b, (dims, ((), ())), preferred_element_type=f32)


def half_kernel(meta_ref, thin_hbm, thick_hbm, rim_hbm, *refs, second, front, back):
    refs = list(refs)
    keep_ref, send_ref = [refs.pop(0) for _ in range(2)] if front else (None, None)
    back_ref, dq_hbm, own_hbm = [refs.pop(0) for _ in range(3)] if back else (None, None, None)
    one_ref, wide_ref, two_ref, score_ref, p_ref, in_sem = refs[:6]
    if back:
        dp_ref, ds_ref, dq_ref, own_ref, out_sem = refs[6:]
    side = 1 - meta_ref[0] if second else meta_ref[0]
    alone = meta_ref[6 if second else 5]
    bias = jnp.where(alone == 1, masked_score, 0.0).astype(f32)
    y_digit = meta_ref[1]
    scale = HEAD_DIM ** -0.5
    near_rows = pl.ds(pl.multiple_of(side * HALF, HALF), HALF)
    far_rows = pl.ds(pl.multiple_of((1 - side) * HALF, HALF), HALF)
    pairs = one_ref.shape[0]
    early = 2
    middle = pairs // 2
    kinds = range(2 if back else 1)

    def pair_of(number):
        return 2 * (number // 2) + (y_digit if number % 2 == 0 else 1 - y_digit)

    def fetches(group):
        some = pl.ds(0, early) if group == 0 else pl.ds(early, pairs - early)
        these = pl.ds(0, len(kinds))
        found = [(thin_hbm.at[some, these, side], one_ref.at[some])]
        sources = (rim_hbm.at[some] if second else None, thick_hbm.at[some, :, side], thick_hbm.at[some, :, 1 - side])
        for place, source in enumerate(sources):
            if source is not None:
                found.append((source, wide_ref.at[some, :, pl.ds(place * HALF, HALF)]))
        return [pltpu.make_async_copy(a, b, in_sem.at[group, place]) for place, (a, b) in enumerate(found)]

    def stores(group):
        some = pl.ds(group * middle, middle)
        found = [(dq_ref.at[some], dq_hbm.at[some]), (own_ref.at[some], own_hbm.at[some])]
        return [pltpu.make_async_copy(a, b, out_sem.at[group, place]) for place, (a, b) in enumerate(found)]

    def multiply(number):
        pair = pair_of(number)
        slot = number % 3
        first_head = lax.broadcasted_iota(jnp.int32, (HALF, PAIR), 1) < HEAD_DIM
        if not second:
            cols = pl.ds(pl.multiple_of(pair * PAIR, PAIR), PAIR)
            for which in range(2):
                wide_ref[pair, which, :HALF] = rim_hbm[which, :, cols]
        for which in kinds:
            one = one_ref[pair, which].astype(f32) * (1.0 if which else scale)
            two_ref[slot, which, :HALF] = jnp.where(first_head, one, 0.0).astype(bf16)
            two_ref[slot, which, HALF:] = jnp.where(first_head, 0.0, one).astype(bf16)
            out = dp_ref if which else score_ref
            out[number % 2] = contract(wide_ref[pair, which], two_ref[slot, which], NT)

    def weigh(number):
        slot = number % 2
        ahead = lax.broadcasted_iota(jnp.int32, (HALF, 2 * HALF), 0) - lax.broadcasted_iota(jnp.int32, (HALF, 2 * HALF), 1) % HALF
        in_rim = ahead * (1 - 2 * side) >= side
        s_edge = jnp.where(in_rim, score_ref[slot, :HALF] + bias, score_ref[slot, 2 * HALF :])
        s_near = score_ref[slot, HALF : 2 * HALF]
        top = jnp.max(jnp.maximum(s_edge, s_near), axis=0, keepdims=True)
        e_edge = jnp.exp(s_edge - top)
        e_near = jnp.exp(s_near - top)
        inv = 1.0 / jnp.sum(e_edge + e_near, axis=0, keepdims=True)
        p_edge = e_edge * inv
        p_near = e_near * inv
        found = [(p_ref, p_edge, p_near)]
        if back:
            d_edge = jnp.where(in_rim, dp_ref[slot, :HALF], dp_ref[slot, 2 * HALF :])
            d_near = dp_ref[slot, HALF : 2 * HALF]
            delta = jnp.sum(p_edge * d_edge + p_near * d_near, axis=0, keepdims=True)
            found.append((ds_ref, p_edge * (d_edge - delta), p_near * (d_near - delta)))
        for ref, edge, near in found:
            ref[slot, :HALF] = jnp.where(in_rim, edge, 0.0).astype(bf16)
            ref[slot, HALF : 2 * HALF] = near.astype(bf16)
            ref[slot, 2 * HALF :] = jnp.where(in_rim, 0.0, edge).astype(bf16)

    def spread(number):
        slot = number % 2
        pair = pair_of(number)
        if front:
            at_ref = send_ref if number % 2 else keep_ref
            start = number // 2 * PAIR
            at = contract(wide_ref[pair, 1], p_ref[slot], TN)
            at_ref[start : start + HEAD_DIM, :] = at[:HEAD_DIM, :HALF].astype(bf16)
            at_ref[start + HEAD_DIM : start + PAIR, :] = at[HEAD_DIM:, HALF:].astype(bf16)
        if not back:
            return
        for which, left in enumerate((ds_ref, p_ref)):
            part = contract(left[slot], two_ref[number % 3, which], NN)
            back_ref[pair, which] = part[:HALF].astype(bf16)
            own_ref[pair, which, near_rows, :] = part[HALF : 2 * HALF].astype(bf16)
            own_ref[pair, which, far_rows, :] = part[2 * HALF :].astype(bf16)
        dqt = contract(wide_ref[pair, 0], ds_ref[slot], TN)
        dqt = jnp.concatenate([dqt[:HEAD_DIM, :HALF], dqt[HEAD_DIM:, HALF:]], axis=0) * scale
        dq_ref[pair] = dqt.T.astype(bf16)
        if (number + 1) % middle == 0:
            for copy in stores(number // middle):
                copy.start()

    for group in range(2):
        for copy in fetches(group):
            copy.start()
    for step in range(pairs + 2):
        if step in (0, early):
            for copy in fetches(step // early):
                copy.wait()
        if step < pairs:
            multiply(step)
        if 0 <= step - 2:
            spread(step - 2)
        if 0 <= step - 1 < pairs:
            weigh(step - 1)
    if back:
        for group in range(2):
            for copy in stores(group):
                copy.wait()


def half_attention(meta, thin, thick, rim, second, front=True, back=True):
    pairs, _, blocks, _, _ = thick.shape
    rows = blocks * HALF
    width = pairs * PAIR
    kinds = 2 if back else 1
    in_hbm = pl.BlockSpec(memory_space=pltpu.HBM)
    held = [pltpu.with_memory_space_constraint(array, pltpu.HBM) for array in (thin, thick)]
    out_specs, out_shape = [], []
    if front:
        out_specs += [in_vmem] * 2
        out_shape += [jax.ShapeDtypeStruct((width // 2, HALF), bf16)] * 2
    if back:
        out_specs += [in_vmem, in_hbm, in_hbm]
        out_shape += [
            jax.ShapeDtypeStruct((pairs, 2, HALF, PAIR), bf16),
            pltpu.HBM((pairs, HALF, PAIR), bf16),
            pltpu.HBM((pairs, 2, rows, PAIR), bf16),
        ]
    scratch = [
        pltpu.VMEM((pairs, kinds, HALF, PAIR), bf16),
        pltpu.VMEM((pairs, 2, 3 * HALF, PAIR), bf16),
        pltpu.VMEM((3, kinds, 2 * HALF, PAIR), bf16),
        pltpu.VMEM((2, 3 * HALF, 2 * HALF), f32),
        pltpu.VMEM((2, 3 * HALF, 2 * HALF), bf16),
        pltpu.SemaphoreType.DMA((2, 4)),
    ]
    if back:
        scratch += [
            pltpu.VMEM((2, 3 * HALF, 2 * HALF), f32),
            pltpu.VMEM((2, 3 * HALF, 2 * HALF), bf16),
            pltpu.VMEM((pairs, HALF, PAIR), bf16),
            pltpu.VMEM((pairs, 2, rows, PAIR), bf16),
            pltpu.SemaphoreType.DMA((2, 2)),
        ]
    return pl.pallas_call(
        functools.partial(half_kernel, second=second, front=front, back=back),
        in_specs=[in_smem, in_hbm, in_hbm, pl.BlockSpec(memory_space=pl.ANY) if second else in_vmem],
        out_specs=out_specs,
        out_shape=out_shape,
        scratch_shapes=scratch,
        cost_estimate=pl.CostEstimate(flops=(4 * front + 8 * back) * HALF * 3 * HALF * width, bytes_accessed=16 * rows * width,
                                      transcendentals=HALF * 2 * HALF * width // HEAD_DIM),
        compiler_params=pltpu.CompilerParams(vmem_limit_bytes=24 << 20),
    )(meta, *held, rim)


def rim_kernel(side_ref, k_hbm, v_hbm, out_ref, sems):
    rows = pl.ds(pl.multiple_of(side_ref[0] * HALF, HALF), HALF)
    copies = [pltpu.make_async_copy(ref.at[rows, :], out_ref.at[which], sems.at[which]) for which, ref in enumerate((k_hbm, v_hbm))]
    for copy in copies:
        copy.start()
    for copy in copies:
        copy.wait()


def packed_rim(side, k, v):
    in_hbm = pl.BlockSpec(memory_space=pltpu.HBM)
    return pl.pallas_call(
        rim_kernel,
        in_specs=[in_smem, in_hbm, in_hbm],
        out_specs=in_vmem,
        out_shape=jax.ShapeDtypeStruct((2, HALF, k.shape[1]), bf16),
        scratch_shapes=[pltpu.SemaphoreType.DMA((2,))],
        compiler_params=pltpu.CompilerParams(vmem_limit_bytes=4 << 20),
    )(side, *[pltpu.with_memory_space_constraint(array, pltpu.HBM) for array in (k, v)])


def prepare_kernel(meta_ref, q_ref, k_ref, v_ref, g_ref, w_ref, thin_ref, thick_ref, rim_ref):
    pairs, _, blocks, _, _ = thin_ref.shape
    for pair in range(pairs):
        cols = slice(pair * PAIR, (pair + 1) * PAIR)
        for block in range(blocks):
            rows = slice(block * HALF, (block + 1) * HALF)
            thin_ref[pair, 0, block] = q_ref[rows, cols]
            thick_ref[pair, 0, block] = k_ref[rows, cols]
            thick_ref[pair, 1, block] = v_ref[rows, cols]
        rim_rows = pl.ds(pl.multiple_of((1 - meta_ref[0]) * HALF, HALF), HALF)
        rim_ref[pair, 0] = k_ref[rim_rows, cols]
        rim_ref[pair, 1] = v_ref[rim_rows, cols]
    step = 2 * PAIR
    for col in range(0, w_ref.shape[0], step):
        part = contract(g_ref[...], w_ref[col : col + step, :], NT).astype(bf16)
        for pair in range(2):
            for block in range(blocks):
                thin_ref[col // PAIR + pair, 1, block] = part[block * HALF : (block + 1) * HALF, pair * PAIR : (pair + 1) * PAIR]


def prepared(meta, q, k, v, g, w):
    rows, width = q.shape
    pairs, blocks = width // PAIR, rows // HALF
    whole = jax.ShapeDtypeStruct((pairs, 2, blocks, HALF, PAIR), bf16)
    return pl.pallas_call(
        prepare_kernel,
        in_specs=[in_smem] + [in_vmem] * 5,
        out_specs=[in_vmem] * 3,
        out_shape=[whole, whole, jax.ShapeDtypeStruct((pairs, 2, HALF, PAIR), bf16)],
        cost_estimate=pl.CostEstimate(flops=2 * rows * width * width, bytes_accessed=14 * rows * width + 2 * width * width, transcendentals=0),
        name="prepared",
    )(meta, q, k, v, g, w)


def product_kernel(meta_ref, *refs):
    side, mine, z_digit = meta_ref[0], meta_ref[2], meta_ref[3]
    ats, (g_ref, g_dp_ref, g_y_ref, g_y_dp_ref), outs = refs[:8], refs[8:12], refs[12:]
    own = outs[0].shape[1]
    size = outs[0].shape[0]
    rights = []
    for row in (side, 1 - side):
        rows = pl.ds(pl.multiple_of(row * HALF, HALF), HALF)
        cols = pl.ds(pl.multiple_of(mine * own, own), own)
        rights += [ref[rows, cols] for ref in (g_ref, g_y_ref, g_dp_ref, g_y_dp_ref)]
    right = jnp.concatenate(rights, axis=0)
    for step, out_ref in enumerate(outs):
        rows = pl.ds(pl.multiple_of((z_digit ^ step) * size, size), size)
        left = jnp.concatenate([ref[rows, :] for ref in ats], axis=1)
        out_ref[...] = contract(left, right, NN).astype(out_ref.dtype)


def products(meta, ats, gs, radix, own):
    size = ats[0].shape[0] // radix
    return pl.pallas_call(
        product_kernel,
        in_specs=[in_smem] + [in_vmem] * 12,
        out_specs=[in_vmem] * radix,
        out_shape=[jax.ShapeDtypeStruct((size, own), f32)] + [jax.ShapeDtypeStruct((size, own), bf16)] * (radix - 1),
        compiler_params=pltpu.CompilerParams(vmem_limit_bytes=12 << 20),
        name="product",
    )(meta, *ats, *gs)


def sum_kernel(meta_ref, own_ref, *refs):
    pieces, (keep_ref, send_ref) = refs[:-2], refs[-2:]
    half = keep_ref.shape[0]
    for x_digit, ref in ((meta_ref[4], keep_ref), (1 - meta_ref[4], send_ref)):
        rows = pl.ds(pl.multiple_of(x_digit * half, half), half)
        total = own_ref[rows, :]
        for piece in pieces:
            total = total + piece[rows, :].astype(f32)
        ref[...] = total.astype(ref.dtype)


def summed(meta, own, pieces):
    half = own.shape[0] // 2
    return pl.pallas_call(
        sum_kernel,
        in_specs=[in_smem] + [in_vmem] * (1 + len(pieces)),
        out_specs=[in_vmem] * 2,
        out_shape=[jax.ShapeDtypeStruct((half, own.shape[1]), f32), jax.ShapeDtypeStruct((half, own.shape[1]), bf16)],
        compiler_params=pltpu.CompilerParams(vmem_limit_bytes=12 << 20),
        name="summed",
    )(meta, own, *pieces)


def join_kernel(meta_ref, dq1_ref, own1_ref, dq2_ref, own2_ref, rim_ref, dq_out, dk_out, dv_out):
    side = meta_ref[0]
    for row, rim, dq_ref in ((side, rim_ref, dq1_ref), (1 - side, None, dq2_ref)):
        rows = pl.ds(pl.multiple_of(row * HALF, HALF), HALF)
        for pair in range(dq1_ref.shape[0]):
            cols = slice(pair * PAIR, (pair + 1) * PAIR)
            dq_out[rows, cols] = dq_ref[pair]
            for which, out in enumerate((dk_out, dv_out)):
                total = own1_ref[pair, which, rows].astype(f32) + own2_ref[pair, which, rows].astype(f32)
                if rim is not None:
                    total = total + rim[pair, which].astype(f32)
                out[rows, cols] = total.astype(bf16)


def joined(meta, own1, own2, rim, shape):
    out = jax.ShapeDtypeStruct(shape, bf16)
    return pl.pallas_call(
        join_kernel,
        in_specs=[in_smem] + [in_vmem] * 5,
        out_specs=[in_vmem] * 3,
        out_shape=[out] * 3,
        cost_estimate=pl.CostEstimate(flops=6 * shape[0] * shape[1], bytes_accessed=16 * shape[0] * shape[1], transcendentals=0),
        name="joined",
    )(meta, *own1, *own2, rim)


def finish_kernel(meta_ref, dk_hbm, dv_hbm, rim_ref, dk_out, dv_out, rows_ref, in_sem, out_sem):
    rows = pl.ds(pl.multiple_of((1 - meta_ref[0]) * HALF, HALF), HALF)
    loads = [pltpu.make_async_copy(ref.at[rows, :], rows_ref.at[which], in_sem.at[which]) for which, ref in enumerate((dk_hbm, dv_hbm))]
    saves = [pltpu.make_async_copy(rows_ref.at[which], ref.at[rows, :], out_sem.at[which]) for which, ref in enumerate((dk_out, dv_out))]
    for load in loads:
        load.start()
    for which in range(2):
        loads[which].wait()
        for pair in range(rim_ref.shape[0]):
            cols = slice(pair * PAIR, (pair + 1) * PAIR)
            total = rows_ref[which, :, cols].astype(f32) + rim_ref[pair, which].astype(f32)
            rows_ref[which, :, cols] = total.astype(bf16)
        saves[which].start()
    for save in saves:
        save.wait()


def finished(meta, dk, dv, rim):
    in_hbm = pl.BlockSpec(memory_space=pltpu.HBM)
    out = jax.ShapeDtypeStruct(dk.shape, bf16)
    return pl.pallas_call(
        finish_kernel,
        in_specs=[in_smem, in_hbm, in_hbm, in_vmem],
        out_specs=[in_hbm] * 2,
        out_shape=[out] * 2,
        scratch_shapes=[pltpu.VMEM((2, HALF, dk.shape[1]), bf16), pltpu.SemaphoreType.DMA((2,)), pltpu.SemaphoreType.DMA((2,))],
        input_output_aliases={1: 0, 2: 1},
        cost_estimate=pl.CostEstimate(flops=2 * HALF * dk.shape[1], bytes_accessed=12 * HALF * dk.shape[1], transcendentals=0),
        compiler_params=pltpu.CompilerParams(vmem_limit_bytes=12 << 20),
        name="finished",
    )(meta, pltpu.with_memory_space_constraint(dk, pltpu.HBM), pltpu.with_memory_space_constraint(dv, pltpu.HBM), rim)


def swapped(value, stride, count):
    return lax.ppermute(value, "seq", [(i, i ^ stride) for i in range(count)])


def turned(value, count):
    return [lax.ppermute(value, "dp", [(i, (i + step) % count) for i in range(count)]) for step in range(1, count)]


def upper_stages(count):
    found = []
    stride = 4
    while stride < count:
        radix = min(4, count // stride)
        found.append((stride, radix))
        stride *= radix
    return found


def scattered_sum(block, strides, stages, me, count):
    tail = list(block.shape[-2:])
    left = strides
    for number, (stride, radix) in enumerate(stages):
        axis = [place for place, (low, size) in enumerate(left) if low <= stride < low * size][0]
        base, total = left[axis]
        inner = stride // base
        outer = total // (inner * radix)
        dims = [size for _, size in left]
        block = block.reshape(dims[:axis] + [outer, radix, inner] + dims[axis + 1 :] + tail)
        digit = (me // stride) % radix
        received = []
        for step in range(1, radix):
            pairs = [(source, source ^ (step * stride)) for source in range(count)]
            sent = lax.dynamic_index_in_dim(block, digit ^ step, axis + 1, keepdims=False)
            received.append(lax.ppermute(sent, "seq", pairs))
        total_sum = lax.dynamic_index_in_dim(block, digit, axis + 1, keepdims=False).astype(f32)
        for piece in received:
            total_sum = total_sum + piece.astype(f32)
        block = total_sum if number == len(stages) - 1 else total_sum.astype(bf16)
        left = left[:axis] + [(stride * radix, outer), (base, inner)] + left[axis + 1 :]
        keep = [(low, size) for low, size in left if size > 1]
        block = block.reshape([size for _, size in keep] + tail)
        left = keep
    return block.reshape(tail)


def on_device(queries, keys, values, out_grad, out_weight):
    q, k, v, g = queries[0], keys[0], values[0], out_grad[0]
    rows, width = q.shape
    assert rows == 2 * HALF
    count = lax.axis_size("seq")
    dp_count = lax.axis_size("dp")
    assert count >= 8 and count & (count - 1) == 0
    place = lax.axis_index("seq")
    mine = lax.axis_index("dp")
    odd = place % 2
    y_digit = (place // 2) % 2
    sides = (odd, 1 - odd)
    long_pairs = [(i, i + 1 if i % 2 else i - 1) for i in range(1, count - 1)]
    near_pairs = [(i, i ^ 1) for i in range(count)]
    block = width // count
    own_width = width // dp_count
    stages = upper_stages(count)
    direct = 2 * block == PAIR and len(stages) == 1 and dp_count == 2
    alone = (place == 0) | (place == count - 1)
    meta = jnp.stack([odd, y_digit if direct else 0 * y_digit, mine, place // 4 % stages[0][1], odd, alone, 0 * odd]).astype(jnp.int32)

    rim1 = packed_rim(meta[:1], k, v)
    first_rim = lax.ppermute(rim1, "seq", long_pairs)
    if direct:
        g_y = swapped(g, 2, count)
    thin, thick, rim2 = prepared(meta, q, k, v, g, out_weight)
    second_rim = lax.ppermute(rim2, "seq", near_pairs)
    if direct:
        g_dp = turned(g, dp_count)[0]
        g_y_dp = turned(g_y, dp_count)[0]
        gs = [g, g_dp, g_y, g_y_dp]

    keep1, send1, back1, *own1 = half_attention(meta, thin, thick, first_rim, False)
    from_long = lax.ppermute(back1, "seq", long_pairs)
    if direct:
        at_y1 = swapped(send1, 2, count)
        at_dp1 = turned(keep1, dp_count)[0]
        at_y_dp1 = turned(at_y1, dp_count)[0]
    keep2, send2 = half_attention(meta, thin, thick, second_rim, True, back=False)
    back2, *own2 = half_attention(meta, thin, thick, second_rim, True, front=False)
    if direct:
        at_y2 = swapped(send2, 2, count)
        at_dp2 = turned(keep2, dp_count)[0]
        at_y_dp2 = turned(at_y2, dp_count)[0]
    from_near = lax.ppermute(back2, "seq", near_pairs)

    frames = rows * count * dp_count
    if direct:
        ats = [keep1, at_y1, at_dp1, at_y_dp1, keep2, at_y2, at_dp2, at_y_dp2]
        terms = products(meta, ats, gs, count // 4, own_width)
        pieces = []
        for step in range(1, count // 4):
            pieces.append(swapped(terms[step], 4 * step, count))
        kept, sent = summed(meta, terms[0], pieces)
        wo_grad = kept + swapped(sent, 1, count).astype(f32)
    else:
        wo_grad = general_sum((keep1, send1), (keep2, send2), g, sides, place, mine, y_digit, count, dp_count)
    dq, dk, dv = joined(meta, own1, own2, from_long, q.shape)
    dk, dv = finished(meta, dk, dv, from_near)
    return dq[None], dk[None], dv[None], wo_grad * frames ** -0.5


def general_sum(first, second, g, sides, place, mine, y_digit, count, dp_count):
    width = g.shape[1]
    block = width // count
    own_width = width // dp_count
    g_parts = [lax.dynamic_slice_in_dim(g, mine * own_width, own_width, 1)]
    for step in range(1, dp_count):
        sent = lax.dynamic_slice_in_dim(g, (mine + step) % dp_count * own_width, own_width, 1)
        g_parts.append(lax.ppermute(sent, "dp", [(i, (i + step) % dp_count) for i in range(dp_count)]))
    g_here = jnp.stack(g_parts)
    g_there = swapped(g_here, 2, count)
    term = None
    for side, (even, odd) in zip(sides, (first, second)):
        at = jnp.stack([even.reshape(-1, PAIR, HALF), odd.reshape(-1, PAIR, HALF)], axis=1)
        parts = at.reshape(count // 4, 2, 2 * block, HALF)
        kept = lax.dynamic_index_in_dim(parts, y_digit, 1, keepdims=False).reshape(width // 2, HALF)
        sent = lax.dynamic_index_in_dim(parts, 1 - y_digit, 1, keepdims=False).reshape(width // 2, HALF)
        pack = jnp.stack([kept, swapped(sent, 2, count)])
        for utt, part in enumerate([pack] + turned(pack, dp_count)):
            for row, source in ((0, g_here), (1, g_there)):
                piece = contract(part[row], lax.dynamic_slice_in_dim(source[utt], side * HALF, HALF, 0), NN)
                term = piece if term is None else term + piece
    term = term.astype(bf16).reshape(count // 4, 2, block, own_width)
    return scattered_sum(term, [(4, count // 4), (1, 2)], upper_stages(count) + [(1, 2)], place, count)


def solution(mesh):
    spread = P("dp", "seq", None)
    return jax.shard_map(
        on_device,
        mesh=mesh,
        in_specs=(spread, spread, spread, spread, P()),
        out_specs=(spread, spread, spread, P("seq", "dp")),
        check_vma=False,
    )
```
